128 devices in a mesh: gx: 8 (over y, core), gy: 16 (over x, z).
Axes of the slice: x: 4, y: 4, z: 4, core: 2. Of those that a mesh axis runs over, the one named last changes fastest.
Arguments:
- dist_old: bfloat16 [12288, 8, 4096], P(('gx', 'gy')), may hold values from 0.0625 to 16, as said below
- source_owner: int32 [12288], P(('gx', 'gy')), may hold values from 0 to 127, as said below
- levels: int32 [12288], P(('gx', 'gy')), may hold values from 0 to 2
- active: int32 [12288, 8], P(('gx', 'gy')), may hold values 0 or 1
Outputs:
- dist_new: bfloat16 [12288, 8, 4096], P(('gx', 'gy'))
The draws below stay inside these ranges and needn't reach their ends.
Inputs may be any that keep to these rules, and one draw needn't show every extreme that they name: `dist_old`: Positive. New slot k of device d receives old slot k of device source_owner[d * 96 + k]; for each k these sources over d are a permutation of the devices. A device takes at most 1 block from any one device, and exactly 1 from some.
All inputs are finite; a program needn't handle non-finite values. No bound on the sum of `active` on one device may be relied on, other than what follows from the above.
Results may differ from the reference program's by a relative error of at most 0.0045.
Values may be sent and summed in bfloat16 or wider, within the bound.
No kernel may reach another device: no remote copies, remote signals or barrier semaphores. Data moves between devices by JAX's collectives and lax.ppermute only.
A program may use at most 128 MiB of HBM per device.

```python
import math
import jax
import jax.numpy as jnp
from jax import lax

VS = 16
BX = 4
BY = 4
BZ = 6
BLOCKS = 12288
N_GX = 8
N_GY = 16
DEVICES = 128


def draw_dist_old(key, part):
    total = VS * VS * VS
    shape = (BLOCKS, 8, total)
    first = jax.random.fold_in(jax.random.fold_in(key, 5), 0)
    values = jnp.exp(jax.random.uniform(first, shape, jnp.float32, math.log(0.25), math.log(4.0)))
    return values.astype(jnp.bfloat16)


def draw_source_owner(key, part):
    devices = DEVICES
    blocks = BX * BY * BZ
    rounds = (blocks + devices - 1) // devices
    slots = jnp.arange(blocks, dtype=jnp.int32)
    turn = slots // devices
    place = slots % devices
    base_key = jax.random.fold_in(key, 17)
    targets = []
    offsets = []
    shuffles = []
    for number in range(rounds):
        round_key = jax.random.fold_in(base_key, number)
        key_target, key_offset, key_shuffle = jax.random.split(round_key, 3)
        targets.append(jax.random.permutation(key_target, devices).astype(jnp.int32))
        offsets.append(jax.random.permutation(key_offset, devices).astype(jnp.int32))
        shuffles.append(jax.random.permutation(key_shuffle, devices).astype(jnp.int32))
    target_table = jnp.stack(targets)
    offset_table = jnp.stack(offsets)
    shuffle_table = jnp.stack(shuffles)
    shift_amount = shuffle_table[turn, place]
    position = (offset_table[turn].T + shift_amount[None, :]) % devices
    sources = target_table[turn[None, :], position]
    return sources.reshape(-1).astype(jnp.int32)


def plant(drawn, own_key, smallest, largest):
    extent = drawn.shape
    spot = [jax.random.randint(jax.random.fold_in(own_key, axis), (), 0, extent[axis]) for axis in range(len(extent))]
    drawn = drawn.at[tuple(spot)].set(smallest)
    longest = extent.index(max(extent))
    spot[longest] = (spot[longest] + 1) % extent[longest]
    return drawn.at[tuple(spot)].set(largest)


def setup_inputs(seed: int = 0) -> dict:
    key_of = jax.random.split(jax.random.key(seed), 5)
    return {
        "dist_old": draw_dist_old(jax.random.fold_in(key_of[4], 71), 0),
        "source_owner": draw_source_owner(jax.random.fold_in(key_of[4], 71), 0),
        "levels": plant(jax.random.randint(key_of[2], (BLOCKS,), 0, 3), jax.random.fold_in(key_of[2], 1), 0, 2).astype(jnp.int32),
        "active": plant((jax.random.randint(key_of[3], (BLOCKS, 8), 0, 4) < 3).astype(jnp.int32), jax.random.fold_in(key_of[3], 1), 0, 1),
    }


RELAX_INCREMENT = 0.3
COURANT = 0.028

def velocity_table(points):
    total = points * points * points
    index = jnp.arange(total, dtype=jnp.int32)
    stacked = jnp.stack([index // (points * points), index // points % points, index % points])
    return 2 * stacked + 1 - points

def collide(cell_rows, points):
    total = points * points * points
    weights = velocity_table(points).astype(jnp.float32)
    along_x, along_y, along_z = (weights[0], weights[1], weights[2])
    filler = jnp.zeros_like(along_x)
    columns = [jnp.ones_like(along_x), along_x, along_y, along_z, along_x * along_x, along_y * along_y, along_z * along_z, along_x * along_y, along_x * along_z, along_y * along_z]
    moments_basis = jnp.stack(columns + [filler] * 6, axis=1)
    raw_sums = jnp.dot(cell_rows, moments_basis.astype(jnp.bfloat16), preferred_element_type=jnp.float32) / total
    spacing = 3.0 / points
    zeroth_moment_field = raw_sums[:, 0]
    drift_x = spacing * raw_sums[:, 1] / zeroth_moment_field
    drift_y = spacing * raw_sums[:, 2] / zeroth_moment_field
    drift_z = spacing * raw_sums[:, 3] / zeroth_moment_field
    square = spacing * spacing
    spread_second_moment_first = square * raw_sums[:, 4] / zeroth_moment_field - drift_x * drift_x
    spread_second_moment_second = square * raw_sums[:, 5] / zeroth_moment_field - drift_y * drift_y
    spread_second_moment_third = square * raw_sums[:, 6] / zeroth_moment_field - drift_z * drift_z
    spread_xy = square * raw_sums[:, 7] / zeroth_moment_field - drift_x * drift_y
    spread_xz = square * raw_sums[:, 8] / zeroth_moment_field - drift_x * drift_z
    spread_yz = square * raw_sums[:, 9] / zeroth_moment_field - drift_y * drift_z
    thermal_energy_per_particle = (spread_second_moment_first + spread_second_moment_second + spread_second_moment_third) / 3.0
    anisotropic_factor_first_first = 1.5 * thermal_energy_per_particle - 0.5 * spread_second_moment_first
    anisotropic_factor_second_second = 1.5 * thermal_energy_per_particle - 0.5 * spread_second_moment_second
    anisotropic_factor_third_third = 1.5 * thermal_energy_per_particle - 0.5 * spread_second_moment_third
    lam_xy = -0.5 * spread_xy
    lam_xz = -0.5 * spread_xz
    lam_yz = -0.5 * spread_yz
    adj_xx = anisotropic_factor_second_second * anisotropic_factor_third_third - lam_yz * lam_yz
    adj_yy = anisotropic_factor_first_first * anisotropic_factor_third_third - lam_xz * lam_xz
    adj_zz = anisotropic_factor_first_first * anisotropic_factor_second_second - lam_xy * lam_xy
    adj_xy = lam_xz * lam_yz - lam_xy * anisotropic_factor_third_third
    adj_xz = lam_xy * lam_yz - lam_xz * anisotropic_factor_second_second
    adj_yz = lam_xy * lam_xz - anisotropic_factor_first_first * lam_yz
    determinant = anisotropic_factor_first_first * adj_xx + lam_xy * adj_xy + lam_xz * adj_xz
    inv_xx = adj_xx / determinant
    inv_yy = adj_yy / determinant
    inv_zz = adj_zz / determinant
    inv_xy = adj_xy / determinant
    inv_xz = adj_xz / determinant
    inv_yz = adj_yz / determinant
    pull_x = inv_xx * drift_x + inv_xy * drift_y + inv_xz * drift_z
    pull_y = inv_xy * drift_x + inv_yy * drift_y + inv_yz * drift_z
    pull_z = inv_xz * drift_x + inv_yz * drift_y + inv_zz * drift_z
    quadratic = drift_x * pull_x + drift_y * pull_y + drift_z * pull_z
    log_prefactor = jnp.log(zeroth_moment_field) + 3.0 * math.log(6.0) - 1.5 * math.log(2.0 * math.pi) - 0.5 * jnp.log(determinant)
    zero_rows = jnp.zeros_like(zeroth_moment_field)
    coefficients = jnp.stack([log_prefactor - 0.5 * quadratic, spacing * pull_x, spacing * pull_y, spacing * pull_z, -0.5 * square * inv_xx, -0.5 * square * inv_yy, -0.5 * square * inv_zz, -square * inv_xy, -square * inv_xz, -square * inv_yz] + [zero_rows] * 6, axis=1)
    exponent = jnp.dot(coefficients, moments_basis.T, precision=lax.Precision.HIGHEST)
    gauss = jnp.exp(exponent)
    inverse_relax_period = 1.0 - jnp.exp(-RELAX_INCREMENT * zeroth_moment_field * jnp.sqrt(thermal_energy_per_particle))
    moved = cell_rows.astype(jnp.float32)
    return (moved + inverse_relax_period[:, None] * (gauss - moved)).astype(jnp.bfloat16)

def to_grid(blocks, blocks_x, blocks_y, blocks_z):
    trailing = blocks.shape[2:]
    shaped = blocks.reshape((blocks_x, blocks_y, blocks_z, 2, 2, 2) + trailing)
    permute_order = (0, 3, 1, 4, 2, 5) + tuple(range(6, 6 + len(trailing)))
    return shaped.transpose(permute_order).reshape((2 * blocks_x, 2 * blocks_y, 2 * blocks_z) + trailing)

def from_grid(grid, blocks_x, blocks_y, blocks_z):
    trailing = grid.shape[3:]
    shaped = grid.reshape((blocks_x, 2, blocks_y, 2, blocks_z, 2) + trailing)
    permute_order = (0, 2, 4, 1, 3, 5) + tuple(range(6, 6 + len(trailing)))
    return shaped.transpose(permute_order).reshape((blocks_x * blocks_y * blocks_z, 8) + trailing)

def assemble(grid, behind_x, beyond_x, behind_y, beyond_y):
    along_x = jnp.concatenate([behind_x[None], grid, beyond_x[None]], axis=0)
    lower_y = jnp.pad(behind_y, ((1, 1), (0, 0), (0, 0)))[:, None]
    upper_y = jnp.pad(beyond_y, ((1, 1), (0, 0), (0, 0)))[:, None]
    return jnp.concatenate([lower_y, along_x, upper_y], axis=1)

def advance(padded, courant, active_grid, points):
    speeds = velocity_table(points).astype(jnp.float32) * (3.0 / points)
    center = padded[1:-1, 1:-1, 1:-1].astype(jnp.float32)
    behind = [padded[:-2, 1:-1, 1:-1], padded[1:-1, :-2, 1:-1], padded[1:-1, 1:-1, :-2]]
    beyond = [padded[2:, 1:-1, 1:-1], padded[1:-1, 2:, 1:-1], padded[1:-1, 1:-1, 2:]]
    net_flux = jnp.zeros_like(center)
    for direction in range(3):
        forward = jnp.maximum(speeds[direction], 0.0)
        backward = jnp.minimum(speeds[direction], 0.0)
        net_flux = net_flux + forward * (center - behind[direction].astype(jnp.float32)) + backward * (beyond[direction].astype(jnp.float32) - center)
    result = active_grid[..., None] * (center - courant[..., None] * net_flux)
    return result.astype(jnp.bfloat16)

def reference(dist_old, source_owner, levels, active):
    blocks = BX * BY * BZ
    devices = N_GX * N_GY
    total = VS * VS * VS
    old_blocks = dist_old.reshape(devices, blocks, 8, total)
    sources = source_owner.reshape(devices, blocks)
    cell_mask = active.reshape(devices, blocks, 8)
    level_table = levels.reshape(devices, blocks)
    slots = jnp.arange(blocks, dtype=jnp.int32)

    def relax_device(device):
        gathered = old_blocks[sources[device], slots]
        relaxed = collide(gathered.reshape(-1, total), VS).reshape(blocks, 8, total)
        return jnp.where(cell_mask[device][:, :, None] > 0, relaxed, jnp.zeros_like(relaxed))
    kept = lax.map(relax_device, jnp.arange(devices, dtype=jnp.int32))

    def grid_of(device):
        return to_grid(kept[device], BX, BY, BZ)

    def advance_device(device):
        row_index = device // N_GY
        column_index = device % N_GY
        own_grid = grid_of(device)
        empty_x = jnp.zeros_like(own_grid[0])
        empty_y = jnp.zeros_like(own_grid[:, 0])
        behind_x = jnp.where(row_index > 0, grid_of(jnp.maximum(device - N_GY, 0))[-1], empty_x)
        beyond_x = jnp.where(row_index < N_GX - 1, grid_of(jnp.minimum(device + N_GY, devices - 1))[0], empty_x)
        behind_y = jnp.where(column_index > 0, grid_of(jnp.maximum(device - 1, 0))[:, -1], empty_y)
        beyond_y = jnp.where(column_index < N_GY - 1, grid_of(jnp.minimum(device + 1, devices - 1))[:, 0], empty_y)
        widened = assemble(own_grid, behind_x, beyond_x, behind_y, beyond_y)
        padded = jnp.pad(widened, ((0, 0), (0, 0), (1, 1), (0, 0)))
        courant = COURANT * jnp.exp2(level_table[device].astype(jnp.float32))
        courant_grid = to_grid(jnp.broadcast_to(courant[:, None], (blocks, 8)), BX, BY, BZ)
        active_grid = to_grid(cell_mask[device].astype(jnp.float32), BX, BY, BZ)
        return from_grid(advance(padded, courant_grid, active_grid, VS), BX, BY, BZ)
    stepped = lax.map(advance_device, jnp.arange(devices, dtype=jnp.int32))
    return stepped.reshape(devices * blocks, 8, total)
```

```python
import math

import jax
import jax.numpy as jnp
import ml_dtypes
import numpy as np
from jax import lax
from jax.experimental import pallas as pl
from jax.experimental.pallas import tpu as pltpu
from jax.sharding import PartitionSpec as P

VS = 16
BX, BY, BZ = 4, 4, 6
BLOCKS = BX * BY * BZ
TOTAL = VS * VS * VS
CELLS = 8
SLAB = BY * BZ
RELAX_INCREMENT = 0.3
COURANT = 0.028
SPACING = 3.0 / VS
LOG2E = 1.0 / math.log(2.0)

CHUNKS = 2
WIDTH = TOTAL // CHUNKS
TILES = WIDTH // 128
PIECE = 16
GROUP = 8
STEP = 512
ZERO_BLOCK = BLOCKS
X_HALO = BLOCKS + 1
Y_HALO = X_HALO + SLAB
HELD = Y_HALO + BX * BZ


def basis_rows():
    index = np.arange(TOTAL)
    x, y, z = (2 * i + 1 - VS for i in (index // (VS * VS), index // VS % VS, index % VS))
    rows = np.zeros((16, TOTAL), np.float32)
    rows[:10] = [np.ones_like(x), x, y, z, x * x, y * y, z * z, x * y, x * z, y * z]
    whole = np.zeros((128, TOTAL), np.float32)
    for copy in range(3):
        whole[16 * copy : 16 * copy + 16] = rows
    return whole.astype(ml_dtypes.bfloat16)


def coefficients_of(sums):
    raw = [sums[i : i + 1] * (1.0 / TOTAL) for i in range(10)]
    density = raw[0]
    drift = [SPACING * raw[1 + a] / density for a in range(3)]
    square = SPACING * SPACING
    spread = [square * raw[4 + a] / density - drift[a] * drift[a] for a in range(3)]
    spread_xy = square * raw[7] / density - drift[0] * drift[1]
    spread_xz = square * raw[8] / density - drift[0] * drift[2]
    spread_yz = square * raw[9] / density - drift[1] * drift[2]
    temperature = (spread[0] + spread[1] + spread[2]) / 3.0
    xx, yy, zz = (1.5 * temperature - 0.5 * s for s in spread)
    xy, xz, yz = (-0.5 * s for s in (spread_xy, spread_xz, spread_yz))
    adj_xx, adj_yy, adj_zz = yy * zz - yz * yz, xx * zz - xz * xz, xx * yy - xy * xy
    adj_xy, adj_xz, adj_yz = xz * yz - xy * zz, xy * yz - xz * yy, xy * xz - xx * yz
    determinant = xx * adj_xx + xy * adj_xy + xz * adj_xz
    inv = [a / determinant for a in (adj_xx, adj_yy, adj_zz, adj_xy, adj_xz, adj_yz)]
    pull = [
        inv[0] * drift[0] + inv[3] * drift[1] + inv[4] * drift[2],
        inv[3] * drift[0] + inv[1] * drift[1] + inv[5] * drift[2],
        inv[4] * drift[0] + inv[5] * drift[1] + inv[2] * drift[2],
    ]
    quadratic = drift[0] * pull[0] + drift[1] * pull[1] + drift[2] * pull[2]
    log_prefactor = (
        jnp.log(density)
        + (3.0 * math.log(6.0) - 1.5 * math.log(2.0 * math.pi))
        - 0.5 * jnp.log(determinant)
    )
    rows = [log_prefactor - 0.5 * quadratic]
    rows += [SPACING * p for p in pull]
    rows += [-0.5 * square * i for i in inv[:3]]
    rows += [-square * i for i in inv[3:]]
    fraction = 1.0 - jnp.exp(-RELAX_INCREMENT * density * jnp.sqrt(temperature))
    return [LOG2E * r for r in rows], fraction


def collide_kernel(asked, dist, basis, *rest):
    sends = rest[:CHUNKS]
    held, relaxed, sums, factors, target, in_sems, out_sems = rest[CHUNKS:]
    pieces = BLOCKS // PIECE

    def arrival(piece):
        rows = pl.ds(piece * PIECE, PIECE)
        return pltpu.make_async_copy(dist.at[rows], held.at[rows], in_sems.at[piece])

    for piece in range(pieces):
        arrival(piece).start()

    @pl.loop(0, asked.shape[0])
    def _(device):
        target[asked[device]] = device

    for piece in range(pieces):
        arrival(piece).wait()
        cells = held[pl.ds(piece * PIECE, PIECE)].astype(jnp.float32)
        cells = cells.reshape(PIECE * CELLS, TOTAL).astype(jnp.bfloat16)
        sums[:, pl.ds(piece * PIECE * CELLS, PIECE * CELLS)] = lax.dot_general(
            basis[0:16, :], cells, (((1,), (1,)), ((), ())), preferred_element_type=jnp.float32
        )

    rows, fraction = coefficients_of(sums[...])
    exact = [[], [], []]
    for row in rows:
        for part in range(3):
            near = row.astype(jnp.bfloat16).astype(jnp.float32)
            exact[part].append(near)
            row = row - near
    zero = jnp.zeros((6, BLOCKS * CELLS), jnp.float32)
    stacked = jnp.concatenate(
        exact[0]
        + [zero]
        + exact[1]
        + [zero]
        + exact[2]
        + [zero, fraction, jnp.zeros((79, BLOCKS * CELLS), jnp.float32)],
        axis=0,
    )
    factors[...] = stacked.T

    @pl.loop(0, BLOCKS // GROUP)
    def _(group):
        first = group * GROUP
        own = factors[pl.ds(pl.multiple_of(first * CELLS, GROUP * CELLS), GROUP * CELLS), :]
        left = own.astype(jnp.bfloat16)
        fraction = own[:, 48:49]
        for step in range(TOTAL // STEP):
            lanes = pl.ds(step * STEP, STEP)
            gauss = jnp.exp2(
                jnp.dot(left, basis[:, lanes], preferred_element_type=jnp.float32)
            )
            moved = held[pl.ds(first, GROUP), :, lanes].astype(jnp.float32)
            moved = moved.reshape(GROUP * CELLS, STEP)
            mixed = moved + fraction * (gauss - moved)
            relaxed[pl.ds(first, GROUP), :, lanes] = mixed.reshape(GROUP, CELLS, STEP).astype(
                jnp.bfloat16
            )
        for block in range(GROUP):
            for chunk in range(CHUNKS):
                pltpu.make_async_copy(
                    relaxed.at[first + block, :, pl.ds(chunk * WIDTH, WIDTH)],
                    sends[chunk].at[target[first + block]],
                    out_sems.at[chunk],
                ).start()

    for chunk in range(CHUNKS):
        pltpu.make_async_copy(
            relaxed.at[:, :, pl.ds(chunk * WIDTH, WIDTH)],
            sends[chunk].at[pl.ds(0, BLOCKS)],
            out_sems.at[chunk],
        ).wait()


def collide(asked, dist, devices):
    return pl.pallas_call(
        collide_kernel,
        out_shape=[jax.ShapeDtypeStruct((devices, CELLS, WIDTH), jnp.bfloat16)] * CHUNKS,
        in_specs=[
            pl.BlockSpec(memory_space=pltpu.SMEM),
            pl.BlockSpec(memory_space=pl.ANY),
            pl.BlockSpec(memory_space=pltpu.VMEM),
        ],
        out_specs=[pl.BlockSpec(memory_space=pl.ANY)] * CHUNKS,
        scratch_shapes=[
            pltpu.VMEM((BLOCKS, CELLS, TOTAL), jnp.bfloat16),
            pltpu.VMEM((BLOCKS, CELLS, TOTAL), jnp.bfloat16),
            pltpu.VMEM((16, BLOCKS * CELLS), jnp.float32),
            pltpu.VMEM((BLOCKS * CELLS, 128), jnp.float32),
            pltpu.SMEM((devices,), jnp.int32),
            pltpu.SemaphoreType.DMA((BLOCKS // PIECE,)),
            pltpu.SemaphoreType.DMA((CHUNKS,)),
        ],
        compiler_params=pltpu.CompilerParams(vmem_limit_bytes=40 << 20),
        cost_estimate=pl.CostEstimate(
            flops=2 * BLOCKS * CELLS * TOTAL * 144,
            bytes_accessed=4 * BLOCKS * CELLS * TOTAL,
            transcendentals=BLOCKS * CELLS * TOTAL,
        ),
        name="collide",
    )(asked, dist, basis_rows())


def row_masks():
    row = lax.broadcasted_iota(jnp.int32, (CELLS, 128), 0)
    return row < 4, (row & 2) == 0, (row & 1) == 0


def swap(x, distance, low):
    if distance == 4:
        return pltpu.roll(x, 4, 0)
    return jnp.where(low, pltpu.roll(x, CELLS - distance, 0), pltpu.roll(x, distance, 0))


def faces_kernel(chunk, owner, received, mask, face_x, face_down, face_up, held, sems):
    low_x, low_y, _ = row_masks()
    x_first = 0 if chunk == 0 else (BX - 1) * SLAB

    def fetch(block, place, sem):
        pltpu.make_async_copy(received.at[owner[block]], held.at[place], sems.at[sem]).start()

    def block_y(pair, edge):
        return pair // 3 * SLAB + edge * BZ + pair % 3 * 2

    @pl.loop(0, SLAB)
    def _(i):
        fetch(x_first + i, i, 0)

    @pl.loop(0, 12)
    def _(pair):
        for side in range(2):
            fetch(block_y(pair, 0) + side, SLAB + 2 * pair + side, 1)
            fetch(block_y(pair, BY - 1) + side, 2 * SLAB + 2 * pair + side, 2)

    for sem in range(3):
        rows = pl.ds(sem * SLAB, SLAB)
        pltpu.make_async_copy(received.at[pl.ds(0, SLAB)], held.at[rows], sems.at[sem]).wait()

    @pl.loop(0, 12)
    def _(pair):
        def load(place, block, lanes):
            return held[place, :, lanes].astype(jnp.float32) * mask[block]

        for tile in range(TILES):
            lanes = pl.ds(tile * 128, 128)
            a, b = (load(2 * pair + s, x_first + 2 * pair + s, lanes) for s in range(2))
            keep = low_x if chunk == 0 else ~low_x
            face_x[pair, :, lanes] = jnp.where(keep, a, swap(b, 4, low_x)).astype(jnp.bfloat16)
            up = tile % 2
            edge = up * (BY - 1)
            place = SLAB + up * SLAB + 2 * pair
            a, b = (load(place + s, block_y(pair, edge) + s, lanes) for s in range(2))
            keep = ~low_y if up else low_y
            face = face_up if up else face_down
            face[pair, :, pl.ds(tile // 2 * 128, 128)] = jnp.where(
                keep, a, swap(b, 2, low_y)
            ).astype(jnp.bfloat16)


def faces(chunk, owner, received, mask):
    shapes = [(12, CELLS, WIDTH), (12, CELLS, WIDTH // 2), (12, CELLS, WIDTH // 2)]
    return pl.pallas_call(
        lambda *refs: faces_kernel(chunk, *refs),
        out_shape=[jax.ShapeDtypeStruct(s, jnp.bfloat16) for s in shapes],
        in_specs=[
            pl.BlockSpec(memory_space=pltpu.SMEM),
            pl.BlockSpec(memory_space=pl.ANY),
            pl.BlockSpec(memory_space=pltpu.VMEM),
        ],
        out_specs=[pl.BlockSpec(memory_space=pltpu.VMEM)] * 3,
        scratch_shapes=[
            pltpu.VMEM((3 * SLAB, CELLS, WIDTH), jnp.bfloat16),
            pltpu.SemaphoreType.DMA((3,)),
        ],
        compiler_params=pltpu.CompilerParams(vmem_limit_bytes=24 << 20),
        cost_estimate=pl.CostEstimate(
            flops=8 * SLAB * CELLS * WIDTH,
            bytes_accessed=8 * SLAB * CELLS * WIDTH,
            transcendentals=0,
        ),
        name=f"faces{chunk}",
    )(owner, received, mask)


def advance_kernel(chunk, owner, received, mask, rate, halo_x, halo_down, halo_up, *rest):
    out, held, kept, made, in_sems, out_sems = rest[-6:]
    low_x, low_y, low_z = row_masks()
    lane = lax.broadcasted_iota(jnp.int32, (CELLS, 128), 1)
    speed_z = SPACING * jnp.abs(2 * (lane % VS) + 1 - VS).astype(jnp.float32)
    speed_y = [
        SPACING * jnp.abs(2 * (lane // VS + 8 * odd) + 1 - VS).astype(jnp.float32) for odd in range(2)
    ]
    rising_z = lane % VS >= VS // 2
    from_below = rising_z & ~low_z
    from_above = ~rising_z & low_z

    def slab_copy(slab):
        rows = pl.ds(slab * SLAB, SLAB)
        return pltpu.make_async_copy(received.at[pl.ds(0, SLAB)], held.at[rows], in_sems.at[slab])

    for slab in range(BX):

        @pl.loop(slab * SLAB, slab * SLAB + SLAB)
        def _(block):
            pltpu.make_async_copy(
                received.at[owner[block]], held.at[block], in_sems.at[slab]
            ).start()

    kept[ZERO_BLOCK] = jnp.zeros((CELLS, WIDTH), jnp.float32)

    @pl.loop(0, 12)
    def _(pair):
        for tile in range(TILES):
            lanes = pl.ds(tile * 128, 128)
            face = halo_x[pair, :, lanes].astype(jnp.float32)
            kept[X_HALO + 2 * pair, :, lanes] = face
            kept[X_HALO + 2 * pair + 1, :, lanes] = swap(face, 4, low_x)
            halo = halo_down if tile % 2 else halo_up
            face = halo[pair, :, pl.ds(tile // 2 * 128, 128)].astype(jnp.float32)
            kept[Y_HALO + 2 * pair, :, lanes] = face
            kept[Y_HALO + 2 * pair + 1, :, lanes] = swap(face, 2, low_y)

    for slab in range(BX):
        slab_copy(slab).wait()

        @pl.loop(slab * SLAB, slab * SLAB + SLAB)
        def _(block):
            own_mask = mask[block]
            for tile in range(TILES):
                lanes = pl.ds(tile * 128, 128)
                kept[block, :, lanes] = held[block, :, lanes].astype(jnp.float32) * own_mask

    def result_copy(bx):
        rows = pl.ds(bx * SLAB, SLAB)
        return pltpu.make_async_copy(
            made.at[rows], out.at[rows, :, pl.ds(chunk * WIDTH, WIDTH)], out_sems.at[bx]
        )

    for bx in range(BX):

        @pl.loop(0, SLAB)
        def _(within):
            by, bz = within // BZ, within % BZ
            block = bx * SLAB + within
            if chunk == 0:
                next_x = X_HALO + within if bx == BX - 1 else block + SLAB
            else:
                next_x = X_HALO + within if bx == 0 else block - SLAB
            side = Y_HALO + bx * BZ + bz
            above_y = jnp.where(by == BY - 1, side, block + BZ)
            below_y = jnp.where(by == 0, side, block - BZ)
            above_z = jnp.where(bz == BZ - 1, ZERO_BLOCK, block + 1)
            below_z = jnp.where(bz == 0, ZERO_BLOCK, block - 1)
            own_rate = rate[block]
            for tile in range(TILES):
                lanes = pl.ds(tile * 128, 128)
                odd = tile % 2
                own = kept[block, :, lanes]
                other = kept[next_x, :, lanes]
                from_x = swap(
                    jnp.where(low_x, other, own) if chunk == 0 else jnp.where(low_x, own, other),
                    4,
                    low_x,
                )
                other = kept[below_y if odd else above_y, :, lanes]
                from_y = swap(
                    jnp.where(low_y, own, other) if odd else jnp.where(low_y, other, own), 2, low_y
                )
                from_z = swap(
                    jnp.where(
                        from_below,
                        kept[below_z, :, lanes],
                        jnp.where(from_above, kept[above_z, :, lanes], own),
                    ),
                    1,
                    low_z,
                )
                speed_x = SPACING * abs(2 * (chunk * (VS // CHUNKS) + tile // 2) + 1 - VS)
                flux = (
                    speed_x * (own - from_x)
                    + speed_y[odd] * (own - from_y)
                    + speed_z * (own - from_z)
                )
                made[block, :, lanes] = (own - own_rate * flux).astype(jnp.bfloat16)

        result_copy(bx).start()
    for bx in range(BX):
        result_copy(bx).wait()


def advance(chunk, owner, received, mask, rate, halos, earlier):
    anywhere = pl.BlockSpec(memory_space=pl.ANY)
    vmem = pl.BlockSpec(memory_space=pltpu.VMEM)
    extra = [] if earlier is None else [earlier]
    return pl.pallas_call(
        lambda *refs: advance_kernel(chunk, *refs),
        out_shape=jax.ShapeDtypeStruct((BLOCKS, CELLS, TOTAL), jnp.bfloat16),
        in_specs=[pl.BlockSpec(memory_space=pltpu.SMEM), anywhere]
        + [vmem] * 5
        + [anywhere] * len(extra),
        out_specs=anywhere,
        scratch_shapes=[
            pltpu.VMEM((BLOCKS, CELLS, WIDTH), jnp.bfloat16),
            pltpu.VMEM((HELD, CELLS, WIDTH), jnp.float32),
            pltpu.VMEM((BLOCKS, CELLS, WIDTH), jnp.bfloat16),
            pltpu.SemaphoreType.DMA((BX,)),
            pltpu.SemaphoreType.DMA((BX,)),
        ],
        input_output_aliases={} if earlier is None else {7: 0},
        compiler_params=pltpu.CompilerParams(vmem_limit_bytes=40 << 20),
        cost_estimate=pl.CostEstimate(
            flops=24 * BLOCKS * CELLS * WIDTH,
            bytes_accessed=5 * BLOCKS * CELLS * WIDTH,
            transcendentals=0,
        ),
        name=f"advance{chunk}",
    )(owner, received, mask, rate, *halos, *extra)


def after(received, source_owner, levels, active):
    n_gx, n_gy = lax.axis_size("gx"), lax.axis_size("gy")
    mask = jnp.broadcast_to(
        active.astype(jnp.float32)[:, :, None], (BLOCKS, CELLS, 128)
    )
    courant = COURANT * jnp.exp2(levels.astype(jnp.float32))
    rate = mask * courant[:, None, None]

    def up(n):
        return [(i, i + 1) for i in range(n - 1)]

    def down(n):
        return [(i + 1, i) for i in range(n - 1)]

    out = None
    for chunk in range(CHUNKS):
        face_x, face_down, face_up = faces(chunk, source_owner, received[chunk], mask)
        halos = (
            lax.ppermute(face_x, "gx", down(n_gx) if chunk == 0 else up(n_gx)),
            lax.ppermute(face_up, "gy", up(n_gy)),
            lax.ppermute(face_down, "gy", down(n_gy)),
        )
        out = advance(chunk, source_owner, received[chunk], mask, rate, halos, out)
    return out


def per_device(dist_old, source_owner, levels, active):
    axes = ("gx", "gy")
    n_gx, n_gy = lax.axis_size("gx"), lax.axis_size("gy")
    devices = n_gx * n_gy
    slots = lax.broadcasted_iota(jnp.int32, (devices, BLOCKS), 1)
    owners = lax.broadcasted_iota(jnp.int32, (devices, BLOCKS), 0)
    request = BLOCKS + jnp.sum(
        jnp.where(source_owner[None, :] == owners, slots - BLOCKS, 0), axis=1
    )
    asked = lax.all_to_all(
        request.reshape(devices, 1), axes, split_axis=0, concat_axis=0, tiled=True
    ).reshape(devices)
    sends = collide(asked, dist_old, devices)

    received = [
        lax.all_to_all(s, axes, split_axis=0, concat_axis=0, tiled=True) for s in sends
    ]
    return after(received, source_owner, levels, active)


def solution(mesh):
    return jax.shard_map(
        per_device,
        mesh=mesh,
        in_specs=(
            P(("gx", "gy"), None, None),
            P(("gx", "gy")),
            P(("gx", "gy")),
            P(("gx", "gy"), None),
        ),
        out_specs=P(("gx", "gy"), None, None),
        check_vma=False,
    )
```

```python
import math

import jax
import jax.numpy as jnp
import ml_dtypes
import numpy as np
from jax import lax
from jax.experimental import pallas as pl
from jax.experimental.pallas import tpu as pltpu
from jax.sharding import PartitionSpec as P

VS = 16
BX, BY, BZ = 4, 4, 6
BLOCKS = BX * BY * BZ
TOTAL = VS * VS * VS
CELLS = 8
SLAB = BY * BZ
RELAX_INCREMENT = 0.3
COURANT = 0.028
SPACING = 3.0 / VS
LOG2E = 1.0 / math.log(2.0)

SPLIT = (0, 24, 32)
CHUNKS = len(SPLIT) - 1
PIECE = 16
GROUP = 8
STEP = 512
X_HALO = BLOCKS
Y_HALO = X_HALO + SLAB
HELD = Y_HALO + BX * BZ


def lanes_of(chunk):
    return pl.ds(SPLIT[chunk] * 128, width_of(chunk))


def width_of(chunk):
    return 128 * (SPLIT[chunk + 1] - SPLIT[chunk])


def tiles_of(chunk):
    found, count_x, count_y = [], [0, 0], [0, 0]
    for tile in range(SPLIT[chunk], SPLIT[chunk + 1]):
        x, y = int(tile >= TOTAL // 256), tile % 2
        found.append((tile - SPLIT[chunk], x, y, count_x[x], count_y[y]))
        count_x[x] += 1
        count_y[y] += 1
    return found, count_x, count_y


def lanes(tile):
    return pl.ds(tile * 128, 128)


def basis_rows():
    index = np.arange(TOTAL)
    x, y, z = (2 * i + 1 - VS for i in (index // (VS * VS), index // VS % VS, index % VS))
    rows = np.zeros((16, TOTAL), np.float32)
    rows[:10] = [np.ones_like(x), x, y, z, x * x, y * y, z * z, x * y, x * z, y * z]
    whole = np.zeros((128, TOTAL), np.float32)
    for copy in range(3):
        whole[16 * copy : 16 * copy + 16] = rows
    return whole.astype(ml_dtypes.bfloat16)


def coefficients_of(sums):
    raw = [sums[i : i + 1] * (1.0 / TOTAL) for i in range(10)]
    density = raw[0]
    drift = [SPACING * raw[1 + a] / density for a in range(3)]
    square = SPACING * SPACING
    spread = [square * raw[4 + a] / density - drift[a] * drift[a] for a in range(3)]
    spread_xy = square * raw[7] / density - drift[0] * drift[1]
    spread_xz = square * raw[8] / density - drift[0] * drift[2]
    spread_yz = square * raw[9] / density - drift[1] * drift[2]
    temperature = (spread[0] + spread[1] + spread[2]) / 3.0
    xx, yy, zz = (1.5 * temperature - 0.5 * s for s in spread)
    xy, xz, yz = (-0.5 * s for s in (spread_xy, spread_xz, spread_yz))
    adj_xx, adj_yy, adj_zz = yy * zz - yz * yz, xx * zz - xz * xz, xx * yy - xy * xy
    adj_xy, adj_xz, adj_yz = xz * yz - xy * zz, xy * yz - xz * yy, xy * xz - xx * yz
    determinant = xx * adj_xx + xy * adj_xy + xz * adj_xz
    inv = [a / determinant for a in (adj_xx, adj_yy, adj_zz, adj_xy, adj_xz, adj_yz)]
    pull = [
        inv[0] * drift[0] + inv[3] * drift[1] + inv[4] * drift[2],
        inv[3] * drift[0] + inv[1] * drift[1] + inv[5] * drift[2],
        inv[4] * drift[0] + inv[5] * drift[1] + inv[2] * drift[2],
    ]
    quadratic = drift[0] * pull[0] + drift[1] * pull[1] + drift[2] * pull[2]
    log_prefactor = (
        jnp.log(density)
        + (3.0 * math.log(6.0) - 1.5 * math.log(2.0 * math.pi))
        - 0.5 * jnp.log(determinant)
    )
    rows = [log_prefactor - 0.5 * quadratic]
    rows += [SPACING * p for p in pull]
    rows += [-0.5 * square * i for i in inv[:3]]
    rows += [-square * i for i in inv[3:]]
    fraction = 1.0 - jnp.exp(-RELAX_INCREMENT * density * jnp.sqrt(temperature))
    return [LOG2E * r for r in rows], fraction


def relax_kernel(dist, basis, *rest):
    outs = rest[:CHUNKS]
    held, relaxed, sums, factors, in_sems, out_sems = rest[CHUNKS:]
    pieces = BLOCKS // PIECE

    def arrival(piece):
        rows = pl.ds(piece * PIECE, PIECE)
        return pltpu.make_async_copy(dist.at[rows], held.at[rows], in_sems.at[piece])

    def departure(first, count, chunk):
        rows, lanes = pl.ds(first, count), lanes_of(chunk)
        return pltpu.make_async_copy(
            relaxed.at[rows, :, lanes], outs[chunk].at[rows], out_sems.at[chunk]
        )

    for piece in range(pieces):
        arrival(piece).start()
    for piece in range(pieces):
        arrival(piece).wait()
        cells = held[pl.ds(piece * PIECE, PIECE)].astype(jnp.float32)
        cells = cells.reshape(PIECE * CELLS, TOTAL).astype(jnp.bfloat16)
        sums[:, pl.ds(piece * PIECE * CELLS, PIECE * CELLS)] = lax.dot_general(
            basis[0:16, :], cells, (((1,), (1,)), ((), ())), preferred_element_type=jnp.float32
        )

    rows, fraction = coefficients_of(sums[...])
    exact = [[], [], []]
    for row in rows:
        for part in range(3):
            near = row.astype(jnp.bfloat16).astype(jnp.float32)
            exact[part].append(near)
            row = row - near
    zero = jnp.zeros((6, BLOCKS * CELLS), jnp.float32)
    stacked = jnp.concatenate(
        exact[0]
        + [zero]
        + exact[1]
        + [zero]
        + exact[2]
        + [zero, fraction, jnp.zeros((79, BLOCKS * CELLS), jnp.float32)],
        axis=0,
    )
    factors[...] = stacked.T

    @pl.loop(0, BLOCKS // GROUP)
    def _(group):
        first = group * GROUP
        own = factors[pl.ds(pl.multiple_of(first * CELLS, GROUP * CELLS), GROUP * CELLS), :]
        left = own.astype(jnp.bfloat16)
        fraction = jnp.broadcast_to(own[:, 48:49], (GROUP * CELLS, 128))
        for step in range(TOTAL // STEP):
            power = jnp.dot(
                left, basis[:, pl.ds(step * STEP, STEP)], preferred_element_type=jnp.float32
            )
            for tile in range(STEP // 128):
                lanes = pl.ds(step * STEP + tile * 128, 128)
                gauss = jnp.exp2(power[:, tile * 128 : tile * 128 + 128])
                moved = held[pl.ds(first, GROUP), :, lanes].astype(jnp.float32)
                moved = moved.reshape(GROUP * CELLS, 128)
                mixed = moved + fraction * (gauss - moved)
                relaxed[pl.ds(first, GROUP), :, lanes] = mixed.reshape(
                    GROUP, CELLS, 128
                ).astype(jnp.bfloat16)
        for chunk in range(CHUNKS):
            departure(first, GROUP, chunk).start()

    for chunk in range(CHUNKS):
        departure(0, BLOCKS, chunk).wait()


def relax(dist):
    return pl.pallas_call(
        relax_kernel,
        out_shape=[
            jax.ShapeDtypeStruct((BLOCKS, CELLS, width_of(c)), jnp.bfloat16) for c in range(CHUNKS)
        ],
        in_specs=[
            pl.BlockSpec(memory_space=pl.ANY),
            pl.BlockSpec(memory_space=pltpu.VMEM),
        ],
        out_specs=[pl.BlockSpec(memory_space=pl.ANY)] * CHUNKS,
        scratch_shapes=[
            pltpu.VMEM((BLOCKS, CELLS, TOTAL), jnp.bfloat16),
            pltpu.VMEM((BLOCKS, CELLS, TOTAL), jnp.bfloat16),
            pltpu.VMEM((16, BLOCKS * CELLS), jnp.float32),
            pltpu.VMEM((BLOCKS * CELLS, 128), jnp.float32),
            pltpu.SemaphoreType.DMA((BLOCKS // PIECE,)),
            pltpu.SemaphoreType.DMA((CHUNKS,)),
        ],
        compiler_params=pltpu.CompilerParams(vmem_limit_bytes=60 << 20),
        cost_estimate=pl.CostEstimate(
            flops=2 * BLOCKS * CELLS * TOTAL * 1500,
            bytes_accessed=4 * BLOCKS * CELLS * TOTAL,
            transcendentals=BLOCKS * CELLS * TOTAL,
        ),
        name="relax",
    )(dist, basis_rows())


def pack_kernel(asked, relaxed, send, sem):
    @pl.loop(0, asked.shape[0])
    def _(device):
        slot = asked[device]

        @pl.when(slot < BLOCKS)
        def _():
            pltpu.make_async_copy(relaxed.at[slot], send.at[device], sem).start()

    pltpu.make_async_copy(relaxed, send.at[pl.ds(0, BLOCKS)], sem).wait()


def pack(chunk, asked, relaxed, devices):
    width = width_of(chunk)
    return pl.pallas_call(
        pack_kernel,
        out_shape=jax.ShapeDtypeStruct((devices, CELLS, width), jnp.bfloat16),
        in_specs=[
            pl.BlockSpec(memory_space=pltpu.SMEM),
            pl.BlockSpec(memory_space=pl.ANY),
        ],
        out_specs=pl.BlockSpec(memory_space=pl.ANY),
        scratch_shapes=[pltpu.SemaphoreType.DMA(())],
        cost_estimate=pl.CostEstimate(
            flops=0, bytes_accessed=4 * BLOCKS * CELLS * width, transcendentals=0
        ),
        name=f"pack{chunk}",
    )(asked, relaxed)


def row_masks():
    row = lax.broadcasted_iota(jnp.int32, (CELLS, 128), 0)
    return row < 4, (row & 2) == 0, (row & 1) == 0


def swap(x, distance):
    if distance == 4:
        return pltpu.roll(x, 4, 0)
    row = lax.broadcasted_iota(jnp.int32, (CELLS, 128), 0)
    return jnp.take_along_axis(x, row ^ distance, axis=0)


def face_kinds(chunk):
    _, count_x, count_y = tiles_of(chunk)
    counts = [("x", 0, count_x[0]), ("x", 1, count_x[1]), ("y", 0, count_y[0]), ("y", 1, count_y[1])]
    return [k for k in counts if k[2]]


def face_block(axis, up, pair):
    if axis == "x":
        return (BX - 1) * SLAB * up + 2 * pair
    return pair // 3 * SLAB + up * (BY - 1) * BZ + pair % 3 * 2


def faces_kernel(chunk, owner, received, mask, *rest):
    kinds = face_kinds(chunk)
    faces, (held, sems) = rest[: len(kinds)], rest[len(kinds) :]
    low_x, low_y, _ = row_masks()

    for n, (axis, up, _) in enumerate(kinds):

        @pl.loop(0, 12)
        def _(pair):
            for side in range(2):
                block = face_block(axis, up, pair) + side
                pltpu.make_async_copy(
                    received.at[owner[block]], held.at[n * SLAB + 2 * pair + side], sems.at[n]
                ).start()

    for n, (axis, up, _) in enumerate(kinds):
        rows = pl.ds(n * SLAB, SLAB)
        pltpu.make_async_copy(received.at[pl.ds(0, SLAB)], held.at[rows], sems.at[n]).wait()

        @pl.loop(0, 12)
        def _(pair):
            block = face_block(axis, up, pair)
            masks = [mask[block + side] for side in range(2)]
            for tile, x, y, place_x, place_y in tiles_of(chunk)[0]:
                if up != (x if axis == "x" else y):
                    continue
                a, b = (
                    held[n * SLAB + 2 * pair + side, :, lanes(tile)].astype(jnp.float32)
                    * masks[side]
                    for side in range(2)
                )
                low = low_x if axis == "x" else low_y
                b = swap(b, 4 if axis == "x" else 2)
                face = jnp.where(low, b, a) if up else jnp.where(low, a, b)
                place = place_x if axis == "x" else place_y
                faces[n][pair, :, lanes(place)] = face.astype(jnp.bfloat16)


def faces(chunk, owner, received, mask):
    kinds = face_kinds(chunk)
    moved = sum(128 * tiles for _, _, tiles in kinds)
    return pl.pallas_call(
        lambda *refs: faces_kernel(chunk, *refs),
        out_shape=[
            jax.ShapeDtypeStruct((12, CELLS, 128 * tiles), jnp.bfloat16) for _, _, tiles in kinds
        ],
        in_specs=[
            pl.BlockSpec(memory_space=pltpu.SMEM),
            pl.BlockSpec(memory_space=pl.ANY),
            pl.BlockSpec(memory_space=pltpu.VMEM),
        ],
        out_specs=[pl.BlockSpec(memory_space=pltpu.VMEM)] * len(kinds),
        scratch_shapes=[
            pltpu.VMEM((len(kinds) * SLAB, CELLS, width_of(chunk)), jnp.bfloat16),
            pltpu.SemaphoreType.DMA((len(kinds),)),
        ],
        compiler_params=pltpu.CompilerParams(vmem_limit_bytes=20 << 20),
        cost_estimate=pl.CostEstimate(
            flops=8 * SLAB * CELLS * moved,
            bytes_accessed=8 * SLAB * CELLS * moved,
            transcendentals=0,
        ),
        name=f"faces{chunk}",
    )(owner, received, mask)


def advance_kernel(chunk, owner, received, mask, rate, *rest):
    kinds = face_kinds(chunk)
    halos, (out, held, kept, made, in_sems, out_sems) = rest[: len(kinds)], rest[-6:]
    tiles = tiles_of(chunk)[0]
    low_x, low_y, low_z = row_masks()
    lane = lax.broadcasted_iota(jnp.int32, (CELLS, 128), 1)
    speed_z = SPACING * jnp.abs(2 * (lane % VS) + 1 - VS).astype(jnp.float32)
    speed_y = [
        SPACING * jnp.abs(2 * (lane // VS + 8 * odd) + 1 - VS).astype(jnp.float32)
        for odd in range(2)
    ]
    rising_z = lane % VS >= VS // 2
    from_below = rising_z & ~low_z
    from_above = ~rising_z & low_z
    nothing = jnp.zeros((CELLS, 128), jnp.float32)

    for slab in range(BX):

        @pl.loop(slab * SLAB, slab * SLAB + SLAB)
        def _(block):
            pltpu.make_async_copy(
                received.at[owner[block]], held.at[block], in_sems.at[slab]
            ).start()

    for (axis, up, _), halo in zip(kinds, halos):

        @pl.loop(0, 12)
        def _(pair):
            for tile, x, y, place_x, place_y in tiles:
                if up != (x if axis == "x" else y):
                    continue
                place = place_x if axis == "x" else place_y
                first = X_HALO if axis == "x" else Y_HALO
                face = halo[pair, :, lanes(place)].astype(jnp.float32)
                kept[first + 2 * pair, :, lanes(tile)] = face
                kept[first + 2 * pair + 1, :, lanes(tile)] = swap(face, 4 if axis == "x" else 2)

    for slab in range(BX):
        rows = pl.ds(slab * SLAB, SLAB)
        pltpu.make_async_copy(received.at[pl.ds(0, SLAB)], held.at[rows], in_sems.at[slab]).wait()

        @pl.loop(slab * SLAB, slab * SLAB + SLAB)
        def _(block):
            own_mask = mask[block]
            for tile in range(len(tiles)):
                kept[block, :, lanes(tile)] = (
                    held[block, :, lanes(tile)].astype(jnp.float32) * own_mask
                )

    def result_copy(bx):
        rows = pl.ds(bx * SLAB, SLAB)
        return pltpu.make_async_copy(
            made.at[rows], out.at[rows, :, lanes_of(chunk)], out_sems.at[bx]
        )

    for bx in range(BX):

        @pl.loop(0, BY)
        def _(by):
            line = bx * SLAB + by * BZ
            side = Y_HALO + bx * BZ
            near_y = [
                jnp.where(by == BY - 1, side, line + BZ),
                jnp.where(by == 0, side, line - BZ),
            ]
            near_x = [
                X_HALO + by * BZ if bx == BX - 1 else line + SLAB,
                X_HALO + by * BZ if bx == 0 else line - SLAB,
            ]
            for tile, x, y, _, _ in tiles:
                own_line = [kept[line + bz, :, lanes(tile)] for bz in range(BZ)]
                speed_x = SPACING * abs(2 * ((SPLIT[chunk] + tile) // 2) + 1 - VS)
                for bz in range(BZ):
                    own = own_line[bz]
                    below = own_line[bz - 1] if bz else nothing
                    above = own_line[bz + 1] if bz < BZ - 1 else nothing
                    other = kept[near_x[x] + bz, :, lanes(tile)]
                    from_x = swap(
                        jnp.where(low_x, own, other) if x else jnp.where(low_x, other, own), 4
                    )
                    other = kept[near_y[y] + bz, :, lanes(tile)]
                    from_y = swap(
                        jnp.where(low_y, own, other) if y else jnp.where(low_y, other, own), 2
                    )
                    from_z = swap(
                        jnp.where(from_below, below, jnp.where(from_above, above, own)), 1
                    )
                    flux = (
                        speed_x * (own - from_x)
                        + speed_y[y] * (own - from_y)
                        + speed_z * (own - from_z)
                    )
                    made[line + bz, :, lanes(tile)] = (own - rate[line + bz] * flux).astype(
                        jnp.bfloat16
                    )

        result_copy(bx).start()
    for bx in range(BX):
        result_copy(bx).wait()


def advance(chunk, owner, received, mask, rate, halos, earlier):
    anywhere = pl.BlockSpec(memory_space=pl.ANY)
    vmem = pl.BlockSpec(memory_space=pltpu.VMEM)
    extra = [] if earlier is None else [earlier]
    width = width_of(chunk)
    return pl.pallas_call(
        lambda *refs: advance_kernel(chunk, *refs),
        out_shape=jax.ShapeDtypeStruct((BLOCKS, CELLS, TOTAL), jnp.bfloat16),
        in_specs=[pl.BlockSpec(memory_space=pltpu.SMEM), anywhere]
        + [vmem] * (2 + len(halos))
        + [anywhere] * len(extra),
        out_specs=anywhere,
        scratch_shapes=[
            pltpu.VMEM((BLOCKS, CELLS, width), jnp.bfloat16),
            pltpu.VMEM((HELD, CELLS, width), jnp.float32),
            pltpu.VMEM((BLOCKS, CELLS, width), jnp.bfloat16),
            pltpu.SemaphoreType.DMA((BX,)),
            pltpu.SemaphoreType.DMA((BX,)),
        ],
        input_output_aliases={} if earlier is None else {4 + len(halos): 0},
        compiler_params=pltpu.CompilerParams(vmem_limit_bytes=40 << 20),
        cost_estimate=pl.CostEstimate(
            flops=100 * BLOCKS * CELLS * width,
            bytes_accessed=5 * BLOCKS * CELLS * width,
            transcendentals=0,
        ),
        name=f"advance{chunk}",
    )(owner, received, mask, rate, *halos, *extra)


def after(received, source_owner, levels, active):
    n_gx, n_gy = lax.axis_size("gx"), lax.axis_size("gy")
    mask = jnp.broadcast_to(
        active.astype(jnp.float32)[:, :, None], (BLOCKS, CELLS, 128)
    )
    courant = COURANT * jnp.exp2(levels.astype(jnp.float32))
    rate = mask * courant[:, None, None]

    def up(n):
        return [(i, i + 1) for i in range(n - 1)]

    def down(n):
        return [(i + 1, i) for i in range(n - 1)]

    out = None
    for chunk in range(CHUNKS):
        arrived = received[chunk]
        if out is not None:
            arrived, out = lax.optimization_barrier((arrived, out))
        sent = faces(chunk, source_owner, arrived, mask)
        halos = []
        for (axis, to_above, _), face in zip(face_kinds(chunk), sent):
            name, n = ("gx", n_gx) if axis == "x" else ("gy", n_gy)
            halos.append(lax.ppermute(face, name, up(n) if to_above else down(n)))
        out = advance(chunk, source_owner, arrived, mask, rate, halos, out)
    return out


def per_device(dist_old, source_owner, levels, active):
    axes = ("gx", "gy")
    n_gx, n_gy = lax.axis_size("gx"), lax.axis_size("gy")
    devices = n_gx * n_gy
    slots = lax.broadcasted_iota(jnp.int32, (devices, BLOCKS), 1)
    owners = lax.broadcasted_iota(jnp.int32, (devices, BLOCKS), 0)
    request = BLOCKS + jnp.sum(
        jnp.where(source_owner[None, :] == owners, slots - BLOCKS, 0), axis=1
    )
    asked = lax.all_to_all(request, axes, split_axis=0, concat_axis=0, tiled=True)
    received = [
        lax.all_to_all(
            pack(chunk, asked, relaxed, devices), axes, split_axis=0, concat_axis=0, tiled=True
        )
        for chunk, relaxed in enumerate(relax(dist_old))
    ]
    return after(received, source_owner, levels, active)


def solution(mesh):
    return jax.shard_map(
        per_device,
        mesh=mesh,
        in_specs=(
            P(("gx", "gy"), None, None),
            P(("gx", "gy")),
            P(("gx", "gy")),
            P(("gx", "gy"), None),
        ),
        out_specs=P(("gx", "gy"), None, None),
        check_vma=False,
    )
```

```python
import math

import jax
import jax.numpy as jnp
import ml_dtypes
import numpy as np
from jax import lax
from jax.experimental import pallas as pl
from jax.experimental.pallas import tpu as pltpu
from jax.sharding import PartitionSpec as P

VS = 16
BX, BY, BZ = 4, 4, 6
BLOCKS = BX * BY * BZ
TOTAL = VS * VS * VS
CELLS = 8
SLAB = BY * BZ
RELAX_INCREMENT = 0.3
COURANT = 0.028
SPACING = 3.0 / VS
LOG2E = 1.0 / math.log(2.0)

TILES = TOTAL // 128
PIECE = 16
RELAX_VMEM = 60 << 20
PACK_VMEM = 54 << 20
FACES_VMEM = 16 << 20
ADVANCE_VMEM = 28 << 20
EDGE_VMEM = 20 << 20
GROUP = 8
STEP = 512


def lanes(tile):
    return pl.ds(tile * 128, 128)


def basis_rows():
    index = np.arange(TOTAL)
    x, y, z = (2 * i + 1 - VS for i in (index // (VS * VS), index // VS % VS, index % VS))
    rows = np.zeros((16, TOTAL), np.float32)
    rows[:10] = [np.ones_like(x), x, y, z, x * x, y * y, z * z, x * y, x * z, y * z]
    whole = np.zeros((48, TOTAL), np.float32)
    for copy in range(3):
        whole[16 * copy : 16 * copy + 16] = rows
    return whole.astype(ml_dtypes.bfloat16)


def coefficients_of(sums):
    raw = [sums[i : i + 1] * (1.0 / TOTAL) for i in range(10)]
    density = raw[0]
    drift = [SPACING * raw[1 + a] / density for a in range(3)]
    square = SPACING * SPACING
    spread = [square * raw[4 + a] / density - drift[a] * drift[a] for a in range(3)]
    spread_xy = square * raw[7] / density - drift[0] * drift[1]
    spread_xz = square * raw[8] / density - drift[0] * drift[2]
    spread_yz = square * raw[9] / density - drift[1] * drift[2]
    temperature = (spread[0] + spread[1] + spread[2]) / 3.0
    xx, yy, zz = (1.5 * temperature - 0.5 * s for s in spread)
    xy, xz, yz = (-0.5 * s for s in (spread_xy, spread_xz, spread_yz))
    adj_xx, adj_yy, adj_zz = yy * zz - yz * yz, xx * zz - xz * xz, xx * yy - xy * xy
    adj_xy, adj_xz, adj_yz = xz * yz - xy * zz, xy * yz - xz * yy, xy * xz - xx * yz
    determinant = xx * adj_xx + xy * adj_xy + xz * adj_xz
    inv = [a / determinant for a in (adj_xx, adj_yy, adj_zz, adj_xy, adj_xz, adj_yz)]
    pull = [
        inv[0] * drift[0] + inv[3] * drift[1] + inv[4] * drift[2],
        inv[3] * drift[0] + inv[1] * drift[1] + inv[5] * drift[2],
        inv[4] * drift[0] + inv[5] * drift[1] + inv[2] * drift[2],
    ]
    quadratic = drift[0] * pull[0] + drift[1] * pull[1] + drift[2] * pull[2]
    log_prefactor = (
        jnp.log(density)
        + (3.0 * math.log(6.0) - 1.5 * math.log(2.0 * math.pi))
        - 0.5 * jnp.log(determinant)
    )
    rows = [log_prefactor - 0.5 * quadratic]
    rows += [SPACING * p for p in pull]
    rows += [-0.5 * square * i for i in inv[:3]]
    rows += [-square * i for i in inv[3:]]
    fraction = 1.0 - jnp.exp(-RELAX_INCREMENT * density * jnp.sqrt(temperature))
    return [LOG2E * r for r in rows], fraction


def relax_kernel(dist, basis, out, held, relaxed, sums, factors, in_sems, out_sem):
    pieces = BLOCKS // PIECE

    def arrival(piece):
        rows = pl.ds(piece * PIECE, PIECE)
        return pltpu.make_async_copy(dist.at[rows], held.at[rows], in_sems.at[piece])

    for piece in range(pieces):
        arrival(piece).start()
    for piece in range(pieces):
        arrival(piece).wait()
        cells = held[pl.ds(piece * PIECE, PIECE)].astype(jnp.float32)
        cells = cells.reshape(PIECE * CELLS, TOTAL).astype(jnp.bfloat16)
        sums[:, pl.ds(piece * PIECE * CELLS, PIECE * CELLS)] = lax.dot_general(
            basis[0:16, :], cells, (((1,), (1,)), ((), ())), preferred_element_type=jnp.float32
        )

    rows, fraction = coefficients_of(sums[...])
    exact = [[], [], []]
    for row in rows:
        for part in range(3):
            near = row.astype(jnp.bfloat16).astype(jnp.float32)
            exact[part].append(near)
            row = row - near
    zero = jnp.zeros((6, BLOCKS * CELLS), jnp.float32)
    stacked = jnp.concatenate(
        exact[0]
        + [zero]
        + exact[1]
        + [zero]
        + exact[2]
        + [zero, fraction, jnp.zeros((79, BLOCKS * CELLS), jnp.float32)],
        axis=0,
    )
    factors[...] = stacked.T

    @pl.loop(0, BLOCKS // GROUP)
    def _(group):
        first = group * GROUP
        own = factors[pl.ds(pl.multiple_of(first * CELLS, GROUP * CELLS), GROUP * CELLS), :]
        left = own[:, :48].astype(jnp.bfloat16)
        fraction = jnp.broadcast_to(own[:, 48:49], (GROUP * CELLS, 128))
        for step in range(TOTAL // STEP):
            power = jnp.dot(
                left, basis[:, pl.ds(step * STEP, STEP)], preferred_element_type=jnp.float32
            )
            for tile in range(STEP // 128):
                place = lanes(step * (STEP // 128) + tile)
                gauss = jnp.exp2(power[:, tile * 128 : tile * 128 + 128])
                moved = held[pl.ds(first, GROUP), :, place].astype(jnp.float32)
                moved = moved.reshape(GROUP * CELLS, 128)
                mixed = moved + fraction * (gauss - moved)
                relaxed[pl.ds(first, GROUP), :, place] = mixed.reshape(
                    GROUP, CELLS, 128
                ).astype(jnp.bfloat16)
        rows = pl.ds(first, GROUP)
        pltpu.make_async_copy(relaxed.at[rows], out.at[rows], out_sem).start()

    pltpu.make_async_copy(relaxed, out, out_sem).wait()


VMEM = pl.BlockSpec(memory_space=pltpu.VMEM)
ANY = pl.BlockSpec(memory_space=pl.ANY)
WHOLE = (BLOCKS, CELLS, TOTAL)


def relax(dist):
    return pl.pallas_call(
        relax_kernel,
        out_shape=jax.ShapeDtypeStruct(WHOLE, jnp.bfloat16),
        in_specs=[ANY, VMEM],
        out_specs=ANY,
        scratch_shapes=[
            pltpu.VMEM(WHOLE, jnp.bfloat16),
            pltpu.VMEM(WHOLE, jnp.bfloat16),
            pltpu.VMEM((16, BLOCKS * CELLS), jnp.float32),
            pltpu.VMEM((BLOCKS * CELLS, 128), jnp.float32),
            pltpu.SemaphoreType.DMA((BLOCKS // PIECE,)),
            pltpu.SemaphoreType.DMA(()),
        ],
        compiler_params=pltpu.CompilerParams(vmem_limit_bytes=RELAX_VMEM),
        cost_estimate=pl.CostEstimate(
            flops=2 * BLOCKS * CELLS * TOTAL * 1500,
            bytes_accessed=4 * BLOCKS * CELLS * TOTAL,
            transcendentals=BLOCKS * CELLS * TOTAL,
        ),
        name="relax",
    )(dist, basis_rows())


def pack_kernel(asked, relaxed, send, held, row, target, row_sem, in_sems, out_sem):
    def arrival(piece):
        rows = pl.ds(piece * PIECE, PIECE)
        return pltpu.make_async_copy(relaxed.at[rows], held.at[rows], in_sems.at[piece])

    for piece in range(BLOCKS // PIECE):
        arrival(piece).start()
    device = lax.broadcasted_iota(jnp.int32, asked.shape, 0)
    slot = lax.broadcasted_iota(jnp.int32, asked.shape, 1)
    row[...] = jnp.broadcast_to(
        jnp.sum(jnp.where(asked[...] == slot, device, 0), axis=0, keepdims=True), row.shape
    )
    to_scalars = pltpu.make_async_copy(row, target, row_sem)
    to_scalars.start()
    to_scalars.wait()
    for piece in range(BLOCKS // PIECE):
        arrival(piece).wait()
        for block in range(piece * PIECE, piece * PIECE + PIECE):
            pltpu.make_async_copy(held.at[block], send.at[target[0, block]], out_sem).start()
    pltpu.make_async_copy(held, send.at[pl.ds(0, BLOCKS)], out_sem).wait()


def pack(asked, relaxed):
    devices = asked.shape[0]
    return pl.pallas_call(
        pack_kernel,
        out_shape=jax.ShapeDtypeStruct((devices, CELLS, TOTAL), jnp.bfloat16),
        in_specs=[VMEM, ANY],
        out_specs=ANY,
        scratch_shapes=[
            pltpu.VMEM(WHOLE, jnp.bfloat16),
            pltpu.VMEM((8, 128), jnp.int32),
            pltpu.SMEM((8, 128), jnp.int32),
            pltpu.SemaphoreType.DMA(()),
            pltpu.SemaphoreType.DMA((BLOCKS // PIECE,)),
            pltpu.SemaphoreType.DMA(()),
        ],
        compiler_params=pltpu.CompilerParams(vmem_limit_bytes=PACK_VMEM),
        cost_estimate=pl.CostEstimate(
            flops=0, bytes_accessed=4 * BLOCKS * CELLS * TOTAL, transcendentals=0
        ),
        name="pack",
    )(asked, relaxed)


def row_masks():
    row = lax.broadcasted_iota(jnp.int32, (CELLS, 128), 0)
    return row < 4, (row & 2) == 0, (row & 1) == 0


def swap(x, distance):
    if distance == 4:
        return pltpu.roll(x, 4, 0)
    row = lax.broadcasted_iota(jnp.int32, (CELLS, 128), 0)
    return jnp.take_along_axis(x, row ^ distance, axis=0)


PARTS = 4
FACES = (("y", 0), ("y", 1), ("x", 0), ("x", 1))
FACE = (12, CELLS, TOTAL // 2)


def face_block(axis, up, pair):
    if axis == "x":
        return (BX - 1) * SLAB * up + 2 * pair
    return pair // 3 * SLAB + up * (BY - 1) * BZ + pair % 3 * 2


def face_tiles(axis, up):
    return [t for t in range(TILES) if up == (t % 2 if axis == "y" else t // (TILES // 2))]


def faces_kernel(owner, arrived, mask, *rest):
    sent, (received, sems) = rest[: len(FACES)], rest[len(FACES) :]
    part = arrived.shape[0] // PARTS
    copies = [
        pltpu.make_async_copy(
            arrived.at[pl.ds(i * part, part)], received.at[pl.ds(i * part, part)], sems.at[i]
        )
        for i in range(PARTS)
    ]
    for copy in copies:
        copy.start()
    for copy in copies:
        copy.wait()
    low_x, low_y, _ = row_masks()
    for (axis, up), face in zip(FACES, sent):
        low, distance = (low_x, 4) if axis == "x" else (low_y, 2)

        @pl.loop(0, 12)
        def _(pair):
            block = face_block(axis, up, pair)
            sources = [owner[block + side] for side in range(2)]
            masks = [mask[block + side] for side in range(2)]
            for place, tile in enumerate(face_tiles(axis, up)):
                a, b = (
                    received[sources[side], :, lanes(tile)].astype(jnp.float32) * masks[side]
                    for side in range(2)
                )
                b = swap(b, distance)
                joined = jnp.where(low, b, a) if up else jnp.where(low, a, b)
                face[pair, :, lanes(place)] = joined.astype(jnp.bfloat16)


def faces(owner, received, mask):
    moved = 4 * math.prod(FACE)
    return pl.pallas_call(
        faces_kernel,
        out_shape=[jax.ShapeDtypeStruct(FACE, jnp.bfloat16) for _ in FACES]
        + [jax.ShapeDtypeStruct(received.shape, received.dtype)],
        in_specs=[pl.BlockSpec(memory_space=pltpu.SMEM), ANY, VMEM],
        out_specs=[VMEM] * (len(FACES) + 1),
        scratch_shapes=[pltpu.SemaphoreType.DMA((PARTS,))],
        compiler_params=pltpu.CompilerParams(vmem_limit_bytes=FACES_VMEM),
        cost_estimate=pl.CostEstimate(
            flops=8 * moved, bytes_accessed=4 * moved, transcendentals=0
        ),
        name="faces",
    )(owner, received, mask)


def speeds():
    lane = lax.broadcasted_iota(jnp.int32, (CELLS, 128), 1)
    speed_y = [
        SPACING * jnp.abs(2 * (lane // VS + 8 * odd) + 1 - VS).astype(jnp.float32)
        for odd in range(2)
    ]
    speed_z = SPACING * jnp.abs(2 * (lane % VS) + 1 - VS).astype(jnp.float32)
    return speed_y, speed_z, lane % VS >= VS // 2


def speed_x(tile):
    return SPACING * abs(2 * (tile // 2) + 1 - VS)


def advance_kernel(owner, received, mask, rate, partial, kept):
    low_x, low_y, low_z = row_masks()
    speed_y, speed_z, rising_z = speeds()
    from_below = rising_z & ~low_z
    from_above = ~rising_z & low_z
    nothing = jnp.zeros((CELLS, 128), jnp.float32)

    @pl.loop(0, BLOCKS)
    def _(block):
        source, own_mask = owner[block], mask[block]
        for tile in range(TILES):
            kept[block, :, lanes(tile)] = (
                received[source, :, lanes(tile)].astype(jnp.float32) * own_mask
            )

    kept[BLOCKS] = jnp.zeros((CELLS, TOTAL), jnp.float32)

    @pl.loop(0, BX * BY)
    def _(column):
        bx, by = column // BY, column % BY
        line = column * BZ
        outside = BLOCKS
        near_x = (
            [jnp.where(bx == BX - 1, outside, line + SLAB), jnp.where(bx == BX - 1, 0, 1)],
            [jnp.where(bx == 0, outside, line - SLAB), jnp.where(bx == 0, 0, 1)],
        )
        near_y = (
            [jnp.where(by == BY - 1, outside, line + BZ), jnp.where(by == BY - 1, 0, 1)],
            [jnp.where(by == 0, outside, line - BZ), jnp.where(by == 0, 0, 1)],
        )
        for tile in range(TILES):
            x, y = tile // (TILES // 2), tile % 2
            own_line = [kept[line + bz, :, lanes(tile)] for bz in range(BZ)]
            for bz in range(BZ):
                own = own_line[bz]
                below = own_line[bz - 1] if bz else nothing
                above = own_line[bz + 1] if bz < BZ - 1 else nothing
                start, stride = near_x[x]
                other = kept[start + stride * bz, :, lanes(tile)]
                from_x = swap(
                    jnp.where(low_x, own, other) if x else jnp.where(low_x, other, own), 4
                )
                start, stride = near_y[y]
                other = kept[start + stride * bz, :, lanes(tile)]
                from_y = swap(
                    jnp.where(low_y, own, other) if y else jnp.where(low_y, other, own), 2
                )
                from_z = swap(
                    jnp.where(from_below, below, jnp.where(from_above, above, own)), 1
                )
                flux = (
                    speed_x(tile) * (own - from_x)
                    + speed_y[y] * (own - from_y)
                    + speed_z * (own - from_z)
                )
                partial[line + bz, :, lanes(tile)] = own - rate[line + bz] * flux


def advance(owner, received, mask, rate):
    return pl.pallas_call(
        advance_kernel,
        out_shape=jax.ShapeDtypeStruct(WHOLE, jnp.float32),
        in_specs=[pl.BlockSpec(memory_space=pltpu.SMEM)] + [VMEM] * 3,
        out_specs=VMEM,
        scratch_shapes=[pltpu.VMEM((BLOCKS + 1, CELLS, TOTAL), jnp.float32)],
        compiler_params=pltpu.CompilerParams(vmem_limit_bytes=ADVANCE_VMEM),
        cost_estimate=pl.CostEstimate(
            flops=100 * math.prod(WHOLE), bytes_accessed=6 * math.prod(WHOLE), transcendentals=0
        ),
        name="advance",
    )(owner, received, mask, rate)


def edge_kernel(partial, rate, down_y, up_y, down_x, up_x, out, made, sems):
    low_x, low_y, _ = row_masks()
    speed_y, _, _ = speeds()

    def add(halo, axis, up, slots):
        low, distance = (low_x, 4) if axis == "x" else (low_y, 2)
        edge = ~low if up else low

        @pl.loop(*slots)
        def _(pair):
            block = face_block(axis, 1 - up, pair)
            for place, tile in enumerate(face_tiles(axis, up)):
                face = halo[pair, :, lanes(place)].astype(jnp.float32)
                speed = speed_x(tile) if axis == "x" else speed_y[up]
                other = swap(face, distance)
                near = (jnp.where(edge, face, 0.0), jnp.where(edge, other, 0.0))
                for side in range(2):
                    gain = rate[block + side] * (speed * swap(near[side], distance))
                    partial_at = (block + side, slice(None), lanes(tile))
                    partial[partial_at] = partial[partial_at] + gain

    def result_copy(bx):
        rows = pl.ds(bx * SLAB, SLAB)
        return pltpu.make_async_copy(made.at[rows], out.at[rows], sems.at[bx])

    for bx in range(BX):
        if bx == 0:
            add(up_x, "x", 1, (0, 12))
        if bx == BX - 1:
            add(down_x, "x", 0, (0, 12))
        add(down_y, "y", 0, (3 * bx, 3 * bx + 3))
        add(up_y, "y", 1, (3 * bx, 3 * bx + 3))

        @pl.loop(bx * SLAB, bx * SLAB + SLAB)
        def _(block):
            made[block] = partial[block].astype(jnp.bfloat16)

        result_copy(bx).start()
    for bx in range(BX):
        result_copy(bx).wait()


def edge(partial, rate, halos):
    return pl.pallas_call(
        edge_kernel,
        out_shape=jax.ShapeDtypeStruct(WHOLE, jnp.bfloat16),
        in_specs=[VMEM] * 6,
        out_specs=ANY,
        scratch_shapes=[pltpu.VMEM(WHOLE, jnp.bfloat16), pltpu.SemaphoreType.DMA((BX,))],
        compiler_params=pltpu.CompilerParams(vmem_limit_bytes=EDGE_VMEM),
        cost_estimate=pl.CostEstimate(
            flops=4 * math.prod(WHOLE), bytes_accessed=6 * math.prod(WHOLE), transcendentals=0
        ),
        name="edge",
    )(partial, rate, *halos)


def after(received, source_owner, levels, active):
    n_gx, n_gy = lax.axis_size("gx"), lax.axis_size("gy")
    mask = jnp.broadcast_to(
        active.astype(jnp.float32)[:, :, None], (BLOCKS, CELLS, 128)
    )
    courant = COURANT * jnp.exp2(levels.astype(jnp.float32))
    rate = mask * courant[:, None, None]

    def up(n):
        return [(i, i + 1) for i in range(n - 1)]

    def down(n):
        return [(i + 1, i) for i in range(n - 1)]

    *sent, received = faces(source_owner, received, mask)
    halos = []
    for (axis, to_above), face in zip(FACES, sent):
        name, n = ("gx", n_gx) if axis == "x" else ("gy", n_gy)
        halos.append(lax.ppermute(face, name, up(n) if to_above else down(n)))
    return edge(advance(source_owner, received, mask, rate), rate, halos)


def per_device(dist_old, source_owner, levels, active):
    axes = ("gx", "gy")
    devices = lax.axis_size("gx") * lax.axis_size("gy")
    owners = lax.broadcasted_iota(jnp.int32, (devices, BLOCKS), 0)
    slots = lax.broadcasted_iota(jnp.int32, (devices, BLOCKS), 1)
    request = BLOCKS + jnp.sum(
        jnp.where(source_owner[None, :] == owners, slots - BLOCKS, 0), axis=1, keepdims=True
    )
    asked = lax.all_to_all(
        jnp.broadcast_to(request, (devices, 128)), axes, split_axis=0, concat_axis=0, tiled=True
    )
    send = pack(asked, relax(dist_old))
    received = lax.all_to_all(send, axes, split_axis=0, concat_axis=0, tiled=True)
    return after(received, source_owner, levels, active)


def solution(mesh):
    return jax.shard_map(
        per_device,
        mesh=mesh,
        in_specs=(
            P(("gx", "gy"), None, None),
            P(("gx", "gy")),
            P(("gx", "gy")),
            P(("gx", "gy"), None),
        ),
        out_specs=P(("gx", "gy"), None, None),
        check_vma=False,
    )
```

```python
import math

import jax
import jax.numpy as jnp
import ml_dtypes
import numpy as np
from jax import lax
from jax.experimental import pallas as pl
from jax.experimental.pallas import tpu as pltpu
from jax.sharding import PartitionSpec as P

VS = 16
BX, BY, BZ = 4, 4, 6
BLOCKS = BX * BY * BZ
TOTAL = VS * VS * VS
CELLS = 8
SLAB = BY * BZ
RELAX_INCREMENT = 0.3
COURANT = 0.028
SPACING = 3.0 / VS
LOG2E = 1.0 / math.log(2.0)

TILES = TOTAL // 128
LATE = tuple(range(TILES // 2 + 1, TILES, 2))
CHUNKS = (tuple(t for t in range(TILES) if t not in LATE), LATE)
PIECE = 16
RELAX_VMEM = 60 << 20
PACK_VMEM = 54 << 20
FACES_VMEM = 16 << 20
ADVANCE_VMEM = 28 << 20
EDGE_VMEM = 20 << 20
GROUP = 8
STEP = 512


def runs_of(chunk):
    runs = []
    for place, tile in enumerate(CHUNKS[chunk]):
        if runs and runs[-1][1] + runs[-1][2] == tile:
            runs[-1][2] += 1
        else:
            runs.append([place, tile, 1])
    return runs


def shape_of(chunk, rows=BLOCKS):
    return (rows, CELLS, 128 * len(CHUNKS[chunk]))


def lanes(tile):
    return pl.ds(tile * 128, 128)


def basis_rows():
    index = np.arange(TOTAL)
    x, y, z = (2 * i + 1 - VS for i in (index // (VS * VS), index // VS % VS, index % VS))
    rows = np.zeros((16, TOTAL), np.float32)
    rows[:10] = [np.ones_like(x), x, y, z, x * x, y * y, z * z, x * y, x * z, y * z]
    whole = np.zeros((48, TOTAL), np.float32)
    for copy in range(3):
        whole[16 * copy : 16 * copy + 16] = rows
    return whole.astype(ml_dtypes.bfloat16)


def coefficients_of(sums):
    raw = [sums[i : i + 1] * (1.0 / TOTAL) for i in range(10)]
    density = raw[0]
    drift = [SPACING * raw[1 + a] / density for a in range(3)]
    square = SPACING * SPACING
    spread = [square * raw[4 + a] / density - drift[a] * drift[a] for a in range(3)]
    spread_xy = square * raw[7] / density - drift[0] * drift[1]
    spread_xz = square * raw[8] / density - drift[0] * drift[2]
    spread_yz = square * raw[9] / density - drift[1] * drift[2]
    temperature = (spread[0] + spread[1] + spread[2]) / 3.0
    xx, yy, zz = (1.5 * temperature - 0.5 * s for s in spread)
    xy, xz, yz = (-0.5 * s for s in (spread_xy, spread_xz, spread_yz))
    adj_xx, adj_yy, adj_zz = yy * zz - yz * yz, xx * zz - xz * xz, xx * yy - xy * xy
    adj_xy, adj_xz, adj_yz = xz * yz - xy * zz, xy * yz - xz * yy, xy * xz - xx * yz
    determinant = xx * adj_xx + xy * adj_xy + xz * adj_xz
    inv = [a / determinant for a in (adj_xx, adj_yy, adj_zz, adj_xy, adj_xz, adj_yz)]
    pull = [
        inv[0] * drift[0] + inv[3] * drift[1] + inv[4] * drift[2],
        inv[3] * drift[0] + inv[1] * drift[1] + inv[5] * drift[2],
        inv[4] * drift[0] + inv[5] * drift[1] + inv[2] * drift[2],
    ]
    quadratic = drift[0] * pull[0] + drift[1] * pull[1] + drift[2] * pull[2]
    log_prefactor = (
        jnp.log(density)
        + (3.0 * math.log(6.0) - 1.5 * math.log(2.0 * math.pi))
        - 0.5 * jnp.log(determinant)
    )
    rows = [log_prefactor - 0.5 * quadratic]
    rows += [SPACING * p for p in pull]
    rows += [-0.5 * square * i for i in inv[:3]]
    rows += [-square * i for i in inv[3:]]
    fraction = 1.0 - jnp.exp(-RELAX_INCREMENT * density * jnp.sqrt(temperature))
    return [LOG2E * r for r in rows], fraction


def relax_kernel(dist, basis, *rest):
    outs, relaxed = rest[: len(CHUNKS)], rest[len(CHUNKS) : 2 * len(CHUNKS)]
    held, sums, factors, in_sems, out_sems = rest[2 * len(CHUNKS) :]
    pieces = BLOCKS // PIECE

    def arrival(piece):
        rows = pl.ds(piece * PIECE, PIECE)
        return pltpu.make_async_copy(dist.at[rows], held.at[rows], in_sems.at[piece])

    for piece in range(pieces):
        arrival(piece).start()
    for piece in range(pieces):
        arrival(piece).wait()
        cells = held[pl.ds(piece * PIECE, PIECE)].astype(jnp.float32)
        cells = cells.reshape(PIECE * CELLS, TOTAL).astype(jnp.bfloat16)
        sums[:, pl.ds(piece * PIECE * CELLS, PIECE * CELLS)] = lax.dot_general(
            basis[0:16, :], cells, (((1,), (1,)), ((), ())), preferred_element_type=jnp.float32
        )

    rows, fraction = coefficients_of(sums[...])
    exact = [[], [], []]
    for row in rows:
        for part in range(3):
            near = row.astype(jnp.bfloat16).astype(jnp.float32)
            exact[part].append(near)
            row = row - near
    zero = jnp.zeros((6, BLOCKS * CELLS), jnp.float32)
    stacked = jnp.concatenate(
        exact[0]
        + [zero]
        + exact[1]
        + [zero]
        + exact[2]
        + [zero, fraction, jnp.zeros((79, BLOCKS * CELLS), jnp.float32)],
        axis=0,
    )
    factors[...] = stacked.T

    @pl.loop(0, BLOCKS // GROUP)
    def _(group):
        first = group * GROUP
        own = factors[pl.ds(pl.multiple_of(first * CELLS, GROUP * CELLS), GROUP * CELLS), :]
        left = own[:, :48].astype(jnp.bfloat16)
        fraction = jnp.broadcast_to(own[:, 48:49], (GROUP * CELLS, 128))
        for step in range(TOTAL // STEP):
            power = jnp.dot(
                left, basis[:, pl.ds(step * STEP, STEP)], preferred_element_type=jnp.float32
            )
            for tile in range(STEP // 128):
                whole = step * (STEP // 128) + tile
                late = int(whole in LATE)
                gauss = jnp.exp2(power[:, tile * 128 : tile * 128 + 128])
                moved = held[pl.ds(first, GROUP), :, lanes(whole)].astype(jnp.float32)
                moved = moved.reshape(GROUP * CELLS, 128)
                mixed = moved + fraction * (gauss - moved)
                relaxed[late][pl.ds(first, GROUP), :, lanes(CHUNKS[late].index(whole))] = (
                    mixed.reshape(GROUP, CELLS, 128).astype(jnp.bfloat16)
                )
        rows = pl.ds(first, GROUP)
        for made, out, sem in zip(relaxed, outs, range(len(CHUNKS))):
            pltpu.make_async_copy(made.at[rows], out.at[rows], out_sems.at[sem]).start()

    for made, out, sem in zip(relaxed, outs, range(len(CHUNKS))):
        pltpu.make_async_copy(made, out, out_sems.at[sem]).wait()


VMEM = pl.BlockSpec(memory_space=pltpu.VMEM)
ANY = pl.BlockSpec(memory_space=pl.ANY)
WHOLE = (BLOCKS, CELLS, TOTAL)


def relax(dist):
    return pl.pallas_call(
        relax_kernel,
        out_shape=[jax.ShapeDtypeStruct(shape_of(c), jnp.bfloat16) for c in range(len(CHUNKS))],
        in_specs=[ANY, VMEM],
        out_specs=[ANY] * len(CHUNKS),
        scratch_shapes=[pltpu.VMEM(shape_of(c), jnp.bfloat16) for c in range(len(CHUNKS))]
        + [
            pltpu.VMEM(WHOLE, jnp.bfloat16),
            pltpu.VMEM((16, BLOCKS * CELLS), jnp.float32),
            pltpu.VMEM((BLOCKS * CELLS, 128), jnp.float32),
            pltpu.SemaphoreType.DMA((BLOCKS // PIECE,)),
            pltpu.SemaphoreType.DMA((len(CHUNKS),)),
        ],
        compiler_params=pltpu.CompilerParams(vmem_limit_bytes=RELAX_VMEM),
        cost_estimate=pl.CostEstimate(
            flops=2 * BLOCKS * CELLS * TOTAL * 1500,
            bytes_accessed=4 * BLOCKS * CELLS * TOTAL,
            transcendentals=BLOCKS * CELLS * TOTAL,
        ),
        name="relax",
    )(dist, basis_rows())


def pack_kernel(asked, relaxed, send, held, row, target, row_sem, in_sems, out_sem):
    def arrival(piece):
        rows = pl.ds(piece * PIECE, PIECE)
        return pltpu.make_async_copy(relaxed.at[rows], held.at[rows], in_sems.at[piece])

    for piece in range(BLOCKS // PIECE):
        arrival(piece).start()
    device = lax.broadcasted_iota(jnp.int32, asked.shape, 0)
    slot = lax.broadcasted_iota(jnp.int32, asked.shape, 1)
    row[...] = jnp.broadcast_to(
        jnp.sum(jnp.where(asked[...] == slot, device, 0), axis=0, keepdims=True), row.shape
    )
    to_scalars = pltpu.make_async_copy(row, target, row_sem)
    to_scalars.start()
    to_scalars.wait()
    for piece in range(BLOCKS // PIECE):
        arrival(piece).wait()
        for block in range(piece * PIECE, piece * PIECE + PIECE):
            pltpu.make_async_copy(held.at[block], send.at[target[0, block]], out_sem).start()
    pltpu.make_async_copy(held, send.at[pl.ds(0, BLOCKS)], out_sem).wait()


def pack(chunk, asked, relaxed):
    devices = asked.shape[0]
    return pl.pallas_call(
        pack_kernel,
        out_shape=jax.ShapeDtypeStruct(shape_of(chunk, devices), jnp.bfloat16),
        in_specs=[VMEM, ANY],
        out_specs=ANY,
        scratch_shapes=[
            pltpu.VMEM(shape_of(chunk), jnp.bfloat16),
            pltpu.VMEM((8, 128), jnp.int32),
            pltpu.SMEM((8, 128), jnp.int32),
            pltpu.SemaphoreType.DMA(()),
            pltpu.SemaphoreType.DMA((BLOCKS // PIECE,)),
            pltpu.SemaphoreType.DMA(()),
        ],
        compiler_params=pltpu.CompilerParams(vmem_limit_bytes=PACK_VMEM),
        cost_estimate=pl.CostEstimate(
            flops=0, bytes_accessed=4 * math.prod(shape_of(chunk)), transcendentals=0
        ),
        name=f"pack{chunk}",
    )(asked, relaxed)


def row_masks():
    row = lax.broadcasted_iota(jnp.int32, (CELLS, 128), 0)
    return row < 4, (row & 2) == 0, (row & 1) == 0


def swap(x, distance):
    if distance == 4:
        return pltpu.roll(x, 4, 0)
    row = lax.broadcasted_iota(jnp.int32, (CELLS, 128), 0)
    return jnp.take_along_axis(x, row ^ distance, axis=0)


PARTS = 4


def face_kinds(chunk):
    kinds = (("y", 1), ("x", 1), ("y", 0), ("x", 0))
    return [kind for kind in kinds if face_tiles(chunk, *kind)]


def face_shape(chunk, kind):
    return (12, CELLS, 128 * len(face_tiles(chunk, *kind)))


def face_block(axis, up, pair):
    if axis == "x":
        return (BX - 1) * SLAB * up + 2 * pair
    return pair // 3 * SLAB + up * (BY - 1) * BZ + pair % 3 * 2


def face_tiles(chunk, axis, up):
    return [
        (place, tile)
        for place, tile in enumerate(CHUNKS[chunk])
        if up == (tile % 2 if axis == "y" else tile // (TILES // 2))
    ]


def write_faces(chunk, owner, received, mask, sent):
    low_x, low_y, _ = row_masks()
    for (axis, up), face in zip(face_kinds(chunk), sent):
        low, distance = (low_x, 4) if axis == "x" else (low_y, 2)

        @pl.loop(0, 12)
        def _(pair):
            block = face_block(axis, up, pair)
            sources = [owner[block + side] for side in range(2)]
            masks = [mask[block + side] for side in range(2)]
            for n, (place, _) in enumerate(face_tiles(chunk, axis, up)):
                a, b = (
                    received[sources[side], :, lanes(place)].astype(jnp.float32) * masks[side]
                    for side in range(2)
                )
                b = swap(b, distance)
                joined = jnp.where(low, b, a) if up else jnp.where(low, a, b)
                face[pair, :, lanes(n)] = joined.astype(jnp.bfloat16)


def faces_kernel(chunk, owner, arrived, mask, *rest):
    if chunk:
        write_faces(chunk, owner, arrived, mask, rest)
        return
    *sent, received, sems = rest
    part = arrived.shape[0] // PARTS
    copies = [
        pltpu.make_async_copy(
            arrived.at[pl.ds(i * part, part)], received.at[pl.ds(i * part, part)], sems.at[i]
        )
        for i in range(PARTS)
    ]
    for copy in copies:
        copy.start()
    for copy in copies:
        copy.wait()
    write_faces(chunk, owner, received, mask, sent)


def faces(chunk, owner, arrived, mask):
    kinds = face_kinds(chunk)
    shapes = [jax.ShapeDtypeStruct(face_shape(chunk, kind), jnp.bfloat16) for kind in kinds]
    moved = sum(math.prod(s.shape) for s in shapes)
    if chunk == 0:
        shapes.append(jax.ShapeDtypeStruct(arrived.shape, arrived.dtype))
    made = pl.pallas_call(
        lambda *refs: faces_kernel(chunk, *refs),
        out_shape=shapes,
        in_specs=[pl.BlockSpec(memory_space=pltpu.SMEM), VMEM if chunk else ANY, VMEM],
        out_specs=[VMEM] * len(shapes),
        scratch_shapes=[] if chunk else [pltpu.SemaphoreType.DMA((PARTS,))],
        compiler_params=pltpu.CompilerParams(vmem_limit_bytes=FACES_VMEM),
        cost_estimate=pl.CostEstimate(
            flops=8 * moved, bytes_accessed=4 * moved, transcendentals=0
        ),
        name=f"faces{chunk}",
    )(owner, arrived, mask)
    return made[: len(kinds)], arrived if chunk else made[-1]


def speeds():
    lane = lax.broadcasted_iota(jnp.int32, (CELLS, 128), 1)
    speed_y = [
        SPACING * jnp.abs(2 * (lane // VS + 8 * odd) + 1 - VS).astype(jnp.float32)
        for odd in range(2)
    ]
    speed_z = SPACING * jnp.abs(2 * (lane % VS) + 1 - VS).astype(jnp.float32)
    return speed_y, speed_z, lane % VS >= VS // 2


def speed_x(tile):
    return SPACING * abs(2 * (tile // 2) + 1 - VS)


def advance_kernel(chunk, owner, received, mask, rate, partial, kept):
    low_x, low_y, low_z = row_masks()
    speed_y, speed_z, rising_z = speeds()
    from_below = rising_z & ~low_z
    from_above = ~rising_z & low_z
    nothing = jnp.zeros((CELLS, 128), jnp.float32)

    @pl.loop(0, BLOCKS)
    def _(block):
        source, own_mask = owner[block], mask[block]
        for place in range(len(CHUNKS[chunk])):
            kept[block, :, lanes(place)] = (
                received[source, :, lanes(place)].astype(jnp.float32) * own_mask
            )

    kept[BLOCKS] = jnp.zeros(shape_of(chunk)[1:], jnp.float32)

    @pl.loop(0, BX * BY)
    def _(column):
        bx, by = column // BY, column % BY
        line = column * BZ
        outside = BLOCKS
        near_x = (
            [jnp.where(bx == BX - 1, outside, line + SLAB), jnp.where(bx == BX - 1, 0, 1)],
            [jnp.where(bx == 0, outside, line - SLAB), jnp.where(bx == 0, 0, 1)],
        )
        near_y = (
            [jnp.where(by == BY - 1, outside, line + BZ), jnp.where(by == BY - 1, 0, 1)],
            [jnp.where(by == 0, outside, line - BZ), jnp.where(by == 0, 0, 1)],
        )
        for place, tile in enumerate(CHUNKS[chunk]):
            x, y = tile // (TILES // 2), tile % 2
            own_line = [kept[line + bz, :, lanes(place)] for bz in range(BZ)]
            for bz in range(BZ):
                own = own_line[bz]
                below = own_line[bz - 1] if bz else nothing
                above = own_line[bz + 1] if bz < BZ - 1 else nothing
                start, stride = near_x[x]
                other = kept[start + stride * bz, :, lanes(place)]
                from_x = swap(
                    jnp.where(low_x, own, other) if x else jnp.where(low_x, other, own), 4
                )
                start, stride = near_y[y]
                other = kept[start + stride * bz, :, lanes(place)]
                from_y = swap(
                    jnp.where(low_y, own, other) if y else jnp.where(low_y, other, own), 2
                )
                from_z = swap(
                    jnp.where(from_below, below, jnp.where(from_above, above, own)), 1
                )
                flux = (
                    speed_x(tile) * (own - from_x)
                    + speed_y[y] * (own - from_y)
                    + speed_z * (own - from_z)
                )
                partial[line + bz, :, lanes(place)] = own - rate[line + bz] * flux


def advance(chunk, owner, received, mask, rate):
    shape = shape_of(chunk)
    return pl.pallas_call(
        lambda *refs: advance_kernel(chunk, *refs),
        out_shape=jax.ShapeDtypeStruct(shape, jnp.float32),
        in_specs=[pl.BlockSpec(memory_space=pltpu.SMEM)] + [VMEM] * 3,
        out_specs=VMEM,
        scratch_shapes=[pltpu.VMEM((BLOCKS + 1, *shape[1:]), jnp.float32)],
        compiler_params=pltpu.CompilerParams(vmem_limit_bytes=ADVANCE_VMEM),
        cost_estimate=pl.CostEstimate(
            flops=100 * math.prod(shape), bytes_accessed=6 * math.prod(shape), transcendentals=0
        ),
        name=f"advance{chunk}",
    )(owner, received, mask, rate)


def edge_kernel(chunk, _, rate, *rest):
    kinds = face_kinds(chunk)
    halos, (out, partial, made, sems) = rest[: len(kinds)], rest[-4:]
    low_x, low_y, _ = row_masks()
    speed_y, _, _ = speeds()

    def add(kind, halo, slots):
        axis, up = kind
        low, distance = (low_x, 4) if axis == "x" else (low_y, 2)
        edge = ~low if up else low

        @pl.loop(*slots)
        def _(pair):
            block = face_block(axis, 1 - up, pair)
            for n, (place, tile) in enumerate(face_tiles(chunk, *kind)):
                face = halo[pair, :, lanes(n)].astype(jnp.float32)
                speed = speed_x(tile) if axis == "x" else speed_y[up]
                other = swap(face, distance)
                near = (jnp.where(edge, face, 0.0), jnp.where(edge, other, 0.0))
                for side in range(2):
                    gain = rate[block + side] * (speed * swap(near[side], distance))
                    partial_at = (block + side, slice(None), lanes(place))
                    partial[partial_at] = partial[partial_at] + gain

    def result_copies(bx):
        rows = pl.ds(bx * SLAB, SLAB)
        return [
            pltpu.make_async_copy(
                made.at[rows, :, pl.ds(place * 128, length * 128)],
                out.at[rows, :, pl.ds(tile * 128, length * 128)],
                sems.at[bx, n],
            )
            for n, (place, tile, length) in enumerate(runs_of(chunk))
        ]

    for bx in range(BX):
        for kind, halo in zip(kinds, halos):
            if kind[0] == "y":
                add(kind, halo, (3 * bx, 3 * bx + 3))
            elif bx == (0 if kind[1] else BX - 1):
                add(kind, halo, (0, 12))

        @pl.loop(bx * SLAB, bx * SLAB + SLAB)
        def _(block):
            made[block] = partial[block].astype(jnp.bfloat16)

        for copy in result_copies(bx):
            copy.start()
    for bx in range(BX):
        for copy in result_copies(bx):
            copy.wait()


def edge(chunk, partial, rate, halos, earlier):
    shape = shape_of(chunk)
    extra = [] if earlier is None else [earlier]
    out, _ = pl.pallas_call(
        lambda *refs: edge_kernel(chunk, *refs),
        out_shape=[
            jax.ShapeDtypeStruct(WHOLE, jnp.bfloat16),
            jax.ShapeDtypeStruct(shape, jnp.float32),
        ],
        in_specs=[VMEM] * (2 + len(halos)) + [ANY] * len(extra),
        out_specs=[ANY, VMEM],
        scratch_shapes=[
            pltpu.VMEM(shape, jnp.bfloat16),
            pltpu.SemaphoreType.DMA((BX, len(runs_of(chunk)))),
        ],
        input_output_aliases={0: 1} | ({} if earlier is None else {2 + len(halos): 0}),
        compiler_params=pltpu.CompilerParams(vmem_limit_bytes=EDGE_VMEM),
        cost_estimate=pl.CostEstimate(
            flops=4 * math.prod(shape), bytes_accessed=6 * math.prod(shape), transcendentals=0
        ),
        name=f"edge{chunk}",
    )(partial, rate, *halos, *extra)
    return out


def after(received, source_owner, levels, active):
    n_gx, n_gy = lax.axis_size("gx"), lax.axis_size("gy")
    mask = jnp.broadcast_to(
        active.astype(jnp.float32)[:, :, None], (BLOCKS, CELLS, 128)
    )
    courant = COURANT * jnp.exp2(levels.astype(jnp.float32))
    rate = mask * courant[:, None, None]

    def up(n):
        return [(i, i + 1) for i in range(n - 1)]

    def down(n):
        return [(i + 1, i) for i in range(n - 1)]

    out = None
    for chunk, arrived in enumerate(received):
        if out is not None:
            arrived, out = lax.optimization_barrier((arrived, out))
        sent, arrived = faces(chunk, source_owner, arrived, mask)
        halos = []
        for (axis, to_above), face in zip(face_kinds(chunk), sent):
            name, n = ("gx", n_gx) if axis == "x" else ("gy", n_gy)
            halos.append(lax.ppermute(face, name, up(n) if to_above else down(n)))
        partial = advance(chunk, source_owner, arrived, mask, rate)
        out = edge(chunk, partial, rate, halos, out)
    return out


def per_device(dist_old, source_owner, levels, active):
    axes = ("gx", "gy")
    n_gx, n_gy = lax.axis_size("gx"), lax.axis_size("gy")
    devices = n_gx * n_gy
    owners = lax.broadcasted_iota(jnp.int32, (devices, BLOCKS), 0)
    slots = lax.broadcasted_iota(jnp.int32, (devices, BLOCKS), 1)
    request = BLOCKS + jnp.sum(
        jnp.where(source_owner[None, :] == owners, slots - BLOCKS, 0), axis=1, keepdims=True
    )
    asked = jnp.broadcast_to(request, (devices, 128)).reshape(n_gx, n_gy, 128)
    asked = lax.all_to_all(asked, "gx", split_axis=0, concat_axis=0, tiled=True)
    asked = lax.all_to_all(asked, "gy", split_axis=1, concat_axis=1, tiled=True)
    asked = asked.reshape(devices, 128)
    received = [
        lax.all_to_all(
            pack(chunk, asked, relaxed), axes, split_axis=0, concat_axis=0, tiled=True
        )
        for chunk, relaxed in enumerate(relax(dist_old))
    ]
    return after(received, source_owner, levels, active)


def solution(mesh):
    return jax.shard_map(
        per_device,
        mesh=mesh,
        in_specs=(
            P(("gx", "gy"), None, None),
            P(("gx", "gy")),
            P(("gx", "gy")),
            P(("gx", "gy"), None),
        ),
        out_specs=P(("gx", "gy"), None, None),
        check_vma=False,
    )
```

```python
import math

import jax
import jax.numpy as jnp
import ml_dtypes
import numpy as np
from jax import lax
from jax.experimental import pallas as pl
from jax.experimental.pallas import tpu as pltpu
from jax.sharding import PartitionSpec as P

VS = 16
BX, BY, BZ = 4, 4, 6
BLOCKS = BX * BY * BZ
TOTAL = VS * VS * VS
CELLS = 8
SLAB = BY * BZ
RELAX_INCREMENT = 0.3
COURANT = 0.028
SPACING = 3.0 / VS
LOG2E = 1.0 / math.log(2.0)

TILES = TOTAL // 128
LATE = (17, 19, 21, 23, 25, 26, 27, 28, 29, 30, 31)
CHUNKS = (tuple(t for t in range(TILES) if t not in LATE), LATE)
PIECE = 16
RELAX_VMEM = 60 << 20
PACK_VMEM = 54 << 20
FACES_VMEM = 16 << 20
ADVANCE_VMEM = 28 << 20
EDGE_VMEM = 20 << 20
GROUP = 8
STEP = 512


def runs_of(chunk):
    runs = []
    for place, tile in enumerate(CHUNKS[chunk]):
        if runs and runs[-1][1] + runs[-1][2] == tile:
            runs[-1][2] += 1
        else:
            runs.append([place, tile, 1])
    return runs


def shape_of(chunk, rows=BLOCKS):
    return (rows, CELLS, 128 * len(CHUNKS[chunk]))


def lanes(tile):
    return pl.ds(tile * 128, 128)


def basis_rows():
    index = np.arange(TOTAL)
    x, y, z = (2 * i + 1 - VS for i in (index // (VS * VS), index // VS % VS, index % VS))
    rows = np.zeros((16, TOTAL), np.float32)
    rows[:10] = [np.ones_like(x), x, y, z, x * x, y * y, z * z, x * y, x * z, y * z]
    whole = np.zeros((48, TOTAL), np.float32)
    for copy in range(3):
        whole[16 * copy : 16 * copy + 16] = rows
    return whole.astype(ml_dtypes.bfloat16)


def coefficients_of(sums):
    raw = [sums[i : i + 1] * (1.0 / TOTAL) for i in range(10)]
    density = raw[0]
    drift = [SPACING * raw[1 + a] / density for a in range(3)]
    square = SPACING * SPACING
    spread = [square * raw[4 + a] / density - drift[a] * drift[a] for a in range(3)]
    spread_xy = square * raw[7] / density - drift[0] * drift[1]
    spread_xz = square * raw[8] / density - drift[0] * drift[2]
    spread_yz = square * raw[9] / density - drift[1] * drift[2]
    temperature = (spread[0] + spread[1] + spread[2]) / 3.0
    xx, yy, zz = (1.5 * temperature - 0.5 * s for s in spread)
    xy, xz, yz = (-0.5 * s for s in (spread_xy, spread_xz, spread_yz))
    adj_xx, adj_yy, adj_zz = yy * zz - yz * yz, xx * zz - xz * xz, xx * yy - xy * xy
    adj_xy, adj_xz, adj_yz = xz * yz - xy * zz, xy * yz - xz * yy, xy * xz - xx * yz
    determinant = xx * adj_xx + xy * adj_xy + xz * adj_xz
    inv = [a / determinant for a in (adj_xx, adj_yy, adj_zz, adj_xy, adj_xz, adj_yz)]
    pull = [
        inv[0] * drift[0] + inv[3] * drift[1] + inv[4] * drift[2],
        inv[3] * drift[0] + inv[1] * drift[1] + inv[5] * drift[2],
        inv[4] * drift[0] + inv[5] * drift[1] + inv[2] * drift[2],
    ]
    quadratic = drift[0] * pull[0] + drift[1] * pull[1] + drift[2] * pull[2]
    log_prefactor = (
        jnp.log(density)
        + (3.0 * math.log(6.0) - 1.5 * math.log(2.0 * math.pi))
        - 0.5 * jnp.log(determinant)
    )
    rows = [log_prefactor - 0.5 * quadratic]
    rows += [SPACING * p for p in pull]
    rows += [-0.5 * square * i for i in inv[:3]]
    rows += [-square * i for i in inv[3:]]
    fraction = 1.0 - jnp.exp(-RELAX_INCREMENT * density * jnp.sqrt(temperature))
    return [LOG2E * r for r in rows], fraction


def relax_kernel(dist, basis, *rest):
    outs, relaxed = rest[: len(CHUNKS)], rest[len(CHUNKS) : 2 * len(CHUNKS)]
    held, sums, factors, in_sems, out_sems = rest[2 * len(CHUNKS) :]
    pieces = BLOCKS // PIECE

    def arrival(piece):
        rows = pl.ds(piece * PIECE, PIECE)
        return pltpu.make_async_copy(dist.at[rows], held.at[rows], in_sems.at[piece])

    for piece in range(pieces):
        arrival(piece).start()
    for piece in range(pieces):
        arrival(piece).wait()
        cells = held[pl.ds(piece * PIECE, PIECE)].astype(jnp.float32)
        cells = cells.reshape(PIECE * CELLS, TOTAL).astype(jnp.bfloat16)
        sums[:, pl.ds(piece * PIECE * CELLS, PIECE * CELLS)] = lax.dot_general(
            basis[0:16, :], cells, (((1,), (1,)), ((), ())), preferred_element_type=jnp.float32
        )

    rows, fraction = coefficients_of(sums[...])
    exact = [[], [], []]
    for row in rows:
        for part in range(3):
            near = row.astype(jnp.bfloat16).astype(jnp.float32)
            exact[part].append(near)
            row = row - near
    zero = jnp.zeros((6, BLOCKS * CELLS), jnp.float32)
    stacked = jnp.concatenate(
        exact[0]
        + [zero]
        + exact[1]
        + [zero]
        + exact[2]
        + [zero, fraction, jnp.zeros((79, BLOCKS * CELLS), jnp.float32)],
        axis=0,
    )
    factors[...] = stacked.T

    @pl.loop(0, BLOCKS // GROUP)
    def _(group):
        first = group * GROUP
        own = factors[pl.ds(pl.multiple_of(first * CELLS, GROUP * CELLS), GROUP * CELLS), :]
        left = own[:, :48].astype(jnp.bfloat16)
        fraction = jnp.broadcast_to(own[:, 48:49], (GROUP * CELLS, 128))
        for step in range(TOTAL // STEP):
            power = jnp.dot(
                left, basis[:, pl.ds(step * STEP, STEP)], preferred_element_type=jnp.float32
            )
            for tile in range(STEP // 128):
                whole = step * (STEP // 128) + tile
                late = int(whole in LATE)
                gauss = jnp.exp2(power[:, tile * 128 : tile * 128 + 128])
                moved = held[pl.ds(first, GROUP), :, lanes(whole)].astype(jnp.float32)
                moved = moved.reshape(GROUP * CELLS, 128)
                mixed = moved + fraction * (gauss - moved)
                relaxed[late][pl.ds(first, GROUP), :, lanes(CHUNKS[late].index(whole))] = (
                    mixed.reshape(GROUP, CELLS, 128).astype(jnp.bfloat16)
                )
        rows = pl.ds(first, GROUP)
        for made, out, sem in zip(relaxed, outs, range(len(CHUNKS))):
            pltpu.make_async_copy(made.at[rows], out.at[rows], out_sems.at[sem]).start()

    for made, out, sem in zip(relaxed, outs, range(len(CHUNKS))):
        pltpu.make_async_copy(made, out, out_sems.at[sem]).wait()


VMEM = pl.BlockSpec(memory_space=pltpu.VMEM)
ANY = pl.BlockSpec(memory_space=pl.ANY)
WHOLE = (BLOCKS, CELLS, TOTAL)


def relax(dist):
    return pl.pallas_call(
        relax_kernel,
        out_shape=[jax.ShapeDtypeStruct(shape_of(c), jnp.bfloat16) for c in range(len(CHUNKS))],
        in_specs=[ANY, VMEM],
        out_specs=[ANY] * len(CHUNKS),
        scratch_shapes=[pltpu.VMEM(shape_of(c), jnp.bfloat16) for c in range(len(CHUNKS))]
        + [
            pltpu.VMEM(WHOLE, jnp.bfloat16),
            pltpu.VMEM((16, BLOCKS * CELLS), jnp.float32),
            pltpu.VMEM((BLOCKS * CELLS, 128), jnp.float32),
            pltpu.SemaphoreType.DMA((BLOCKS // PIECE,)),
            pltpu.SemaphoreType.DMA((len(CHUNKS),)),
        ],
        compiler_params=pltpu.CompilerParams(vmem_limit_bytes=RELAX_VMEM),
        cost_estimate=pl.CostEstimate(
            flops=2 * BLOCKS * CELLS * TOTAL * 1500,
            bytes_accessed=4 * BLOCKS * CELLS * TOTAL,
            transcendentals=BLOCKS * CELLS * TOTAL,
        ),
        name="relax",
    )(dist, basis_rows())


def pack_kernel(asked, relaxed, send, held, row, target, row_sem, in_sems, out_sem):
    def arrival(piece):
        rows = pl.ds(piece * PIECE, PIECE)
        return pltpu.make_async_copy(relaxed.at[rows], held.at[rows], in_sems.at[piece])

    for piece in range(BLOCKS // PIECE):
        arrival(piece).start()
    device = lax.broadcasted_iota(jnp.int32, asked.shape, 0)
    slot = lax.broadcasted_iota(jnp.int32, asked.shape, 1)
    row[...] = jnp.broadcast_to(
        jnp.sum(jnp.where(asked[...] == slot, device, 0), axis=0, keepdims=True), row.shape
    )
    to_scalars = pltpu.make_async_copy(row, target, row_sem)
    to_scalars.start()
    to_scalars.wait()
    for piece in range(BLOCKS // PIECE):
        arrival(piece).wait()
        for block in range(piece * PIECE, piece * PIECE + PIECE):
            pltpu.make_async_copy(held.at[block], send.at[target[0, block]], out_sem).start()
    pltpu.make_async_copy(held, send.at[pl.ds(0, BLOCKS)], out_sem).wait()


def pack(chunk, asked, relaxed):
    devices = asked.shape[0]
    return pl.pallas_call(
        pack_kernel,
        out_shape=jax.ShapeDtypeStruct(shape_of(chunk, devices), jnp.bfloat16),
        in_specs=[VMEM, ANY],
        out_specs=ANY,
        scratch_shapes=[
            pltpu.VMEM(shape_of(chunk), jnp.bfloat16),
            pltpu.VMEM((8, 128), jnp.int32),
            pltpu.SMEM((8, 128), jnp.int32),
            pltpu.SemaphoreType.DMA(()),
            pltpu.SemaphoreType.DMA((BLOCKS // PIECE,)),
            pltpu.SemaphoreType.DMA(()),
        ],
        compiler_params=pltpu.CompilerParams(vmem_limit_bytes=PACK_VMEM),
        cost_estimate=pl.CostEstimate(
            flops=0, bytes_accessed=4 * math.prod(shape_of(chunk)), transcendentals=0
        ),
        name=f"pack{chunk}",
    )(asked, relaxed)


def row_masks():
    row = lax.broadcasted_iota(jnp.int32, (CELLS, 128), 0)
    return row < 4, (row & 2) == 0, (row & 1) == 0


def swap(x, distance):
    if distance == 4:
        return pltpu.roll(x, 4, 0)
    row = lax.broadcasted_iota(jnp.int32, (CELLS, 128), 0)
    return jnp.take_along_axis(x, row ^ distance, axis=0)


PARTS = 4


def face_kinds(chunk):
    kinds = (("y", 1), ("x", 1), ("y", 0), ("x", 0))
    return [kind for kind in kinds if face_tiles(chunk, *kind)]


def face_shape(chunk, kind):
    return (12, CELLS, 128 * len(face_tiles(chunk, *kind)))


def face_block(axis, up, pair):
    if axis == "x":
        return (BX - 1) * SLAB * up + 2 * pair
    return pair // 3 * SLAB + up * (BY - 1) * BZ + pair % 3 * 2


def face_tiles(chunk, axis, up):
    return [
        (place, tile)
        for place, tile in enumerate(CHUNKS[chunk])
        if up == (tile % 2 if axis == "y" else tile // (TILES // 2))
    ]


def write_faces(chunk, owner, received, mask, sent):
    low_x, low_y, _ = row_masks()
    for (axis, up), face in zip(face_kinds(chunk), sent):
        low, distance = (low_x, 4) if axis == "x" else (low_y, 2)

        @pl.loop(0, 12)
        def _(pair):
            block = face_block(axis, up, pair)
            sources = [owner[block + side] for side in range(2)]
            masks = [mask[block + side] for side in range(2)]
            for n, (place, _) in enumerate(face_tiles(chunk, axis, up)):
                a, b = (
                    received[sources[side], :, lanes(place)].astype(jnp.float32) * masks[side]
                    for side in range(2)
                )
                b = swap(b, distance)
                joined = jnp.where(low, b, a) if up else jnp.where(low, a, b)
                face[pair, :, lanes(n)] = joined.astype(jnp.bfloat16)


def faces_kernel(chunk, owner, arrived, mask, *rest):
    if chunk:
        write_faces(chunk, owner, arrived, mask, rest)
        return
    *sent, received, sems = rest
    part = arrived.shape[0] // PARTS
    copies = [
        pltpu.make_async_copy(
            arrived.at[pl.ds(i * part, part)], received.at[pl.ds(i * part, part)], sems.at[i]
        )
        for i in range(PARTS)
    ]
    for copy in copies:
        copy.start()
    for copy in copies:
        copy.wait()
    write_faces(chunk, owner, received, mask, sent)


def faces(chunk, owner, arrived, mask):
    kinds = face_kinds(chunk)
    shapes = [jax.ShapeDtypeStruct(face_shape(chunk, kind), jnp.bfloat16) for kind in kinds]
    moved = sum(math.prod(s.shape) for s in shapes)
    if chunk == 0:
        shapes.append(jax.ShapeDtypeStruct(arrived.shape, arrived.dtype))
    made = pl.pallas_call(
        lambda *refs: faces_kernel(chunk, *refs),
        out_shape=shapes,
        in_specs=[pl.BlockSpec(memory_space=pltpu.SMEM), VMEM if chunk else ANY, VMEM],
        out_specs=[VMEM] * len(shapes),
        scratch_shapes=[] if chunk else [pltpu.SemaphoreType.DMA((PARTS,))],
        compiler_params=pltpu.CompilerParams(vmem_limit_bytes=FACES_VMEM),
        cost_estimate=pl.CostEstimate(
            flops=8 * moved, bytes_accessed=4 * moved, transcendentals=0
        ),
        name=f"faces{chunk}",
    )(owner, arrived, mask)
    return made[: len(kinds)], arrived if chunk else made[-1]


def speeds():
    lane = lax.broadcasted_iota(jnp.int32, (CELLS, 128), 1)
    speed_y = [
        SPACING * jnp.abs(2 * (lane // VS + 8 * odd) + 1 - VS).astype(jnp.float32)
        for odd in range(2)
    ]
    speed_z = SPACING * jnp.abs(2 * (lane % VS) + 1 - VS).astype(jnp.float32)
    return speed_y, speed_z, lane % VS >= VS // 2


def speed_x(tile):
    return SPACING * abs(2 * (tile // 2) + 1 - VS)


def advance_kernel(chunk, owner, received, mask, rate, partial, kept):
    low_x, low_y, low_z = row_masks()
    speed_y, speed_z, rising_z = speeds()
    from_below = rising_z & ~low_z
    from_above = ~rising_z & low_z
    nothing = jnp.zeros((CELLS, 128), jnp.float32)

    @pl.loop(0, BLOCKS)
    def _(block):
        source, own_mask = owner[block], mask[block]
        for place in range(len(CHUNKS[chunk])):
            kept[block, :, lanes(place)] = (
                received[source, :, lanes(place)].astype(jnp.float32) * own_mask
            )

    kept[BLOCKS] = jnp.zeros(shape_of(chunk)[1:], jnp.float32)

    @pl.loop(0, BX * BY)
    def _(column):
        bx, by = column // BY, column % BY
        line = column * BZ
        outside = BLOCKS
        near_x = (
            [jnp.where(bx == BX - 1, outside, line + SLAB), jnp.where(bx == BX - 1, 0, 1)],
            [jnp.where(bx == 0, outside, line - SLAB), jnp.where(bx == 0, 0, 1)],
        )
        near_y = (
            [jnp.where(by == BY - 1, outside, line + BZ), jnp.where(by == BY - 1, 0, 1)],
            [jnp.where(by == 0, outside, line - BZ), jnp.where(by == 0, 0, 1)],
        )
        for place, tile in enumerate(CHUNKS[chunk]):
            x, y = tile // (TILES // 2), tile % 2
            own_line = [kept[line + bz, :, lanes(place)] for bz in range(BZ)]
            for bz in range(BZ):
                own = own_line[bz]
                below = own_line[bz - 1] if bz else nothing
                above = own_line[bz + 1] if bz < BZ - 1 else nothing
                start, stride = near_x[x]
                other = kept[start + stride * bz, :, lanes(place)]
                from_x = swap(
                    jnp.where(low_x, own, other) if x else jnp.where(low_x, other, own), 4
                )
                start, stride = near_y[y]
                other = kept[start + stride * bz, :, lanes(place)]
                from_y = swap(
                    jnp.where(low_y, own, other) if y else jnp.where(low_y, other, own), 2
                )
                from_z = swap(
                    jnp.where(from_below, below, jnp.where(from_above, above, own)), 1
                )
                flux = (
                    speed_x(tile) * (own - from_x)
                    + speed_y[y] * (own - from_y)
                    + speed_z * (own - from_z)
                )
                partial[line + bz, :, lanes(place)] = own - rate[line + bz] * flux


def advance(chunk, owner, received, mask, rate):
    shape = shape_of(chunk)
    return pl.pallas_call(
        lambda *refs: advance_kernel(chunk, *refs),
        out_shape=jax.ShapeDtypeStruct(shape, jnp.float32),
        in_specs=[pl.BlockSpec(memory_space=pltpu.SMEM)] + [VMEM] * 3,
        out_specs=VMEM,
        scratch_shapes=[pltpu.VMEM((BLOCKS + 1, *shape[1:]), jnp.float32)],
        compiler_params=pltpu.CompilerParams(vmem_limit_bytes=ADVANCE_VMEM),
        cost_estimate=pl.CostEstimate(
            flops=100 * math.prod(shape), bytes_accessed=6 * math.prod(shape), transcendentals=0
        ),
        name=f"advance{chunk}",
    )(owner, received, mask, rate)


def edge_kernel(chunk, _, rate, *rest):
    kinds = face_kinds(chunk)
    halos, (out, partial, made, sems) = rest[: len(kinds)], rest[-4:]
    low_x, low_y, _ = row_masks()
    speed_y, _, _ = speeds()

    def add(kind, halo, slots):
        axis, up = kind
        low, distance = (low_x, 4) if axis == "x" else (low_y, 2)
        edge = ~low if up else low

        @pl.loop(*slots)
        def _(pair):
            block = face_block(axis, 1 - up, pair)
            for n, (place, tile) in enumerate(face_tiles(chunk, *kind)):
                face = halo[pair, :, lanes(n)].astype(jnp.float32)
                speed = speed_x(tile) if axis == "x" else speed_y[up]
                other = swap(face, distance)
                near = (jnp.where(edge, face, 0.0), jnp.where(edge, other, 0.0))
                for side in range(2):
                    gain = rate[block + side] * (speed * swap(near[side], distance))
                    partial_at = (block + side, slice(None), lanes(place))
                    partial[partial_at] = partial[partial_at] + gain

    def result_copies(bx):
        rows = pl.ds(bx * SLAB, SLAB)
        return [
            pltpu.make_async_copy(
                made.at[rows, :, pl.ds(place * 128, length * 128)],
                out.at[rows, :, pl.ds(tile * 128, length * 128)],
                sems.at[bx, n],
            )
            for n, (place, tile, length) in enumerate(runs_of(chunk))
        ]

    for bx in range(BX):
        for kind, halo in zip(kinds, halos):
            if kind[0] == "y":
                add(kind, halo, (3 * bx, 3 * bx + 3))
            elif bx == (0 if kind[1] else BX - 1):
                add(kind, halo, (0, 12))

        @pl.loop(bx * SLAB, bx * SLAB + SLAB)
        def _(block):
            made[block] = partial[block].astype(jnp.bfloat16)

        for copy in result_copies(bx):
            copy.start()
    for bx in range(BX):
        for copy in result_copies(bx):
            copy.wait()


def edge(chunk, partial, rate, halos, earlier):
    shape = shape_of(chunk)
    extra = [] if earlier is None else [earlier]
    out, _ = pl.pallas_call(
        lambda *refs: edge_kernel(chunk, *refs),
        out_shape=[
            jax.ShapeDtypeStruct(WHOLE, jnp.bfloat16),
            jax.ShapeDtypeStruct(shape, jnp.float32),
        ],
        in_specs=[VMEM] * (2 + len(halos)) + [ANY] * len(extra),
        out_specs=[ANY, VMEM],
        scratch_shapes=[
            pltpu.VMEM(shape, jnp.bfloat16),
            pltpu.SemaphoreType.DMA((BX, len(runs_of(chunk)))),
        ],
        input_output_aliases={0: 1} | ({} if earlier is None else {2 + len(halos): 0}),
        compiler_params=pltpu.CompilerParams(vmem_limit_bytes=EDGE_VMEM),
        cost_estimate=pl.CostEstimate(
            flops=4 * math.prod(shape), bytes_accessed=6 * math.prod(shape), transcendentals=0
        ),
        name=f"edge{chunk}",
    )(partial, rate, *halos, *extra)
    return out


def after(received, source_owner, levels, active):
    n_gx, n_gy = lax.axis_size("gx"), lax.axis_size("gy")
    mask = jnp.broadcast_to(
        active.astype(jnp.float32)[:, :, None], (BLOCKS, CELLS, 128)
    )
    courant = COURANT * jnp.exp2(levels.astype(jnp.float32))
    rate = mask * courant[:, None, None]

    def up(n):
        return [(i, i + 1) for i in range(n - 1)]

    def down(n):
        return [(i + 1, i) for i in range(n - 1)]

    out = None
    for chunk, arrived in enumerate(received):
        if out is not None:
            arrived, out = lax.optimization_barrier((arrived, out))
        sent, arrived = faces(chunk, source_owner, arrived, mask)
        halos = []
        for (axis, to_above), face in zip(face_kinds(chunk), sent):
            name, n = ("gx", n_gx) if axis == "x" else ("gy", n_gy)
            halos.append(lax.ppermute(face, name, up(n) if to_above else down(n)))
        partial = advance(chunk, source_owner, arrived, mask, rate)
        out = edge(chunk, partial, rate, halos, out)
    return out


def per_device(dist_old, source_owner, levels, active):
    axes = ("gx", "gy")
    devices = lax.axis_size("gx") * lax.axis_size("gy")
    owners = lax.broadcasted_iota(jnp.int32, (devices, BLOCKS), 0)
    slots = lax.broadcasted_iota(jnp.int32, (devices, BLOCKS), 1)
    request = BLOCKS + jnp.sum(
        jnp.where(source_owner[None, :] == owners, slots - BLOCKS, 0), axis=1, keepdims=True
    )
    asked = lax.all_to_all(
        jnp.broadcast_to(request, (devices, 128)), axes, split_axis=0, concat_axis=0, tiled=True
    )
    received = [
        lax.all_to_all(
            pack(chunk, asked, relaxed), axes, split_axis=0, concat_axis=0, tiled=True
        )
        for chunk, relaxed in enumerate(relax(dist_old))
    ]
    return after(received, source_owner, levels, active)


def solution(mesh):
    return jax.shard_map(
        per_device,
        mesh=mesh,
        in_specs=(
            P(("gx", "gy"), None, None),
            P(("gx", "gy")),
            P(("gx", "gy")),
            P(("gx", "gy"), None),
        ),
        out_specs=P(("gx", "gy"), None, None),
        check_vma=False,
    )
```

```python
import math

import jax
import jax.numpy as jnp
import ml_dtypes
import numpy as np
from jax import lax
from jax.experimental import pallas as pl
from jax.experimental.pallas import tpu as pltpu
from jax.sharding import PartitionSpec as P

VS = 16
BX, BY, BZ = 4, 4, 6
BLOCKS = BX * BY * BZ
TOTAL = VS * VS * VS
CELLS = 8
SLAB = BY * BZ
RELAX_INCREMENT = 0.3
COURANT = 0.028
SPACING = 3.0 / VS
LOG2E = 1.0 / math.log(2.0)

TILES = TOTAL // 128
LATE = tuple(range(TILES // 2 + 5, TILES, 2))
CHUNKS = (tuple(t for t in range(TILES) if t not in LATE), LATE)
PIECE = 16
RELAX_VMEM = 60 << 20
PACK_VMEM = 52 << 20
FACES_VMEM = (12 << 20, 4 << 20)
ADVANCE_VMEM = (20 << 20, 8 << 20)
EDGE_VMEM = 48 << 20
GROUP = 8
STEP = 512


def shape_of(chunk, rows=BLOCKS):
    return (rows, CELLS, 128 * len(CHUNKS[chunk]))


def lanes(tile):
    return pl.ds(tile * 128, 128)


def basis_rows():
    index = np.arange(TOTAL)
    x, y, z = (2 * i + 1 - VS for i in (index // (VS * VS), index // VS % VS, index % VS))
    rows = np.zeros((16, TOTAL), np.float32)
    rows[:10] = [np.ones_like(x), x, y, z, x * x, y * y, z * z, x * y, x * z, y * z]
    whole = np.zeros((48, TOTAL), np.float32)
    for copy in range(3):
        whole[16 * copy : 16 * copy + 16] = rows
    return whole.astype(ml_dtypes.bfloat16)


def coefficients_of(sums):
    raw = [sums[i : i + 1] * (1.0 / TOTAL) for i in range(10)]
    density = raw[0]
    drift = [SPACING * raw[1 + a] / density for a in range(3)]
    square = SPACING * SPACING
    spread = [square * raw[4 + a] / density - drift[a] * drift[a] for a in range(3)]
    spread_xy = square * raw[7] / density - drift[0] * drift[1]
    spread_xz = square * raw[8] / density - drift[0] * drift[2]
    spread_yz = square * raw[9] / density - drift[1] * drift[2]
    temperature = (spread[0] + spread[1] + spread[2]) / 3.0
    xx, yy, zz = (1.5 * temperature - 0.5 * s for s in spread)
    xy, xz, yz = (-0.5 * s for s in (spread_xy, spread_xz, spread_yz))
    adj_xx, adj_yy, adj_zz = yy * zz - yz * yz, xx * zz - xz * xz, xx * yy - xy * xy
    adj_xy, adj_xz, adj_yz = xz * yz - xy * zz, xy * yz - xz * yy, xy * xz - xx * yz
    determinant = xx * adj_xx + xy * adj_xy + xz * adj_xz
    inv = [a / determinant for a in (adj_xx, adj_yy, adj_zz, adj_xy, adj_xz, adj_yz)]
    pull = [
        inv[0] * drift[0] + inv[3] * drift[1] + inv[4] * drift[2],
        inv[3] * drift[0] + inv[1] * drift[1] + inv[5] * drift[2],
        inv[4] * drift[0] + inv[5] * drift[1] + inv[2] * drift[2],
    ]
    quadratic = drift[0] * pull[0] + drift[1] * pull[1] + drift[2] * pull[2]
    log_prefactor = (
        jnp.log(density)
        + (3.0 * math.log(6.0) - 1.5 * math.log(2.0 * math.pi))
        - 0.5 * jnp.log(determinant)
    )
    rows = [log_prefactor - 0.5 * quadratic]
    rows += [SPACING * p for p in pull]
    rows += [-0.5 * square * i for i in inv[:3]]
    rows += [-square * i for i in inv[3:]]
    fraction = 1.0 - jnp.exp(-RELAX_INCREMENT * density * jnp.sqrt(temperature))
    return [LOG2E * r for r in rows], fraction


def relax_kernel(dist, basis, *rest):
    outs, relaxed = rest[: len(CHUNKS)], rest[len(CHUNKS) : 2 * len(CHUNKS)]
    held, sums, factors, in_sems, out_sems = rest[2 * len(CHUNKS) :]
    pieces = BLOCKS // PIECE

    def arrival(piece):
        rows = pl.ds(piece * PIECE, PIECE)
        return pltpu.make_async_copy(dist.at[rows], held.at[rows], in_sems.at[piece])

    for piece in range(pieces):
        arrival(piece).start()
    for piece in range(pieces):
        arrival(piece).wait()
        cells = held[pl.ds(piece * PIECE, PIECE)].astype(jnp.float32)
        cells = cells.reshape(PIECE * CELLS, TOTAL).astype(jnp.bfloat16)
        sums[:, pl.ds(piece * PIECE * CELLS, PIECE * CELLS)] = lax.dot_general(
            basis[0:16, :], cells, (((1,), (1,)), ((), ())), preferred_element_type=jnp.float32
        )

    rows, fraction = coefficients_of(sums[...])
    exact = [[], [], []]
    for row in rows:
        for part in range(3):
            near = row.astype(jnp.bfloat16).astype(jnp.float32)
            exact[part].append(near)
            row = row - near
    zero = jnp.zeros((6, BLOCKS * CELLS), jnp.float32)
    stacked = jnp.concatenate(
        exact[0]
        + [zero]
        + exact[1]
        + [zero]
        + exact[2]
        + [zero, fraction, jnp.zeros((79, BLOCKS * CELLS), jnp.float32)],
        axis=0,
    )
    factors[...] = stacked.T

    @pl.loop(0, BLOCKS // GROUP)
    def _(group):
        first = group * GROUP
        own = factors[pl.ds(pl.multiple_of(first * CELLS, GROUP * CELLS), GROUP * CELLS), :]
        left = own[:, :48].astype(jnp.bfloat16)
        fraction = jnp.broadcast_to(own[:, 48:49], (GROUP * CELLS, 128))
        for step in range(TOTAL // STEP):
            power = jnp.dot(
                left, basis[:, pl.ds(step * STEP, STEP)], preferred_element_type=jnp.float32
            )
            for tile in range(STEP // 128):
                whole = step * (STEP // 128) + tile
                late = int(whole in LATE)
                gauss = jnp.exp2(power[:, tile * 128 : tile * 128 + 128])
                moved = held[pl.ds(first, GROUP), :, lanes(whole)].astype(jnp.float32)
                moved = moved.reshape(GROUP * CELLS, 128)
                mixed = moved + fraction * (gauss - moved)
                relaxed[late][pl.ds(first, GROUP), :, lanes(CHUNKS[late].index(whole))] = (
                    mixed.reshape(GROUP, CELLS, 128).astype(jnp.bfloat16)
                )
        rows = pl.ds(first, GROUP)
        for made, out, sem in zip(relaxed, outs, range(len(CHUNKS))):
            pltpu.make_async_copy(made.at[rows], out.at[rows], out_sems.at[sem]).start()

    for made, out, sem in zip(relaxed, outs, range(len(CHUNKS))):
        pltpu.make_async_copy(made, out, out_sems.at[sem]).wait()


VMEM = pl.BlockSpec(memory_space=pltpu.VMEM)
ANY = pl.BlockSpec(memory_space=pl.ANY)
WHOLE = (BLOCKS, CELLS, TOTAL)


def relax(dist):
    return pl.pallas_call(
        relax_kernel,
        out_shape=[jax.ShapeDtypeStruct(shape_of(c), jnp.bfloat16) for c in range(len(CHUNKS))],
        in_specs=[ANY, VMEM],
        out_specs=[ANY] * len(CHUNKS),
        scratch_shapes=[pltpu.VMEM(shape_of(c), jnp.bfloat16) for c in range(len(CHUNKS))]
        + [
            pltpu.VMEM(WHOLE, jnp.bfloat16),
            pltpu.VMEM((16, BLOCKS * CELLS), jnp.float32),
            pltpu.VMEM((BLOCKS * CELLS, 128), jnp.float32),
            pltpu.SemaphoreType.DMA((BLOCKS // PIECE,)),
            pltpu.SemaphoreType.DMA((len(CHUNKS),)),
        ],
        compiler_params=pltpu.CompilerParams(vmem_limit_bytes=RELAX_VMEM),
        cost_estimate=pl.CostEstimate(
            flops=2 * BLOCKS * CELLS * TOTAL * 1500,
            bytes_accessed=4 * BLOCKS * CELLS * TOTAL,
            transcendentals=BLOCKS * CELLS * TOTAL,
        ),
        name="relax",
    )(dist, basis_rows())


def pack_kernel(asked, relaxed, send, held, row, target, row_sem, in_sems, out_sem):
    def arrival(piece):
        rows = pl.ds(piece * PIECE, PIECE)
        return pltpu.make_async_copy(relaxed.at[rows], held.at[rows], in_sems.at[piece])

    for piece in range(BLOCKS // PIECE):
        arrival(piece).start()
    device = lax.broadcasted_iota(jnp.int32, asked.shape, 0)
    slot = lax.broadcasted_iota(jnp.int32, asked.shape, 1)
    row[...] = jnp.broadcast_to(
        jnp.sum(jnp.where(asked[...] == slot, device, 0), axis=0, keepdims=True), row.shape
    )
    to_scalars = pltpu.make_async_copy(row, target, row_sem)
    to_scalars.start()
    to_scalars.wait()
    for piece in range(BLOCKS // PIECE):
        arrival(piece).wait()
        for block in range(piece * PIECE, piece * PIECE + PIECE):
            pltpu.make_async_copy(held.at[block], send.at[target[0, block]], out_sem).start()
    pltpu.make_async_copy(held, send.at[pl.ds(0, BLOCKS)], out_sem).wait()


def pack(chunk, asked, relaxed):
    devices = asked.shape[0]
    return pl.pallas_call(
        pack_kernel,
        out_shape=jax.ShapeDtypeStruct(shape_of(chunk, devices), jnp.bfloat16),
        in_specs=[VMEM, ANY],
        out_specs=ANY,
        scratch_shapes=[
            pltpu.VMEM(shape_of(chunk), jnp.bfloat16),
            pltpu.VMEM((8, 128), jnp.int32),
            pltpu.SMEM((8, 128), jnp.int32),
            pltpu.SemaphoreType.DMA(()),
            pltpu.SemaphoreType.DMA((BLOCKS // PIECE,)),
            pltpu.SemaphoreType.DMA(()),
        ],
        compiler_params=pltpu.CompilerParams(vmem_limit_bytes=PACK_VMEM),
        cost_estimate=pl.CostEstimate(
            flops=0, bytes_accessed=4 * math.prod(shape_of(chunk)), transcendentals=0
        ),
        name=f"pack{chunk}",
    )(asked, relaxed)


def row_masks():
    row = lax.broadcasted_iota(jnp.int32, (CELLS, 128), 0)
    return row < 4, (row & 2) == 0, (row & 1) == 0


def swap(x, distance):
    if distance == 4:
        return pltpu.roll(x, 4, 0)
    row = lax.broadcasted_iota(jnp.int32, (CELLS, 128), 0)
    return jnp.take_along_axis(x, row ^ distance, axis=0)


PARTS = 4


KINDS = (("y", 0), ("x", 0), ("y", 1), ("x", 1))
FACE = (12, CELLS, TOTAL // 2)


def kinds_of(chunk):
    return [kind for kind in KINDS if face_tiles(chunk, *kind)]


def face_block(axis, up, pair):
    if axis == "x":
        return (BX - 1) * SLAB * up + 2 * pair
    return pair // 3 * SLAB + up * (BY - 1) * BZ + pair % 3 * 2


def face_tiles(chunk, axis, up):
    whole = [
        t for t in range(TILES) if up == (t % 2 if axis == "y" else t // (TILES // 2))
    ]
    return [(n, CHUNKS[chunk].index(t), t) for n, t in enumerate(whole) if t in CHUNKS[chunk]]


def write_faces(chunk, owner, received, mask, sent):
    low_x, low_y, _ = row_masks()
    for (axis, up), face in zip(kinds_of(chunk), sent):
        low, distance = (low_x, 4) if axis == "x" else (low_y, 2)

        @pl.loop(0, 12)
        def _(pair):
            block = face_block(axis, up, pair)
            sources = [owner[block + side] for side in range(2)]
            masks = [mask[block + side] for side in range(2)]
            for n, place, _ in face_tiles(chunk, axis, up):
                a, b = (
                    received[sources[side], :, lanes(place)].astype(jnp.float32) * masks[side]
                    for side in range(2)
                )
                b = swap(b, distance)
                joined = jnp.where(low, b, a) if up else jnp.where(low, a, b)
                face[pair, :, lanes(n)] = joined.astype(jnp.bfloat16)


def faces_kernel(chunk, owner, arrived, mask, *rest):
    if chunk:
        kinds = kinds_of(chunk)
        sent = rest[-len(kinds) :]
        for kind, before, face in zip(kinds, rest, sent):
            for n, _, _ in face_tiles(0, *kind):
                face[:, :, lanes(n)] = before[:, :, lanes(n)]
        write_faces(chunk, owner, arrived, mask, sent)
        return
    *sent, received, sems = rest
    part = arrived.shape[0] // PARTS
    copies = [
        pltpu.make_async_copy(
            arrived.at[pl.ds(i * part, part)], received.at[pl.ds(i * part, part)], sems.at[i]
        )
        for i in range(PARTS)
    ]
    for copy in copies:
        copy.start()
    for copy in copies:
        copy.wait()
    write_faces(chunk, owner, received, mask, sent)


def faces(chunk, owner, arrived, mask, earlier, after_this):
    extra = after_this
    n = len(kinds_of(chunk))
    shapes = [jax.ShapeDtypeStruct(FACE, jnp.bfloat16)] * n
    moved = n * math.prod(FACE) * len(CHUNKS[chunk]) // TILES
    if chunk == 0:
        shapes.append(jax.ShapeDtypeStruct(arrived.shape, arrived.dtype))
    made = pl.pallas_call(
        lambda *refs: faces_kernel(chunk, *refs),
        out_shape=shapes,
        in_specs=[pl.BlockSpec(memory_space=pltpu.SMEM), VMEM if chunk else ANY]
        + [VMEM] * (1 + len(earlier))
        + [ANY] * len(extra),
        out_specs=[VMEM] * len(shapes),
        scratch_shapes=[] if chunk else [pltpu.SemaphoreType.DMA((PARTS,))],
        compiler_params=pltpu.CompilerParams(vmem_limit_bytes=FACES_VMEM[chunk]),
        cost_estimate=pl.CostEstimate(
            flops=8 * moved, bytes_accessed=4 * moved, transcendentals=0
        ),
        name=f"faces{chunk}",
    )(owner, arrived, mask, *earlier, *extra)
    return made[:n], arrived if chunk else made[-1]


def speeds():
    lane = lax.broadcasted_iota(jnp.int32, (CELLS, 128), 1)
    speed_y = [
        SPACING * jnp.abs(2 * (lane // VS + 8 * odd) + 1 - VS).astype(jnp.float32)
        for odd in range(2)
    ]
    speed_z = SPACING * jnp.abs(2 * (lane % VS) + 1 - VS).astype(jnp.float32)
    return speed_y, speed_z, lane % VS >= VS // 2


def speed_x(tile):
    return SPACING * abs(2 * (tile // 2) + 1 - VS)


def advance_kernel(chunk, owner, received, mask, rate, partial, done, kept):
    done[...] = jnp.zeros_like(done)
    low_x, low_y, low_z = row_masks()
    speed_y, speed_z, rising_z = speeds()
    from_below = rising_z & ~low_z
    from_above = ~rising_z & low_z
    nothing = jnp.zeros((CELLS, 128), jnp.float32)

    @pl.loop(0, BLOCKS)
    def _(block):
        source, own_mask = owner[block], mask[block]
        for place in range(len(CHUNKS[chunk])):
            kept[block, :, lanes(place)] = (
                received[source, :, lanes(place)].astype(jnp.float32) * own_mask
            )

    kept[BLOCKS] = jnp.zeros(shape_of(chunk)[1:], jnp.float32)

    @pl.loop(0, BX * BY)
    def _(column):
        bx, by = column // BY, column % BY
        line = column * BZ
        outside = BLOCKS
        near_x = (
            [jnp.where(bx == BX - 1, outside, line + SLAB), jnp.where(bx == BX - 1, 0, 1)],
            [jnp.where(bx == 0, outside, line - SLAB), jnp.where(bx == 0, 0, 1)],
        )
        near_y = (
            [jnp.where(by == BY - 1, outside, line + BZ), jnp.where(by == BY - 1, 0, 1)],
            [jnp.where(by == 0, outside, line - BZ), jnp.where(by == 0, 0, 1)],
        )
        for place, tile in enumerate(CHUNKS[chunk]):
            x, y = tile // (TILES // 2), tile % 2
            own_line = [kept[line + bz, :, lanes(place)] for bz in range(BZ)]
            for bz in range(BZ):
                own = own_line[bz]
                below = own_line[bz - 1] if bz else nothing
                above = own_line[bz + 1] if bz < BZ - 1 else nothing
                start, stride = near_x[x]
                other = kept[start + stride * bz, :, lanes(place)]
                from_x = swap(
                    jnp.where(low_x, own, other) if x else jnp.where(low_x, other, own), 4
                )
                start, stride = near_y[y]
                other = kept[start + stride * bz, :, lanes(place)]
                from_y = swap(
                    jnp.where(low_y, own, other) if y else jnp.where(low_y, other, own), 2
                )
                from_z = swap(
                    jnp.where(from_below, below, jnp.where(from_above, above, own)), 1
                )
                flux = (
                    speed_x(tile) * (own - from_x)
                    + speed_y[y] * (own - from_y)
                    + speed_z * (own - from_z)
                )
                partial[line + bz, :, lanes(place)] = own - rate[line + bz] * flux


def advance(chunk, owner, received, mask, rate):
    shape = shape_of(chunk)
    return pl.pallas_call(
        lambda *refs: advance_kernel(chunk, *refs),
        out_shape=[
            jax.ShapeDtypeStruct(shape, jnp.float32),
            jax.ShapeDtypeStruct((8, 128), jnp.float32),
        ],
        in_specs=[pl.BlockSpec(memory_space=pltpu.SMEM)] + [VMEM] * 3,
        out_specs=[VMEM] * 2,
        scratch_shapes=[pltpu.VMEM((BLOCKS + 1, *shape[1:]), jnp.float32)],
        compiler_params=pltpu.CompilerParams(vmem_limit_bytes=ADVANCE_VMEM[chunk]),
        cost_estimate=pl.CostEstimate(
            flops=(100, 1)[chunk] * math.prod(shape),
            bytes_accessed=(6, 1)[chunk] * math.prod(shape),
            transcendentals=0,
        ),
        name=f"advance{chunk}",
    )(owner, received, mask, rate)


def edge_kernel(rate, *rest):
    n = len(CHUNKS)
    sources, halos, out, partials = rest[:n], rest[n : n + 4], rest[n + 4], rest[n + 5 : 2 * n + 5]
    made, in_sems, sems = rest[2 * n + 5 :]

    def arrivals(bx):
        rows = pl.ds(bx * SLAB, SLAB)
        return [
            pltpu.make_async_copy(source.at[rows], partial.at[rows], in_sems.at[bx, c])
            for c, (source, partial) in enumerate(zip(sources, partials))
        ]

    for bx in range(BX):
        for copy in arrivals(bx):
            copy.start()
    low_x, low_y, _ = row_masks()
    speed_y, _, _ = speeds()

    def add(kind, halo, slots):
        axis, up = kind
        low, distance = (low_x, 4) if axis == "x" else (low_y, 2)
        edge = ~low if up else low

        @pl.loop(*slots)
        def _(pair):
            block = face_block(axis, 1 - up, pair)
            for chunk, n, place, tile in [
                (c, *found) for c in range(len(CHUNKS)) for found in face_tiles(c, *kind)
            ]:
                partial = partials[chunk]
                face = halo[pair, :, lanes(n)].astype(jnp.float32)
                speed = speed_x(tile) if axis == "x" else speed_y[up]
                other = swap(face, distance)
                near = (jnp.where(edge, face, 0.0), jnp.where(edge, other, 0.0))
                for side in range(2):
                    gain = rate[block + side] * (speed * swap(near[side], distance))
                    partial_at = (block + side, slice(None), lanes(place))
                    partial[partial_at] = partial[partial_at] + gain

    def result_copy(bx):
        rows = pl.ds(bx * SLAB, SLAB)
        return pltpu.make_async_copy(made.at[rows], out.at[rows], sems.at[bx])

    for bx in range(BX):
        for copy in arrivals(bx):
            copy.wait()
        for kind, halo in zip(KINDS, halos):
            if kind[0] == "y":
                add(kind, halo, (3 * bx, 3 * bx + 3))
            elif bx == (0 if kind[1] else BX - 1):
                add(kind, halo, (0, 12))

        @pl.loop(bx * SLAB, bx * SLAB + SLAB)
        def _(block):
            for chunk, partial in enumerate(partials):
                for place, tile in enumerate(CHUNKS[chunk]):
                    made[block, :, lanes(tile)] = partial[block, :, lanes(place)].astype(
                        jnp.bfloat16
                    )

        result_copy(bx).start()
    for bx in range(BX):
        result_copy(bx).wait()


def edge(rate, partials, halos):
    return pl.pallas_call(
        edge_kernel,
        out_shape=jax.ShapeDtypeStruct(WHOLE, jnp.bfloat16),
        in_specs=[VMEM] + [ANY] * len(partials) + [VMEM] * len(halos),
        out_specs=ANY,
        scratch_shapes=[pltpu.VMEM(p.shape, p.dtype) for p in partials]
        + [
            pltpu.VMEM(WHOLE, jnp.bfloat16),
            pltpu.SemaphoreType.DMA((BX, len(partials))),
            pltpu.SemaphoreType.DMA((BX,)),
        ],
        compiler_params=pltpu.CompilerParams(vmem_limit_bytes=EDGE_VMEM),
        cost_estimate=pl.CostEstimate(
            flops=4 * math.prod(WHOLE), bytes_accessed=6 * math.prod(WHOLE), transcendentals=0
        ),
        name="edge",
    )(rate, *partials, *halos)


def after(received, source_owner, levels, active):
    n_gx, n_gy = lax.axis_size("gx"), lax.axis_size("gy")
    mask = jnp.broadcast_to(
        active.astype(jnp.float32)[:, :, None], (BLOCKS, CELLS, 128)
    )
    courant = COURANT * jnp.exp2(levels.astype(jnp.float32))
    rate = mask * courant[:, None, None]

    def up(n):
        return [(i, i + 1) for i in range(n - 1)]

    def down(n):
        return [(i + 1, i) for i in range(n - 1)]

    def exchange(kind):
        axis, to_above = kind
        name, n = ("gx", n_gx) if axis == "x" else ("gy", n_gy)
        return lax.ppermute(sent[kind], name, up(n) if to_above else down(n))

    partials, sent, halos, done = [], {}, {}, []
    for chunk, arrived in enumerate(received):
        kinds = kinds_of(chunk)
        earlier = [sent[kind] for kind in kinds if kind in sent]
        made, arrived = faces(chunk, source_owner, arrived, mask, earlier, done)
        sent.update(zip(kinds, made))
        for kind in kinds:
            if not any(kind in kinds_of(later) for later in range(chunk + 1, len(CHUNKS))):
                halos[kind] = exchange(kind)
        partial, token = advance(chunk, source_owner, arrived, mask, rate)
        partials.append(partial)
        done = [token, *halos.values()]
    return edge(rate, partials, [halos[kind] for kind in KINDS])


def per_device(dist_old, source_owner, levels, active):
    axes = ("gx", "gy")
    devices = lax.axis_size("gx") * lax.axis_size("gy")
    owners = lax.broadcasted_iota(jnp.int32, (devices, BLOCKS), 0)
    slots = lax.broadcasted_iota(jnp.int32, (devices, BLOCKS), 1)
    request = BLOCKS + jnp.sum(
        jnp.where(source_owner[None, :] == owners, slots - BLOCKS, 0), axis=1, keepdims=True
    )
    asked = lax.all_to_all(
        jnp.broadcast_to(request, (devices, 128)), axes, split_axis=0, concat_axis=0, tiled=True
    )
    received = [
        lax.all_to_all(
            pack(chunk, asked, relaxed), axes, split_axis=0, concat_axis=0, tiled=True
        )
        for chunk, relaxed in enumerate(relax(dist_old))
    ]
    return after(received, source_owner, levels, active)


def solution(mesh):
    return jax.shard_map(
        per_device,
        mesh=mesh,
        in_specs=(
            P(("gx", "gy"), None, None),
            P(("gx", "gy")),
            P(("gx", "gy")),
            P(("gx", "gy"), None),
        ),
        out_specs=P(("gx", "gy"), None, None),
        check_vma=False,
    )
```

```python
import math

import jax
import jax.numpy as jnp
import ml_dtypes
import numpy as np
from jax import lax
from jax.experimental import pallas as pl
from jax.experimental.pallas import tpu as pltpu
from jax.sharding import PartitionSpec as P

VS = 16
BX, BY, BZ = 4, 4, 6
BLOCKS = BX * BY * BZ
TOTAL = VS * VS * VS
CELLS = 8
SLAB = BY * BZ
RELAX_INCREMENT = 0.3
COURANT = 0.028
SPACING = 3.0 / VS
LOG2E = 1.0 / math.log(2.0)

TILES = TOTAL // 128
PIECE = 16
RELAX_VMEM = 56 << 20
PACK_VMEM = 49 << 20
FACES_VMEM = 16 << 20
ADVANCE_VMEM = 28 << 20
EDGE_VMEM = 20 << 20
GROUP = 16
STEP = 512


def lanes(tile):
    return pl.ds(tile * 128, 128)


def basis_rows():
    index = np.arange(TOTAL)
    x, y, z = (2 * i + 1 - VS for i in (index // (VS * VS), index // VS % VS, index % VS))
    rows = np.zeros((16, TOTAL), np.float32)
    rows[:10] = [np.ones_like(x), x, y, z, x * x, y * y, z * z, x * y, x * z, y * z]
    whole = np.zeros((48, TOTAL), np.float32)
    for copy in range(3):
        whole[16 * copy : 16 * copy + 16] = rows
    return whole.astype(ml_dtypes.bfloat16)


def coefficients_of(sums):
    raw = [sums[i : i + 1] * (1.0 / TOTAL) for i in range(10)]
    density = raw[0]
    drift = [SPACING * raw[1 + a] / density for a in range(3)]
    square = SPACING * SPACING
    spread = [square * raw[4 + a] / density - drift[a] * drift[a] for a in range(3)]
    spread_xy = square * raw[7] / density - drift[0] * drift[1]
    spread_xz = square * raw[8] / density - drift[0] * drift[2]
    spread_yz = square * raw[9] / density - drift[1] * drift[2]
    temperature = (spread[0] + spread[1] + spread[2]) / 3.0
    xx, yy, zz = (1.5 * temperature - 0.5 * s for s in spread)
    xy, xz, yz = (-0.5 * s for s in (spread_xy, spread_xz, spread_yz))
    adj_xx, adj_yy, adj_zz = yy * zz - yz * yz, xx * zz - xz * xz, xx * yy - xy * xy
    adj_xy, adj_xz, adj_yz = xz * yz - xy * zz, xy * yz - xz * yy, xy * xz - xx * yz
    determinant = xx * adj_xx + xy * adj_xy + xz * adj_xz
    inv = [a / determinant for a in (adj_xx, adj_yy, adj_zz, adj_xy, adj_xz, adj_yz)]
    pull = [
        inv[0] * drift[0] + inv[3] * drift[1] + inv[4] * drift[2],
        inv[3] * drift[0] + inv[1] * drift[1] + inv[5] * drift[2],
        inv[4] * drift[0] + inv[5] * drift[1] + inv[2] * drift[2],
    ]
    quadratic = drift[0] * pull[0] + drift[1] * pull[1] + drift[2] * pull[2]
    log_prefactor = (
        jnp.log(density)
        + (3.0 * math.log(6.0) - 1.5 * math.log(2.0 * math.pi))
        - 0.5 * jnp.log(determinant)
    )
    rows = [log_prefactor - 0.5 * quadratic]
    rows += [SPACING * p for p in pull]
    rows += [-0.5 * square * i for i in inv[:3]]
    rows += [-square * i for i in inv[3:]]
    fraction = 1.0 - jnp.exp(-RELAX_INCREMENT * density * jnp.sqrt(temperature))
    return [LOG2E * r for r in rows], fraction


def moments_kernel(dist, basis, factors, held, sums, in_sems):
    pieces = BLOCKS // PIECE

    def arrival(piece):
        rows = pl.ds(piece * PIECE, PIECE)
        return pltpu.make_async_copy(dist.at[rows], held.at[rows], in_sems.at[piece])

    for piece in range(pieces):
        arrival(piece).start()
    for piece in range(pieces):
        arrival(piece).wait()
        cells = held[pl.ds(piece * PIECE, PIECE)].astype(jnp.float32)
        cells = cells.reshape(PIECE * CELLS, TOTAL).astype(jnp.bfloat16)
        sums[:, pl.ds(piece * PIECE * CELLS, PIECE * CELLS)] = lax.dot_general(
            basis[0:16, :], cells, (((1,), (1,)), ((), ())), preferred_element_type=jnp.float32
        )

    rows, fraction = coefficients_of(sums[...])
    exact = [[], [], []]
    for row in rows:
        for part in range(3):
            near = row.astype(jnp.bfloat16).astype(jnp.float32)
            exact[part].append(near)
            row = row - near
    zero = jnp.zeros((6, BLOCKS * CELLS), jnp.float32)
    stacked = jnp.concatenate(
        exact[0]
        + [zero]
        + exact[1]
        + [zero]
        + exact[2]
        + [zero, fraction, jnp.zeros((79, BLOCKS * CELLS), jnp.float32)],
        axis=0,
    )
    factors[...] = stacked.T


VMEM = pl.BlockSpec(memory_space=pltpu.VMEM)
ANY = pl.BlockSpec(memory_space=pl.ANY)
WHOLE = (BLOCKS, CELLS, TOTAL)


def moments(dist, basis):
    return pl.pallas_call(
        moments_kernel,
        out_shape=jax.ShapeDtypeStruct((BLOCKS * CELLS, 128), jnp.float32),
        in_specs=[ANY, VMEM],
        out_specs=VMEM,
        scratch_shapes=[
            pltpu.VMEM(WHOLE, jnp.bfloat16),
            pltpu.VMEM((16, BLOCKS * CELLS), jnp.float32),
            pltpu.SemaphoreType.DMA((BLOCKS // PIECE,)),
        ],
        compiler_params=pltpu.CompilerParams(vmem_limit_bytes=RELAX_VMEM),
        cost_estimate=pl.CostEstimate(
            flops=2 * BLOCKS * CELLS * TOTAL * 1500,
            bytes_accessed=2 * BLOCKS * CELLS * TOTAL,
            transcendentals=0,
        ),
        name="moments",
    )(dist, basis)


def relax_kernel(
    asked, dist, basis, factors, send, held, relaxed, row, target, row_sem, in_sems, out_sem
):
    def arrival(group):
        rows = pl.ds(group * GROUP, GROUP)
        return pltpu.make_async_copy(dist.at[rows], held.at[rows], in_sems.at[group])

    for group in range(BLOCKS // GROUP):
        arrival(group).start()
    device = lax.broadcasted_iota(jnp.int32, asked.shape, 0)
    slot = lax.broadcasted_iota(jnp.int32, asked.shape, 1)
    row[...] = jnp.broadcast_to(
        jnp.sum(jnp.where(asked[...] == slot, device, 0), axis=0, keepdims=True), row.shape
    )
    to_scalars = pltpu.make_async_copy(row, target, row_sem)
    to_scalars.start()
    to_scalars.wait()

    @pl.loop(0, BLOCKS // GROUP)
    def _(group):
        first = group * GROUP
        arrival(group).wait()
        own = factors[pl.ds(pl.multiple_of(first * CELLS, GROUP * CELLS), GROUP * CELLS), :]
        left = own[:, :48].astype(jnp.bfloat16)
        fraction = jnp.broadcast_to(own[:, 48:49], (GROUP * CELLS, 128))
        for step in range(TOTAL // STEP):
            power = jnp.dot(
                left, basis[:, pl.ds(step * STEP, STEP)], preferred_element_type=jnp.float32
            )
            for tile in range(STEP // 128):
                place = lanes(step * (STEP // 128) + tile)
                gauss = jnp.exp2(power[:, tile * 128 : tile * 128 + 128])
                moved = held[pl.ds(first, GROUP), :, place].astype(jnp.float32)
                moved = moved.reshape(GROUP * CELLS, 128)
                mixed = moved + fraction * (gauss - moved)
                relaxed[pl.ds(first, GROUP), :, place] = mixed.reshape(
                    GROUP, CELLS, 128
                ).astype(jnp.bfloat16)
        for block in range(GROUP):
            pltpu.make_async_copy(
                relaxed.at[first + block], send.at[target[0, first + block]], out_sem
            ).start()

    pltpu.make_async_copy(relaxed, send.at[pl.ds(0, BLOCKS)], out_sem).wait()


def relax(asked, dist, basis, factors):
    devices = asked.shape[0]
    return pl.pallas_call(
        relax_kernel,
        out_shape=jax.ShapeDtypeStruct((devices, CELLS, TOTAL), jnp.bfloat16),
        in_specs=[VMEM, ANY, VMEM, VMEM],
        out_specs=ANY,
        scratch_shapes=[
            pltpu.VMEM(WHOLE, jnp.bfloat16),
            pltpu.VMEM(WHOLE, jnp.bfloat16),
            pltpu.VMEM((8, 128), jnp.int32),
            pltpu.SMEM((8, 128), jnp.int32),
            pltpu.SemaphoreType.DMA(()),
            pltpu.SemaphoreType.DMA((BLOCKS // GROUP,)),
            pltpu.SemaphoreType.DMA(()),
        ],
        compiler_params=pltpu.CompilerParams(vmem_limit_bytes=PACK_VMEM),
        cost_estimate=pl.CostEstimate(
            flops=2 * BLOCKS * CELLS * TOTAL * 64,
            bytes_accessed=4 * BLOCKS * CELLS * TOTAL,
            transcendentals=BLOCKS * CELLS * TOTAL,
        ),
        name="relax",
    )(asked, dist, basis, factors)


def row_masks():
    row = lax.broadcasted_iota(jnp.int32, (CELLS, 128), 0)
    return row < 4, (row & 2) == 0, (row & 1) == 0


def swap(x, distance):
    if distance == 4:
        return pltpu.roll(x, 4, 0)
    row = lax.broadcasted_iota(jnp.int32, (CELLS, 128), 0)
    return jnp.take_along_axis(x, row ^ distance, axis=0)


PARTS = 4
FACES = (("y", 0), ("y", 1), ("x", 0), ("x", 1))
FACE = (12, CELLS, TOTAL // 2)


def face_block(axis, up, pair):
    if axis == "x":
        return (BX - 1) * SLAB * up + 2 * pair
    return pair // 3 * SLAB + up * (BY - 1) * BZ + pair % 3 * 2


def face_tiles(axis, up):
    return [t for t in range(TILES) if up == (t % 2 if axis == "y" else t // (TILES // 2))]


def faces_kernel(owner, arrived, mask, *rest):
    sent, (received, sems) = rest[: len(FACES)], rest[len(FACES) :]
    part = arrived.shape[0] // PARTS
    copies = [
        pltpu.make_async_copy(
            arrived.at[pl.ds(i * part, part)], received.at[pl.ds(i * part, part)], sems.at[i]
        )
        for i in range(PARTS)
    ]
    for copy in copies:
        copy.start()
    for copy in copies:
        copy.wait()
    low_x, low_y, _ = row_masks()
    for (axis, up), face in zip(FACES, sent):
        low, distance = (low_x, 4) if axis == "x" else (low_y, 2)

        @pl.loop(0, 12)
        def _(pair):
            block = face_block(axis, up, pair)
            sources = [owner[block + side] for side in range(2)]
            masks = [mask[block + side] for side in range(2)]
            for place, tile in enumerate(face_tiles(axis, up)):
                a, b = (
                    received[sources[side], :, lanes(tile)].astype(jnp.float32) * masks[side]
                    for side in range(2)
                )
                b = swap(b, distance)
                joined = jnp.where(low, b, a) if up else jnp.where(low, a, b)
                face[pair, :, lanes(place)] = joined.astype(jnp.bfloat16)


def faces(owner, received, mask):
    moved = 4 * math.prod(FACE)
    return pl.pallas_call(
        faces_kernel,
        out_shape=[jax.ShapeDtypeStruct(FACE, jnp.bfloat16) for _ in FACES]
        + [jax.ShapeDtypeStruct(received.shape, received.dtype)],
        in_specs=[pl.BlockSpec(memory_space=pltpu.SMEM), ANY, VMEM],
        out_specs=[VMEM] * (len(FACES) + 1),
        scratch_shapes=[pltpu.SemaphoreType.DMA((PARTS,))],
        compiler_params=pltpu.CompilerParams(vmem_limit_bytes=FACES_VMEM),
        cost_estimate=pl.CostEstimate(
            flops=8 * moved, bytes_accessed=4 * moved, transcendentals=0
        ),
        name="faces",
    )(owner, received, mask)


def speeds():
    lane = lax.broadcasted_iota(jnp.int32, (CELLS, 128), 1)
    speed_y = [
        SPACING * jnp.abs(2 * (lane // VS + 8 * odd) + 1 - VS).astype(jnp.float32)
        for odd in range(2)
    ]
    speed_z = SPACING * jnp.abs(2 * (lane % VS) + 1 - VS).astype(jnp.float32)
    return speed_y, speed_z, lane % VS >= VS // 2


def speed_x(tile):
    return SPACING * abs(2 * (tile // 2) + 1 - VS)


def advance_kernel(owner, received, mask, rate, partial, kept):
    low_x, low_y, low_z = row_masks()
    speed_y, speed_z, rising_z = speeds()
    speed_yz = [speed + speed_z for speed in speed_y]
    from_below = rising_z & ~low_z
    from_above = ~rising_z & low_z
    nothing = jnp.zeros((CELLS, 128), jnp.float32)

    @pl.loop(0, BLOCKS)
    def _(block):
        source, own_mask = owner[block], mask[block]
        for tile in range(TILES):
            kept[block, :, lanes(tile)] = (
                received[source, :, lanes(tile)].astype(jnp.float32) * own_mask
            )

    for bz in range(BZ):
        kept[BLOCKS + bz] = jnp.zeros((CELLS, TOTAL), jnp.float32)

    @pl.loop(0, BX * BY)
    def _(column):
        bx, by = column // BY, column % BY
        line = column * BZ
        outside = BLOCKS
        near_x = (
            jnp.where(bx == BX - 1, outside, line + SLAB),
            jnp.where(bx == 0, outside, line - SLAB),
        )
        near_y = (
            jnp.where(by == BY - 1, outside, line + BZ),
            jnp.where(by == 0, outside, line - BZ),
        )
        rates = [rate[line + bz] for bz in range(BZ)]
        for tile in range(TILES):
            x, y = tile // (TILES // 2), tile % 2
            own_line = [kept[line + bz, :, lanes(tile)] for bz in range(BZ)]
            total = speed_x(tile) + speed_yz[y]
            for bz in range(BZ):
                own = own_line[bz]
                below = own_line[bz - 1] if bz else nothing
                above = own_line[bz + 1] if bz < BZ - 1 else nothing
                other = kept[near_x[x] + bz, :, lanes(tile)]
                from_x = swap(
                    jnp.where(low_x, own, other) if x else jnp.where(low_x, other, own), 4
                )
                other = kept[near_y[y] + bz, :, lanes(tile)]
                from_y = swap(
                    jnp.where(low_y, own, other) if y else jnp.where(low_y, other, own), 2
                )
                from_z = swap(
                    jnp.where(from_below, below, jnp.where(from_above, above, own)), 1
                )
                gain = speed_x(tile) * from_x + speed_y[y] * from_y + speed_z * from_z
                partial[line + bz, :, lanes(tile)] = own + rates[bz] * (gain - total * own)


def advance(owner, received, mask, rate):
    return pl.pallas_call(
        advance_kernel,
        out_shape=jax.ShapeDtypeStruct(WHOLE, jnp.float32),
        in_specs=[pl.BlockSpec(memory_space=pltpu.SMEM)] + [VMEM] * 3,
        out_specs=VMEM,
        scratch_shapes=[pltpu.VMEM((BLOCKS + BZ, CELLS, TOTAL), jnp.float32)],
        compiler_params=pltpu.CompilerParams(vmem_limit_bytes=ADVANCE_VMEM),
        cost_estimate=pl.CostEstimate(
            flops=100 * math.prod(WHOLE), bytes_accessed=6 * math.prod(WHOLE), transcendentals=0
        ),
        name="advance",
    )(owner, received, mask, rate)


def edge_kernel(partial, rate, down_y, up_y, down_x, up_x, out, made, sems):
    low_x, low_y, _ = row_masks()
    speed_y, _, _ = speeds()

    def add(halo, axis, up, slots):
        low, distance = (low_x, 4) if axis == "x" else (low_y, 2)
        edge = ~low if up else low

        @pl.loop(*slots)
        def _(pair):
            block = face_block(axis, 1 - up, pair)
            for place, tile in enumerate(face_tiles(axis, up)):
                face = halo[pair, :, lanes(place)].astype(jnp.float32)
                speed = speed_x(tile) if axis == "x" else speed_y[up]
                other = swap(face, distance)
                near = (jnp.where(edge, face, 0.0), jnp.where(edge, other, 0.0))
                for side in range(2):
                    gain = rate[block + side] * (speed * swap(near[side], distance))
                    partial_at = (block + side, slice(None), lanes(tile))
                    partial[partial_at] = partial[partial_at] + gain

    def result_copy(bx):
        rows = pl.ds(bx * SLAB, SLAB)
        return pltpu.make_async_copy(made.at[rows], out.at[rows], sems.at[bx])

    for bx in range(BX):
        if bx == 0:
            add(up_x, "x", 1, (0, 12))
        if bx == BX - 1:
            add(down_x, "x", 0, (0, 12))
        add(down_y, "y", 0, (3 * bx, 3 * bx + 3))
        add(up_y, "y", 1, (3 * bx, 3 * bx + 3))

        @pl.loop(bx * SLAB, bx * SLAB + SLAB)
        def _(block):
            made[block] = partial[block].astype(jnp.bfloat16)

        result_copy(bx).start()
    for bx in range(BX):
        result_copy(bx).wait()


def edge(partial, rate, halos):
    return pl.pallas_call(
        edge_kernel,
        out_shape=jax.ShapeDtypeStruct(WHOLE, jnp.bfloat16),
        in_specs=[VMEM] * 6,
        out_specs=ANY,
        scratch_shapes=[pltpu.VMEM(WHOLE, jnp.bfloat16), pltpu.SemaphoreType.DMA((BX,))],
        compiler_params=pltpu.CompilerParams(vmem_limit_bytes=EDGE_VMEM),
        cost_estimate=pl.CostEstimate(
            flops=4 * math.prod(WHOLE), bytes_accessed=6 * math.prod(WHOLE), transcendentals=0
        ),
        name="edge",
    )(partial, rate, *halos)


def after(received, source_owner, levels, active):
    n_gx, n_gy = lax.axis_size("gx"), lax.axis_size("gy")
    mask = jnp.broadcast_to(
        active.astype(jnp.float32)[:, :, None], (BLOCKS, CELLS, 128)
    )
    courant = COURANT * jnp.exp2(levels.astype(jnp.float32))
    rate = mask * courant[:, None, None]

    def up(n):
        return [(i, i + 1) for i in range(n - 1)]

    def down(n):
        return [(i + 1, i) for i in range(n - 1)]

    *sent, received = faces(source_owner, received, mask)
    halos = []
    for (axis, to_above), face in zip(FACES, sent):
        name, n = ("gx", n_gx) if axis == "x" else ("gy", n_gy)
        halos.append(lax.ppermute(face, name, up(n) if to_above else down(n)))
    return edge(advance(source_owner, received, mask, rate), rate, halos)


def per_device(dist_old, source_owner, levels, active):
    axes = ("gx", "gy")
    devices = lax.axis_size("gx") * lax.axis_size("gy")
    owners = lax.broadcasted_iota(jnp.int32, (devices, BLOCKS), 0)
    slots = lax.broadcasted_iota(jnp.int32, (devices, BLOCKS), 1)
    request = BLOCKS + jnp.sum(
        jnp.where(source_owner[None, :] == owners, slots - BLOCKS, 0), axis=1, keepdims=True
    )
    asked = lax.all_to_all(
        jnp.broadcast_to(request, (devices, 128)), axes, split_axis=0, concat_axis=0, tiled=True
    )
    basis = jnp.asarray(basis_rows())
    send = relax(asked, dist_old, basis, moments(dist_old, basis))
    received = lax.all_to_all(send, axes, split_axis=0, concat_axis=0, tiled=True)
    return after(received, source_owner, levels, active)


def solution(mesh):
    return jax.shard_map(
        per_device,
        mesh=mesh,
        in_specs=(
            P(("gx", "gy"), None, None),
            P(("gx", "gy")),
            P(("gx", "gy")),
            P(("gx", "gy"), None),
        ),
        out_specs=P(("gx", "gy"), None, None),
        check_vma=False,
    )
```

```python
import math

import jax
import jax.numpy as jnp
import ml_dtypes
import numpy as np
from jax import lax
from jax.experimental import pallas as pl
from jax.experimental.pallas import tpu as pltpu
from jax.sharding import PartitionSpec as P

VS = 16
BX, BY, BZ = 4, 4, 6
BLOCKS = BX * BY * BZ
TOTAL = VS * VS * VS
CELLS = 8
SLAB = BY * BZ
RELAX_INCREMENT = 0.3
COURANT = 0.028
SPACING = 3.0 / VS
LOG2E = 1.0 / math.log(2.0)

TILES = TOTAL // 128
PIECE = 16
RELAX_VMEM = 50 << 20
PACK_VMEM = 49 << 20
FACES_VMEM = 16 << 20
ADVANCE_VMEM = 28 << 20
EDGE_VMEM = 20 << 20
GROUP = 16
STEP = 512


def lanes(tile):
    return pl.ds(tile * 128, 128)


def basis_rows():
    index = np.arange(TOTAL)
    x, y, z = (2 * i + 1 - VS for i in (index // (VS * VS), index // VS % VS, index % VS))
    rows = np.zeros((16, TOTAL), np.float32)
    rows[:10] = [np.ones_like(x), x, y, z, x * x, y * y, z * z, x * y, x * z, y * z]
    whole = np.zeros((48, TOTAL), np.float32)
    for copy in range(3):
        whole[16 * copy : 16 * copy + 16] = rows
    return whole.astype(ml_dtypes.bfloat16)


def coefficients_of(sums):
    raw = [sums[i : i + 1] * (1.0 / TOTAL) for i in range(10)]
    density = raw[0]
    drift = [SPACING * raw[1 + a] / density for a in range(3)]
    square = SPACING * SPACING
    spread = [square * raw[4 + a] / density - drift[a] * drift[a] for a in range(3)]
    spread_xy = square * raw[7] / density - drift[0] * drift[1]
    spread_xz = square * raw[8] / density - drift[0] * drift[2]
    spread_yz = square * raw[9] / density - drift[1] * drift[2]
    temperature = (spread[0] + spread[1] + spread[2]) / 3.0
    xx, yy, zz = (1.5 * temperature - 0.5 * s for s in spread)
    xy, xz, yz = (-0.5 * s for s in (spread_xy, spread_xz, spread_yz))
    adj_xx, adj_yy, adj_zz = yy * zz - yz * yz, xx * zz - xz * xz, xx * yy - xy * xy
    adj_xy, adj_xz, adj_yz = xz * yz - xy * zz, xy * yz - xz * yy, xy * xz - xx * yz
    determinant = xx * adj_xx + xy * adj_xy + xz * adj_xz
    inv = [a / determinant for a in (adj_xx, adj_yy, adj_zz, adj_xy, adj_xz, adj_yz)]
    pull = [
        inv[0] * drift[0] + inv[3] * drift[1] + inv[4] * drift[2],
        inv[3] * drift[0] + inv[1] * drift[1] + inv[5] * drift[2],
        inv[4] * drift[0] + inv[5] * drift[1] + inv[2] * drift[2],
    ]
    quadratic = drift[0] * pull[0] + drift[1] * pull[1] + drift[2] * pull[2]
    log_prefactor = (
        jnp.log(density)
        + (3.0 * math.log(6.0) - 1.5 * math.log(2.0 * math.pi))
        - 0.5 * jnp.log(determinant)
    )
    rows = [log_prefactor - 0.5 * quadratic]
    rows += [SPACING * p for p in pull]
    rows += [-0.5 * square * i for i in inv[:3]]
    rows += [-square * i for i in inv[3:]]
    fraction = 1.0 - jnp.exp(-RELAX_INCREMENT * density * jnp.sqrt(temperature))
    return [LOG2E * r for r in rows], fraction


def moments_kernel(dist, basis, factors, held, sums, in_sems):
    pieces = BLOCKS // PIECE

    def arrival(piece):
        rows = pl.ds(piece * PIECE, PIECE)
        return pltpu.make_async_copy(dist.at[rows], held.at[rows], in_sems.at[piece])

    for piece in range(pieces):
        arrival(piece).start()
    for piece in range(pieces):
        arrival(piece).wait()
        cells = held[pl.ds(piece * PIECE, PIECE)].astype(jnp.float32)
        cells = cells.reshape(PIECE * CELLS, TOTAL).astype(jnp.bfloat16)
        sums[:, pl.ds(piece * PIECE * CELLS, PIECE * CELLS)] = lax.dot_general(
            basis[0:16, :], cells, (((1,), (1,)), ((), ())), preferred_element_type=jnp.float32
        )

    rows, fraction = coefficients_of(sums[...])
    exact = [[], [], []]
    for row in rows:
        for part in range(3):
            near = row.astype(jnp.bfloat16).astype(jnp.float32)
            exact[part].append(near)
            row = row - near
    zero = jnp.zeros((6, BLOCKS * CELLS), jnp.float32)
    stacked = jnp.concatenate(
        exact[0]
        + [zero]
        + exact[1]
        + [zero]
        + exact[2]
        + [zero, fraction, jnp.zeros((79, BLOCKS * CELLS), jnp.float32)],
        axis=0,
    )
    factors[...] = stacked.T


VMEM = pl.BlockSpec(memory_space=pltpu.VMEM)
ANY = pl.BlockSpec(memory_space=pl.ANY)
WHOLE = (BLOCKS, CELLS, TOTAL)


def moments(dist, basis):
    return pl.pallas_call(
        moments_kernel,
        out_shape=jax.ShapeDtypeStruct((BLOCKS * CELLS, 128), jnp.float32),
        in_specs=[ANY, VMEM],
        out_specs=VMEM,
        scratch_shapes=[
            pltpu.VMEM(WHOLE, jnp.bfloat16),
            pltpu.VMEM((16, BLOCKS * CELLS), jnp.float32),
            pltpu.SemaphoreType.DMA((BLOCKS // PIECE,)),
        ],
        compiler_params=pltpu.CompilerParams(vmem_limit_bytes=RELAX_VMEM),
        cost_estimate=pl.CostEstimate(
            flops=2 * BLOCKS * CELLS * TOTAL * 1500,
            bytes_accessed=2 * BLOCKS * CELLS * TOTAL,
            transcendentals=0,
        ),
        name="moments",
    )(dist, basis)


def relax_kernel(
    asked, dist, basis, factors, send, held, relaxed, row, target, row_sem, in_sems, out_sem
):
    def arrival(group):
        rows = pl.ds(group * GROUP, GROUP)
        return pltpu.make_async_copy(dist.at[rows], held.at[rows], in_sems.at[group])

    for group in range(BLOCKS // GROUP):
        arrival(group).start()
    device = lax.broadcasted_iota(jnp.int32, asked.shape, 0)
    slot = lax.broadcasted_iota(jnp.int32, asked.shape, 1)
    row[...] = jnp.broadcast_to(
        jnp.sum(jnp.where(asked[...] == slot, device, 0), axis=0, keepdims=True), row.shape
    )
    to_scalars = pltpu.make_async_copy(row, target, row_sem)
    to_scalars.start()
    to_scalars.wait()

    @pl.loop(0, BLOCKS // GROUP)
    def _(group):
        first = group * GROUP
        arrival(group).wait()
        own = factors[pl.ds(pl.multiple_of(first * CELLS, GROUP * CELLS), GROUP * CELLS), :]
        left = own[:, :48].astype(jnp.bfloat16)
        fraction = jnp.broadcast_to(own[:, 48:49], (GROUP * CELLS, 128))
        for step in range(TOTAL // STEP):
            power = jnp.dot(
                left, basis[:, pl.ds(step * STEP, STEP)], preferred_element_type=jnp.float32
            )
            for tile in range(STEP // 128):
                place = lanes(step * (STEP // 128) + tile)
                gauss = jnp.exp2(power[:, tile * 128 : tile * 128 + 128])
                moved = held[pl.ds(first, GROUP), :, place].astype(jnp.float32)
                moved = moved.reshape(GROUP * CELLS, 128)
                mixed = moved + fraction * (gauss - moved)
                relaxed[pl.ds(first, GROUP), :, place] = mixed.reshape(
                    GROUP, CELLS, 128
                ).astype(jnp.bfloat16)
        for block in range(GROUP):
            pltpu.make_async_copy(
                relaxed.at[first + block], send.at[target[0, first + block]], out_sem
            ).start()

    pltpu.make_async_copy(relaxed, send.at[pl.ds(0, BLOCKS)], out_sem).wait()


def relax(asked, dist, basis, factors):
    devices = asked.shape[0]
    return pl.pallas_call(
        relax_kernel,
        out_shape=jax.ShapeDtypeStruct((devices, CELLS, TOTAL), jnp.bfloat16),
        in_specs=[VMEM, ANY, VMEM, VMEM],
        out_specs=ANY,
        scratch_shapes=[
            pltpu.VMEM(WHOLE, jnp.bfloat16),
            pltpu.VMEM(WHOLE, jnp.bfloat16),
            pltpu.VMEM((8, 128), jnp.int32),
            pltpu.SMEM((8, 128), jnp.int32),
            pltpu.SemaphoreType.DMA(()),
            pltpu.SemaphoreType.DMA((BLOCKS // GROUP,)),
            pltpu.SemaphoreType.DMA(()),
        ],
        compiler_params=pltpu.CompilerParams(vmem_limit_bytes=PACK_VMEM),
        cost_estimate=pl.CostEstimate(
            flops=2 * BLOCKS * CELLS * TOTAL * 64,
            bytes_accessed=4 * BLOCKS * CELLS * TOTAL,
            transcendentals=BLOCKS * CELLS * TOTAL,
        ),
        name="relax",
    )(asked, dist, basis, factors)


def row_masks():
    row = lax.broadcasted_iota(jnp.int32, (CELLS, 128), 0)
    return row < 4, (row & 2) == 0, (row & 1) == 0


def swap(x, distance):
    if distance == 4:
        return pltpu.roll(x, 4, 0)
    row = lax.broadcasted_iota(jnp.int32, (CELLS, 128), 0)
    return jnp.take_along_axis(x, row ^ distance, axis=0)


FACES = (("y", 0), ("y", 1), ("x", 0), ("x", 1))
FACE = (12, CELLS, TOTAL // 2)


def face_block(axis, up, pair):
    if axis == "x":
        return (BX - 1) * SLAB * up + 2 * pair
    return pair // 3 * SLAB + up * (BY - 1) * BZ + pair % 3 * 2


def face_tiles(axis, up):
    return [t for t in range(TILES) if up == (t % 2 if axis == "y" else t // (TILES // 2))]


GROUPS = (
    [(bx, 0) for bx in range(BX)],
    [(bx, BY - 1) for bx in range(BX)],
    [(0, by) for by in range(1, BY - 1)],
    [(BX - 1, by) for by in range(1, BY - 1)],
    [(bx, by) for bx in range(1, BX - 1) for by in range(1, BY - 1)],
)
PLACES = {column: BZ * n for n, column in enumerate(c for group in GROUPS for c in group)}


def faces_kernel(owner, arrived, mask, *rest):
    sent, (received, sems) = rest[: len(FACES)], rest[len(FACES) :]
    low_x, low_y, _ = row_masks()

    def fetch(group):
        for bx, by in GROUPS[group]:
            for bz in range(BZ):
                pltpu.make_async_copy(
                    arrived.at[owner[(bx * BY + by) * BZ + bz]],
                    received.at[PLACES[bx, by] + bz],
                    sems.at[group],
                ).start()

    def arrive(group):
        count = BZ * len(GROUPS[group])
        pltpu.make_async_copy(
            arrived.at[pl.ds(0, count)],
            received.at[pl.ds(PLACES[GROUPS[group][0]], count)],
            sems.at[group],
        ).wait()

    def write(axis, up):
        face = sent[FACES.index((axis, up))]
        low, distance = (low_x, 4) if axis == "x" else (low_y, 2)

        @pl.loop(0, 12)
        def _(pair):
            block = face_block(axis, up, pair)
            edge = (BX - 1) * up
            places = [PLACES[(edge, n) if axis == "x" else (n, edge)] for n in range(4)]
            line = pair // 3
            place = pair % 3 * 2 + jnp.where(
                line < 2,
                jnp.where(line == 0, places[0], places[1]),
                jnp.where(line == 2, places[2], places[3]),
            )
            masks = [mask[block + side] for side in range(2)]
            for n, tile in enumerate(face_tiles(axis, up)):
                a, b = (
                    received[place + side, :, lanes(tile)].astype(jnp.float32) * masks[side]
                    for side in range(2)
                )
                b = swap(b, distance)
                joined = jnp.where(low, b, a) if up else jnp.where(low, a, b)
                face[pair, :, lanes(n)] = joined.astype(jnp.bfloat16)

    fetch(0)
    fetch(1)
    fetch(2)
    arrive(0)
    write("y", 0)
    fetch(3)
    fetch(4)
    arrive(1)
    write("y", 1)
    arrive(2)
    write("x", 0)
    arrive(3)
    write("x", 1)
    arrive(4)


def faces(owner, received, mask):
    moved = 4 * math.prod(FACE)
    return pl.pallas_call(
        faces_kernel,
        out_shape=[jax.ShapeDtypeStruct(FACE, jnp.bfloat16) for _ in FACES]
        + [jax.ShapeDtypeStruct(WHOLE, received.dtype)],
        in_specs=[pl.BlockSpec(memory_space=pltpu.SMEM), ANY, VMEM],
        out_specs=[VMEM] * (len(FACES) + 1),
        scratch_shapes=[pltpu.SemaphoreType.DMA((len(GROUPS),))],
        compiler_params=pltpu.CompilerParams(vmem_limit_bytes=FACES_VMEM),
        cost_estimate=pl.CostEstimate(
            flops=8 * moved, bytes_accessed=4 * moved, transcendentals=0
        ),
        name="faces",
    )(owner, received, mask)


def speeds():
    lane = lax.broadcasted_iota(jnp.int32, (CELLS, 128), 1)
    speed_y = [
        SPACING * jnp.abs(2 * (lane // VS + 8 * odd) + 1 - VS).astype(jnp.float32)
        for odd in range(2)
    ]
    speed_z = SPACING * jnp.abs(2 * (lane % VS) + 1 - VS).astype(jnp.float32)
    return speed_y, speed_z, lane % VS >= VS // 2


def speed_x(tile):
    return SPACING * abs(2 * (tile // 2) + 1 - VS)


def advance_kernel(received, mask, rate, partial, kept):
    low_x, low_y, low_z = row_masks()
    speed_y, speed_z, rising_z = speeds()
    speed_yz = [speed + speed_z for speed in speed_y]
    from_below = rising_z & ~low_z
    from_above = ~rising_z & low_z
    nothing = jnp.zeros((CELLS, 128), jnp.float32)

    for (bx, by), place in PLACES.items():

        @pl.loop(0, BZ)
        def _(bz):
            block = (bx * BY + by) * BZ + bz
            own_mask = mask[block]
            for tile in range(TILES):
                kept[block, :, lanes(tile)] = (
                    received[place + bz, :, lanes(tile)].astype(jnp.float32) * own_mask
                )

    for bz in range(BZ):
        kept[BLOCKS + bz] = jnp.zeros((CELLS, TOTAL), jnp.float32)

    @pl.loop(0, BX * BY)
    def _(column):
        bx, by = column // BY, column % BY
        line = column * BZ
        outside = BLOCKS
        near_x = (
            jnp.where(bx == BX - 1, outside, line + SLAB),
            jnp.where(bx == 0, outside, line - SLAB),
        )
        near_y = (
            jnp.where(by == BY - 1, outside, line + BZ),
            jnp.where(by == 0, outside, line - BZ),
        )
        rates = [rate[line + bz] for bz in range(BZ)]
        for tile in range(TILES):
            x, y = tile // (TILES // 2), tile % 2
            own_line = [kept[line + bz, :, lanes(tile)] for bz in range(BZ)]
            total = speed_x(tile) + speed_yz[y]
            for bz in range(BZ):
                own = own_line[bz]
                below = own_line[bz - 1] if bz else nothing
                above = own_line[bz + 1] if bz < BZ - 1 else nothing
                other = kept[near_x[x] + bz, :, lanes(tile)]
                from_x = swap(
                    jnp.where(low_x, own, other) if x else jnp.where(low_x, other, own), 4
                )
                other = kept[near_y[y] + bz, :, lanes(tile)]
                from_y = swap(
                    jnp.where(low_y, own, other) if y else jnp.where(low_y, other, own), 2
                )
                from_z = swap(
                    jnp.where(from_below, below, jnp.where(from_above, above, own)), 1
                )
                gain = speed_x(tile) * from_x + speed_y[y] * from_y + speed_z * from_z
                partial[line + bz, :, lanes(tile)] = own + rates[bz] * (gain - total * own)


def advance(received, mask, rate):
    return pl.pallas_call(
        advance_kernel,
        out_shape=jax.ShapeDtypeStruct(WHOLE, jnp.float32),
        in_specs=[VMEM] * 3,
        out_specs=VMEM,
        scratch_shapes=[pltpu.VMEM((BLOCKS + BZ, CELLS, TOTAL), jnp.float32)],
        compiler_params=pltpu.CompilerParams(vmem_limit_bytes=ADVANCE_VMEM),
        cost_estimate=pl.CostEstimate(
            flops=100 * math.prod(WHOLE), bytes_accessed=6 * math.prod(WHOLE), transcendentals=0
        ),
        name="advance",
    )(received, mask, rate)


def edge_kernel(partial, rate, down_y, up_y, down_x, up_x, out, made, sems):
    low_x, low_y, _ = row_masks()
    speed_y, _, _ = speeds()

    def add(halo, axis, up, slots):
        low, distance = (low_x, 4) if axis == "x" else (low_y, 2)
        edge = ~low if up else low

        @pl.loop(*slots)
        def _(pair):
            block = face_block(axis, 1 - up, pair)
            for place, tile in enumerate(face_tiles(axis, up)):
                face = halo[pair, :, lanes(place)].astype(jnp.float32)
                speed = speed_x(tile) if axis == "x" else speed_y[up]
                other = swap(face, distance)
                near = (jnp.where(edge, face, 0.0), jnp.where(edge, other, 0.0))
                for side in range(2):
                    gain = rate[block + side] * (speed * swap(near[side], distance))
                    partial_at = (block + side, slice(None), lanes(tile))
                    partial[partial_at] = partial[partial_at] + gain

    def result_copy(bx):
        rows = pl.ds(bx * SLAB, SLAB)
        return pltpu.make_async_copy(made.at[rows], out.at[rows], sems.at[bx])

    for bx in range(BX):
        if bx == 0:
            add(up_x, "x", 1, (0, 12))
        if bx == BX - 1:
            add(down_x, "x", 0, (0, 12))
        add(down_y, "y", 0, (3 * bx, 3 * bx + 3))
        add(up_y, "y", 1, (3 * bx, 3 * bx + 3))

        @pl.loop(bx * SLAB, bx * SLAB + SLAB)
        def _(block):
            made[block] = partial[block].astype(jnp.bfloat16)

        result_copy(bx).start()
    for bx in range(BX):
        result_copy(bx).wait()


def edge(partial, rate, halos):
    return pl.pallas_call(
        edge_kernel,
        out_shape=jax.ShapeDtypeStruct(WHOLE, jnp.bfloat16),
        in_specs=[VMEM] * 6,
        out_specs=ANY,
        scratch_shapes=[pltpu.VMEM(WHOLE, jnp.bfloat16), pltpu.SemaphoreType.DMA((BX,))],
        compiler_params=pltpu.CompilerParams(vmem_limit_bytes=EDGE_VMEM),
        cost_estimate=pl.CostEstimate(
            flops=4 * math.prod(WHOLE), bytes_accessed=6 * math.prod(WHOLE), transcendentals=0
        ),
        name="edge",
    )(partial, rate, *halos)


def after(received, source_owner, levels, active):
    n_gx, n_gy = lax.axis_size("gx"), lax.axis_size("gy")
    mask = jnp.broadcast_to(
        active.astype(jnp.float32)[:, :, None], (BLOCKS, CELLS, 128)
    )
    courant = COURANT * jnp.exp2(levels.astype(jnp.float32))
    rate = mask * courant[:, None, None]

    def up(n):
        return [(i, i + 1) for i in range(n - 1)]

    def down(n):
        return [(i + 1, i) for i in range(n - 1)]

    *sent, received = faces(source_owner, received, mask)
    halos = []
    for (axis, to_above), face in zip(FACES, sent):
        name, n = ("gx", n_gx) if axis == "x" else ("gy", n_gy)
        halos.append(lax.ppermute(face, name, up(n) if to_above else down(n)))
    return edge(advance(received, mask, rate), rate, halos)


def per_device(dist_old, source_owner, levels, active):
    axes = ("gx", "gy")
    devices = lax.axis_size("gx") * lax.axis_size("gy")
    owners = lax.broadcasted_iota(jnp.int32, (devices, BLOCKS), 0)
    slots = lax.broadcasted_iota(jnp.int32, (devices, BLOCKS), 1)
    request = BLOCKS + jnp.sum(
        jnp.where(source_owner[None, :] == owners, slots - BLOCKS, 0), axis=1, keepdims=True
    )
    asked = lax.all_to_all(
        jnp.broadcast_to(request, (devices, 128)), axes, split_axis=0, concat_axis=0, tiled=True
    )
    basis = jnp.asarray(basis_rows())
    send = relax(asked, dist_old, basis, moments(dist_old, basis))
    received = lax.all_to_all(send, axes, split_axis=0, concat_axis=0, tiled=True)
    return after(received, source_owner, levels, active)


def solution(mesh):
    return jax.shard_map(
        per_device,
        mesh=mesh,
        in_specs=(
            P(("gx", "gy"), None, None),
            P(("gx", "gy")),
            P(("gx", "gy")),
            P(("gx", "gy"), None),
        ),
        out_specs=P(("gx", "gy"), None, None),
        check_vma=False,
    )
```

```python
import math

import jax
import jax.numpy as jnp
import ml_dtypes
import numpy as np
from jax import lax
from jax.experimental import pallas as pl
from jax.experimental.pallas import tpu as pltpu
from jax.sharding import PartitionSpec as P

VS = 16
BX, BY, BZ = 4, 4, 6
BLOCKS = BX * BY * BZ
TOTAL = VS * VS * VS
CELLS = 8
SLAB = BY * BZ
RELAX_INCREMENT = 0.3
COURANT = 0.028
SPACING = 3.0 / VS
LOG2E = 1.0 / math.log(2.0)

TILES = TOTAL // 128
PIECE = 16
RELAX_VMEM = 53 << 20
PACK_VMEM = 49 << 20
FACES_VMEM = 16 << 20
ADVANCE_VMEM = 8 << 20
EDGE_VMEM = 20 << 20
GROUP = 16
STEP = 512


def lanes(tile):
    return pl.ds(tile * 128, 128)


def basis_rows():
    index = np.arange(TOTAL)
    x, y, z = (2 * i + 1 - VS for i in (index // (VS * VS), index // VS % VS, index % VS))
    rows = np.zeros((16, TOTAL), np.float32)
    rows[:10] = [np.ones_like(x), x, y, z, x * x, y * y, z * z, x * y, x * z, y * z]
    whole = np.zeros((48, TOTAL), np.float32)
    for copy in range(3):
        whole[16 * copy : 16 * copy + 16] = rows
    return whole.astype(ml_dtypes.bfloat16)


def coefficients_of(sums):
    raw = [sums[i : i + 1] * (1.0 / TOTAL) for i in range(10)]
    density = raw[0]
    drift = [SPACING * raw[1 + a] / density for a in range(3)]
    square = SPACING * SPACING
    spread = [square * raw[4 + a] / density - drift[a] * drift[a] for a in range(3)]
    spread_xy = square * raw[7] / density - drift[0] * drift[1]
    spread_xz = square * raw[8] / density - drift[0] * drift[2]
    spread_yz = square * raw[9] / density - drift[1] * drift[2]
    temperature = (spread[0] + spread[1] + spread[2]) / 3.0
    xx, yy, zz = (1.5 * temperature - 0.5 * s for s in spread)
    xy, xz, yz = (-0.5 * s for s in (spread_xy, spread_xz, spread_yz))
    adj_xx, adj_yy, adj_zz = yy * zz - yz * yz, xx * zz - xz * xz, xx * yy - xy * xy
    adj_xy, adj_xz, adj_yz = xz * yz - xy * zz, xy * yz - xz * yy, xy * xz - xx * yz
    determinant = xx * adj_xx + xy * adj_xy + xz * adj_xz
    inv = [a / determinant for a in (adj_xx, adj_yy, adj_zz, adj_xy, adj_xz, adj_yz)]
    pull = [
        inv[0] * drift[0] + inv[3] * drift[1] + inv[4] * drift[2],
        inv[3] * drift[0] + inv[1] * drift[1] + inv[5] * drift[2],
        inv[4] * drift[0] + inv[5] * drift[1] + inv[2] * drift[2],
    ]
    quadratic = drift[0] * pull[0] + drift[1] * pull[1] + drift[2] * pull[2]
    log_prefactor = (
        jnp.log(density)
        + (3.0 * math.log(6.0) - 1.5 * math.log(2.0 * math.pi))
        - 0.5 * jnp.log(determinant)
    )
    rows = [log_prefactor - 0.5 * quadratic]
    rows += [SPACING * p for p in pull]
    rows += [-0.5 * square * i for i in inv[:3]]
    rows += [-square * i for i in inv[3:]]
    fraction = 1.0 - jnp.exp(-RELAX_INCREMENT * density * jnp.sqrt(temperature))
    return [LOG2E * r for r in rows], fraction


def moments_kernel(dist, basis_rows, factors, held, basis, sums, in_sems, basis_sem):
    wanted = pltpu.make_async_copy(basis_rows.at[pl.ds(0, 16)], basis, basis_sem)
    wanted.start()
    pieces = BLOCKS // PIECE

    def arrival(piece):
        rows = pl.ds(piece * PIECE, PIECE)
        return pltpu.make_async_copy(dist.at[rows], held.at[rows], in_sems.at[piece])

    for piece in range(pieces):
        arrival(piece).start()
    wanted.wait()
    for piece in range(pieces):
        arrival(piece).wait()
        cells = held[pl.ds(piece * PIECE, PIECE)].astype(jnp.float32)
        cells = cells.reshape(PIECE * CELLS, TOTAL).astype(jnp.bfloat16)
        sums[:, pl.ds(piece * PIECE * CELLS, PIECE * CELLS)] = lax.dot_general(
            basis[...], cells, (((1,), (1,)), ((), ())), preferred_element_type=jnp.float32
        )

    rows, fraction = coefficients_of(sums[...])
    exact = [[], [], []]
    for row in rows:
        for part in range(3):
            near = row.astype(jnp.bfloat16).astype(jnp.float32)
            exact[part].append(near)
            row = row - near
    zero = jnp.zeros((6, BLOCKS * CELLS), jnp.float32)
    stacked = jnp.concatenate(
        exact[0]
        + [zero]
        + exact[1]
        + [zero]
        + exact[2]
        + [zero, fraction, jnp.zeros((79, BLOCKS * CELLS), jnp.float32)],
        axis=0,
    )
    factors[...] = stacked.T


VMEM = pl.BlockSpec(memory_space=pltpu.VMEM)
ANY = pl.BlockSpec(memory_space=pl.ANY)
WHOLE = (BLOCKS, CELLS, TOTAL)


def moments(dist, basis):
    return pl.pallas_call(
        moments_kernel,
        out_shape=jax.ShapeDtypeStruct((BLOCKS * CELLS, 128), jnp.float32),
        in_specs=[ANY, ANY],
        out_specs=VMEM,
        scratch_shapes=[
            pltpu.VMEM(WHOLE, jnp.bfloat16),
            pltpu.VMEM((16, TOTAL), jnp.bfloat16),
            pltpu.VMEM((16, BLOCKS * CELLS), jnp.float32),
            pltpu.SemaphoreType.DMA((BLOCKS // PIECE,)),
            pltpu.SemaphoreType.DMA(()),
        ],
        compiler_params=pltpu.CompilerParams(vmem_limit_bytes=RELAX_VMEM),
        cost_estimate=pl.CostEstimate(
            flops=2 * BLOCKS * CELLS * TOTAL * 1500,
            bytes_accessed=2 * BLOCKS * CELLS * TOTAL,
            transcendentals=0,
        ),
        name="moments",
    )(dist, basis)


def relax_kernel(
    asked, dist, basis, factors, send, held, relaxed, row, target, row_sem, in_sems, out_sem
):
    def arrival(group):
        rows = pl.ds(group * GROUP, GROUP)
        return pltpu.make_async_copy(dist.at[rows], held.at[rows], in_sems.at[group])

    for group in range(BLOCKS // GROUP):
        arrival(group).start()
    device = lax.broadcasted_iota(jnp.int32, asked.shape, 0)
    slot = lax.broadcasted_iota(jnp.int32, asked.shape, 1)
    row[...] = jnp.broadcast_to(
        jnp.sum(jnp.where(asked[...] == slot, device, 0), axis=0, keepdims=True), row.shape
    )
    to_scalars = pltpu.make_async_copy(row, target, row_sem)
    to_scalars.start()
    to_scalars.wait()

    @pl.loop(0, BLOCKS // GROUP)
    def _(group):
        first = group * GROUP
        arrival(group).wait()
        own = factors[pl.ds(pl.multiple_of(first * CELLS, GROUP * CELLS), GROUP * CELLS), :]
        left = own[:, :48].astype(jnp.bfloat16)
        fraction = jnp.broadcast_to(own[:, 48:49], (GROUP * CELLS, 128))
        for step in range(TOTAL // STEP):
            power = jnp.dot(
                left, basis[:, pl.ds(step * STEP, STEP)], preferred_element_type=jnp.float32
            )
            for tile in range(STEP // 128):
                place = lanes(step * (STEP // 128) + tile)
                gauss = jnp.exp2(power[:, tile * 128 : tile * 128 + 128])
                moved = held[pl.ds(first, GROUP), :, place].astype(jnp.float32)
                moved = moved.reshape(GROUP * CELLS, 128)
                mixed = moved + fraction * (gauss - moved)
                relaxed[pl.ds(first, GROUP), :, place] = mixed.reshape(
                    GROUP, CELLS, 128
                ).astype(jnp.bfloat16)
        for block in range(GROUP):
            pltpu.make_async_copy(
                relaxed.at[first + block], send.at[target[0, first + block]], out_sem
            ).start()

    pltpu.make_async_copy(relaxed, send.at[pl.ds(0, BLOCKS)], out_sem).wait()


def relax(asked, dist, basis, factors):
    devices = asked.shape[0]
    return pl.pallas_call(
        relax_kernel,
        out_shape=jax.ShapeDtypeStruct((devices, CELLS, TOTAL), jnp.bfloat16),
        in_specs=[VMEM, ANY, VMEM, VMEM],
        out_specs=ANY,
        scratch_shapes=[
            pltpu.VMEM(WHOLE, jnp.bfloat16),
            pltpu.VMEM(WHOLE, jnp.bfloat16),
            pltpu.VMEM((8, 128), jnp.int32),
            pltpu.SMEM((8, 128), jnp.int32),
            pltpu.SemaphoreType.DMA(()),
            pltpu.SemaphoreType.DMA((BLOCKS // GROUP,)),
            pltpu.SemaphoreType.DMA(()),
        ],
        compiler_params=pltpu.CompilerParams(vmem_limit_bytes=PACK_VMEM),
        cost_estimate=pl.CostEstimate(
            flops=2 * BLOCKS * CELLS * TOTAL * 64,
            bytes_accessed=4 * BLOCKS * CELLS * TOTAL,
            transcendentals=BLOCKS * CELLS * TOTAL,
        ),
        name="relax",
    )(asked, dist, basis, factors)


def row_masks():
    row = lax.broadcasted_iota(jnp.int32, (CELLS, 128), 0)
    return row < 4, (row & 2) == 0, (row & 1) == 0


def swap(x, distance):
    if distance == 4:
        return pltpu.roll(x, 4, 0)
    row = lax.broadcasted_iota(jnp.int32, (CELLS, 128), 0)
    return jnp.take_along_axis(x, row ^ distance, axis=0)


PARTS = 4
PART = TILES // PARTS
FACES = (("y", 0), ("y", 1), ("x", 0), ("x", 1))
FACE = (12, CELLS, TOTAL // 2)


def face_block(axis, up, pair):
    if axis == "x":
        return (BX - 1) * SLAB * up + 2 * pair
    return pair // 3 * SLAB + up * (BY - 1) * BZ + pair % 3 * 2


def face_tiles(axis, up):
    return [t for t in range(TILES) if up == (t % 2 if axis == "y" else t // (TILES // 2))]


GROUPS = (
    [(bx, 0) for bx in range(BX)],
    [(bx, BY - 1) for bx in range(BX)],
    [(0, by) for by in range(1, BY - 1)],
    [(BX - 1, by) for by in range(1, BY - 1)],
    [(bx, by) for bx in range(1, BX - 1) for by in range(1, BY - 1)],
)
PLACES = {column: BZ * n for n, column in enumerate(c for group in GROUPS for c in group)}


def faces_kernel(owner, arrived, mask, *rest):
    sent, (received, sems) = rest[: len(FACES)], rest[len(FACES) :]
    low_x, low_y, _ = row_masks()

    def fetch(group):
        for bx, by in GROUPS[group]:
            for bz in range(BZ):
                pltpu.make_async_copy(
                    arrived.at[owner[(bx * BY + by) * BZ + bz]],
                    received.at[PLACES[bx, by] + bz],
                    sems.at[group],
                ).start()

    def arrive(group):
        count = BZ * len(GROUPS[group])
        pltpu.make_async_copy(
            arrived.at[pl.ds(0, count)],
            received.at[pl.ds(PLACES[GROUPS[group][0]], count)],
            sems.at[group],
        ).wait()

    def write(axis, up):
        face = sent[FACES.index((axis, up))]
        low, distance = (low_x, 4) if axis == "x" else (low_y, 2)

        @pl.loop(0, 12)
        def _(pair):
            block = face_block(axis, up, pair)
            edge = (BX - 1) * up
            places = [PLACES[(edge, n) if axis == "x" else (n, edge)] for n in range(4)]
            line = pair // 3
            place = pair % 3 * 2 + jnp.where(
                line < 2,
                jnp.where(line == 0, places[0], places[1]),
                jnp.where(line == 2, places[2], places[3]),
            )
            masks = [mask[block + side] for side in range(2)]
            for n, tile in enumerate(face_tiles(axis, up)):
                a, b = (
                    received[place + side, :, lanes(tile)].astype(jnp.float32) * masks[side]
                    for side in range(2)
                )
                b = swap(b, distance)
                joined = jnp.where(low, b, a) if up else jnp.where(low, a, b)
                face[pair, :, lanes(n)] = joined.astype(jnp.bfloat16)

    fetch(0)
    fetch(1)
    fetch(2)
    arrive(0)
    write("y", 0)
    fetch(3)
    fetch(4)
    arrive(1)
    write("y", 1)
    arrive(2)
    write("x", 0)
    arrive(3)
    write("x", 1)
    arrive(4)


def faces(owner, received, mask):
    moved = 4 * math.prod(FACE)
    return pl.pallas_call(
        faces_kernel,
        out_shape=[jax.ShapeDtypeStruct(FACE, jnp.bfloat16) for _ in FACES]
        + [jax.ShapeDtypeStruct(WHOLE, received.dtype)],
        in_specs=[pl.BlockSpec(memory_space=pltpu.SMEM), ANY, VMEM],
        out_specs=[VMEM] * (len(FACES) + 1),
        scratch_shapes=[pltpu.SemaphoreType.DMA((len(GROUPS),))],
        compiler_params=pltpu.CompilerParams(vmem_limit_bytes=FACES_VMEM),
        cost_estimate=pl.CostEstimate(
            flops=8 * moved, bytes_accessed=4 * moved, transcendentals=0
        ),
        name="faces",
    )(owner, received, mask)


def speeds():
    lane = lax.broadcasted_iota(jnp.int32, (CELLS, 128), 1)
    speed_y = [
        SPACING * jnp.abs(2 * (lane // VS + 8 * odd) + 1 - VS).astype(jnp.float32)
        for odd in range(2)
    ]
    speed_z = SPACING * jnp.abs(2 * (lane % VS) + 1 - VS).astype(jnp.float32)
    return speed_y, speed_z, lane % VS >= VS // 2


def speed_x(tile):
    return SPACING * abs(2 * (tile // 2) + 1 - VS)


def advance_kernel(part, received, mask, rate, _, partial, done, kept):
    done[...] = jnp.zeros_like(done)
    low_x, low_y, low_z = row_masks()
    speed_y, speed_z, rising_z = speeds()
    speed_yz = [speed + speed_z for speed in speed_y]
    from_below = rising_z & ~low_z
    from_above = ~rising_z & low_z
    nothing = jnp.zeros((CELLS, 128), jnp.float32)

    for (bx, by), place in PLACES.items():

        @pl.loop(0, BZ)
        def _(bz):
            block = (bx * BY + by) * BZ + bz
            own_mask = mask[block]
            for tile in range(PART):
                kept[block, :, lanes(tile)] = (
                    received[place + bz, :, lanes(part * PART + tile)].astype(jnp.float32) * own_mask
                )

    for bz in range(BZ):
        kept[BLOCKS + bz] = jnp.zeros((CELLS, PART * 128), jnp.float32)

    @pl.loop(0, BX * BY)
    def _(column):
        bx, by = column // BY, column % BY
        line = column * BZ
        outside = BLOCKS
        near_x = (
            jnp.where(bx == BX - 1, outside, line + SLAB),
            jnp.where(bx == 0, outside, line - SLAB),
        )
        near_y = (
            jnp.where(by == BY - 1, outside, line + BZ),
            jnp.where(by == 0, outside, line - BZ),
        )
        rates = [rate[line + bz] for bz in range(BZ)]
        for held_at, tile in enumerate(range(part * PART, part * PART + PART)):
            x, y = tile // (TILES // 2), tile % 2
            own_line = [kept[line + bz, :, lanes(held_at)] for bz in range(BZ)]
            total = speed_x(tile) + speed_yz[y]
            for bz in range(BZ):
                own = own_line[bz]
                below = own_line[bz - 1] if bz else nothing
                above = own_line[bz + 1] if bz < BZ - 1 else nothing
                other = kept[near_x[x] + bz, :, lanes(held_at)]
                from_x = swap(
                    jnp.where(low_x, own, other) if x else jnp.where(low_x, other, own), 4
                )
                other = kept[near_y[y] + bz, :, lanes(held_at)]
                from_y = swap(
                    jnp.where(low_y, own, other) if y else jnp.where(low_y, other, own), 2
                )
                from_z = swap(
                    jnp.where(from_below, below, jnp.where(from_above, above, own)), 1
                )
                gain = speed_x(tile) * from_x + speed_y[y] * from_y + speed_z * from_z
                partial[line + bz, :, lanes(held_at)] = own + rates[bz] * (gain - total * own)


def advance(part, received, mask, rate, token):
    shape = (BLOCKS, CELLS, PART * 128)
    return pl.pallas_call(
        lambda *refs: advance_kernel(part, *refs),
        out_shape=[
            jax.ShapeDtypeStruct(shape, jnp.float32),
            jax.ShapeDtypeStruct((8, 128), jnp.float32),
        ],
        in_specs=[VMEM] * 4,
        out_specs=[VMEM] * 2,
        scratch_shapes=[pltpu.VMEM((BLOCKS + BZ, *shape[1:]), jnp.float32)],
        compiler_params=pltpu.CompilerParams(vmem_limit_bytes=ADVANCE_VMEM),
        cost_estimate=pl.CostEstimate(
            flops=100 * math.prod(shape), bytes_accessed=6 * math.prod(shape), transcendentals=0
        ),
        name=f"advance{part}",
    )(received, mask, rate, token)


def edge_kernel(rate, down_y, up_y, down_x, up_x, *rest):
    partials, (out, made, sems) = rest[:PARTS], rest[PARTS:]
    low_x, low_y, _ = row_masks()
    speed_y, _, _ = speeds()

    def add(halo, axis, up, slots):
        low, distance = (low_x, 4) if axis == "x" else (low_y, 2)
        edge = ~low if up else low

        @pl.loop(*slots)
        def _(pair):
            block = face_block(axis, 1 - up, pair)
            for place, tile in enumerate(face_tiles(axis, up)):
                face = halo[pair, :, lanes(place)].astype(jnp.float32)
                speed = speed_x(tile) if axis == "x" else speed_y[up]
                other = swap(face, distance)
                near = (jnp.where(edge, face, 0.0), jnp.where(edge, other, 0.0))
                for side in range(2):
                    gain = rate[block + side] * (speed * swap(near[side], distance))
                    partial = partials[tile // PART]
                    partial_at = (block + side, slice(None), lanes(tile % PART))
                    partial[partial_at] = partial[partial_at] + gain

    def result_copy(bx):
        rows = pl.ds(bx * SLAB, SLAB)
        return pltpu.make_async_copy(made.at[rows], out.at[rows], sems.at[bx])

    for bx in range(BX):
        if bx == 0:
            add(up_x, "x", 1, (0, 12))
        if bx == BX - 1:
            add(down_x, "x", 0, (0, 12))
        add(down_y, "y", 0, (3 * bx, 3 * bx + 3))
        add(up_y, "y", 1, (3 * bx, 3 * bx + 3))

        @pl.loop(bx * SLAB, bx * SLAB + SLAB)
        def _(block):
            for part, partial in enumerate(partials):
                lanes_at = pl.ds(part * PART * 128, PART * 128)
                made[block, :, lanes_at] = partial[block].astype(jnp.bfloat16)

        result_copy(bx).start()
    for bx in range(BX):
        result_copy(bx).wait()


def edge(partials, rate, halos):
    return pl.pallas_call(
        edge_kernel,
        out_shape=jax.ShapeDtypeStruct(WHOLE, jnp.bfloat16),
        in_specs=[VMEM] * (5 + PARTS),
        out_specs=ANY,
        scratch_shapes=[pltpu.VMEM(WHOLE, jnp.bfloat16), pltpu.SemaphoreType.DMA((BX,))],
        compiler_params=pltpu.CompilerParams(vmem_limit_bytes=EDGE_VMEM),
        cost_estimate=pl.CostEstimate(
            flops=4 * math.prod(WHOLE), bytes_accessed=6 * math.prod(WHOLE), transcendentals=0
        ),
        name="edge",
    )(rate, *halos, *partials)


def after(received, source_owner, levels, active):
    n_gx, n_gy = lax.axis_size("gx"), lax.axis_size("gy")
    mask = jnp.broadcast_to(
        active.astype(jnp.float32)[:, :, None], (BLOCKS, CELLS, 128)
    )
    courant = COURANT * jnp.exp2(levels.astype(jnp.float32))
    rate = mask * courant[:, None, None]

    def up(n):
        return [(i, i + 1) for i in range(n - 1)]

    def down(n):
        return [(i + 1, i) for i in range(n - 1)]

    *sent, received = faces(source_owner, received, mask)
    halos, partials, token = [], [], jnp.zeros((8, 128), jnp.float32)
    for part, ((axis, to_above), face) in enumerate(zip(FACES, sent)):
        name, n = ("gx", n_gx) if axis == "x" else ("gy", n_gy)
        if part:
            face, token = lax.optimization_barrier((face, token))
        halos.append(lax.ppermute(face, name, up(n) if to_above else down(n)))
        partial, token = advance(part, received, mask, rate, token)
        partials.append(partial)
    return edge(partials, rate, halos)


def per_device(dist_old, source_owner, levels, active):
    axes = ("gx", "gy")
    devices = lax.axis_size("gx") * lax.axis_size("gy")
    owners = lax.broadcasted_iota(jnp.int32, (devices, BLOCKS), 0)
    slots = lax.broadcasted_iota(jnp.int32, (devices, BLOCKS), 1)
    request = BLOCKS + jnp.sum(
        jnp.where(source_owner[None, :] == owners, slots - BLOCKS, 0), axis=1, keepdims=True
    )
    asked = lax.all_to_all(
        jnp.broadcast_to(request, (devices, 128)), axes, split_axis=0, concat_axis=0, tiled=True
    )
    basis = jnp.asarray(basis_rows())
    send = relax(asked, dist_old, basis, moments(dist_old, basis))
    received = lax.all_to_all(send, axes, split_axis=0, concat_axis=0, tiled=True)
    return after(received, source_owner, levels, active)


def solution(mesh):
    return jax.shard_map(
        per_device,
        mesh=mesh,
        in_specs=(
            P(("gx", "gy"), None, None),
            P(("gx", "gy")),
            P(("gx", "gy")),
            P(("gx", "gy"), None),
        ),
        out_specs=P(("gx", "gy"), None, None),
        check_vma=False,
    )
```

```python
import math

import jax
import jax.numpy as jnp
import ml_dtypes
import numpy as np
from jax import lax
from jax.experimental import pallas as pl
from jax.experimental.pallas import tpu as pltpu
from jax.sharding import PartitionSpec as P

VS = 16
BX, BY, BZ = 4, 4, 6
BLOCKS = BX * BY * BZ
TOTAL = VS * VS * VS
CELLS = 8
SLAB = BY * BZ
RELAX_INCREMENT = 0.3
COURANT = 0.028
SPACING = 3.0 / VS
LOG2E = 1.0 / math.log(2.0)

TILES = TOTAL // 128
PIECE = 16
RELAX_VMEM = 50 << 20
PACK_VMEM = 49 << 20
FACES_VMEM = 16 << 20
ADVANCE_VMEM = 28 << 20
EDGE_VMEM = 20 << 20
GROUP = 16
STEP = 512


def lanes(tile):
    return pl.ds(tile * 128, 128)


def basis_rows():
    index = np.arange(TOTAL)
    x, y, z = (2 * i + 1 - VS for i in (index // (VS * VS), index // VS % VS, index % VS))
    rows = np.zeros((16, TOTAL), np.float32)
    rows[:10] = [np.ones_like(x), x, y, z, x * x, y * y, z * z, x * y, x * z, y * z]
    whole = np.zeros((48, TOTAL), np.float32)
    for copy in range(3):
        whole[16 * copy : 16 * copy + 16] = rows
    return whole.astype(ml_dtypes.bfloat16)


def coefficients_of(sums):
    raw = [sums[i : i + 1] * (1.0 / TOTAL) for i in range(10)]
    density = raw[0]
    drift = [SPACING * raw[1 + a] / density for a in range(3)]
    square = SPACING * SPACING
    spread = [square * raw[4 + a] / density - drift[a] * drift[a] for a in range(3)]
    spread_xy = square * raw[7] / density - drift[0] * drift[1]
    spread_xz = square * raw[8] / density - drift[0] * drift[2]
    spread_yz = square * raw[9] / density - drift[1] * drift[2]
    temperature = (spread[0] + spread[1] + spread[2]) / 3.0
    xx, yy, zz = (1.5 * temperature - 0.5 * s for s in spread)
    xy, xz, yz = (-0.5 * s for s in (spread_xy, spread_xz, spread_yz))
    adj_xx, adj_yy, adj_zz = yy * zz - yz * yz, xx * zz - xz * xz, xx * yy - xy * xy
    adj_xy, adj_xz, adj_yz = xz * yz - xy * zz, xy * yz - xz * yy, xy * xz - xx * yz
    determinant = xx * adj_xx + xy * adj_xy + xz * adj_xz
    inv = [a / determinant for a in (adj_xx, adj_yy, adj_zz, adj_xy, adj_xz, adj_yz)]
    pull = [
        inv[0] * drift[0] + inv[3] * drift[1] + inv[4] * drift[2],
        inv[3] * drift[0] + inv[1] * drift[1] + inv[5] * drift[2],
        inv[4] * drift[0] + inv[5] * drift[1] + inv[2] * drift[2],
    ]
    quadratic = drift[0] * pull[0] + drift[1] * pull[1] + drift[2] * pull[2]
    log_prefactor = (
        jnp.log(density)
        + (3.0 * math.log(6.0) - 1.5 * math.log(2.0 * math.pi))
        - 0.5 * jnp.log(determinant)
    )
    rows = [log_prefactor - 0.5 * quadratic]
    rows += [SPACING * p for p in pull]
    rows += [-0.5 * square * i for i in inv[:3]]
    rows += [-square * i for i in inv[3:]]
    fraction = 1.0 - jnp.exp(-RELAX_INCREMENT * density * jnp.sqrt(temperature))
    return [LOG2E * r for r in rows], fraction


def moments_kernel(dist, factors, held, basis, sums, in_sems):
    pieces = BLOCKS // PIECE

    def arrival(piece):
        rows = pl.ds(piece * PIECE, PIECE)
        return pltpu.make_async_copy(dist.at[rows], held.at[rows], in_sems.at[piece])

    for piece in range(pieces):
        arrival(piece).start()
    point = lax.broadcasted_iota(jnp.int32, (1, TOTAL), 1)
    x, y, z = (
        (2 * i + 1 - VS).astype(jnp.float32)
        for i in (point >> 8, (point >> 4) & (VS - 1), point & (VS - 1))
    )
    table = [jnp.ones_like(x), x, y, z, x * x, y * y, z * z, x * y, x * z, y * z]
    basis[...] = jnp.concatenate(
        table + [jnp.zeros((6, TOTAL), jnp.float32)], axis=0
    ).astype(jnp.bfloat16)
    for piece in range(pieces):
        arrival(piece).wait()
        cells = held[pl.ds(piece * PIECE, PIECE)].astype(jnp.float32)
        cells = cells.reshape(PIECE * CELLS, TOTAL).astype(jnp.bfloat16)
        sums[:, pl.ds(piece * PIECE * CELLS, PIECE * CELLS)] = lax.dot_general(
            basis[...], cells, (((1,), (1,)), ((), ())), preferred_element_type=jnp.float32
        )

    rows, fraction = coefficients_of(sums[...])
    exact = [[], [], []]
    for row in rows:
        for part in range(3):
            near = row.astype(jnp.bfloat16).astype(jnp.float32)
            exact[part].append(near)
            row = row - near
    zero = jnp.zeros((6, BLOCKS * CELLS), jnp.float32)
    stacked = jnp.concatenate(
        exact[0]
        + [zero]
        + exact[1]
        + [zero]
        + exact[2]
        + [zero, fraction, jnp.zeros((79, BLOCKS * CELLS), jnp.float32)],
        axis=0,
    )
    factors[...] = stacked.T


VMEM = pl.BlockSpec(memory_space=pltpu.VMEM)
ANY = pl.BlockSpec(memory_space=pl.ANY)
WHOLE = (BLOCKS, CELLS, TOTAL)


def moments(dist):
    return pl.pallas_call(
        moments_kernel,
        out_shape=jax.ShapeDtypeStruct((BLOCKS * CELLS, 128), jnp.float32),
        in_specs=[ANY],
        out_specs=VMEM,
        scratch_shapes=[
            pltpu.VMEM(WHOLE, jnp.bfloat16),
            pltpu.VMEM((16, TOTAL), jnp.bfloat16),
            pltpu.VMEM((16, BLOCKS * CELLS), jnp.float32),
            pltpu.SemaphoreType.DMA((BLOCKS // PIECE,)),
        ],
        compiler_params=pltpu.CompilerParams(vmem_limit_bytes=RELAX_VMEM),
        cost_estimate=pl.CostEstimate(
            flops=2 * BLOCKS * CELLS * TOTAL * 1500,
            bytes_accessed=2 * BLOCKS * CELLS * TOTAL,
            transcendentals=0,
        ),
        name="moments",
    )(dist)


def relax_kernel(
    asked, dist, basis, factors, send, held, relaxed, row, target, row_sem, in_sems, out_sem
):
    def arrival(group):
        rows = pl.ds(group * GROUP, GROUP)
        return pltpu.make_async_copy(dist.at[rows], held.at[rows], in_sems.at[group])

    for group in range(BLOCKS // GROUP):
        arrival(group).start()
    device = lax.broadcasted_iota(jnp.int32, asked.shape, 0)
    slot = lax.broadcasted_iota(jnp.int32, asked.shape, 1)
    row[...] = jnp.broadcast_to(
        jnp.sum(jnp.where(asked[...] == slot, device, 0), axis=0, keepdims=True), row.shape
    )
    to_scalars = pltpu.make_async_copy(row, target, row_sem)
    to_scalars.start()
    to_scalars.wait()

    @pl.loop(0, BLOCKS // GROUP)
    def _(group):
        first = group * GROUP
        arrival(group).wait()
        own = factors[pl.ds(pl.multiple_of(first * CELLS, GROUP * CELLS), GROUP * CELLS), :]
        left = own[:, :48].astype(jnp.bfloat16)
        fraction = jnp.broadcast_to(own[:, 48:49], (GROUP * CELLS, 128))
        for step in range(TOTAL // STEP):
            power = jnp.dot(
                left, basis[:, pl.ds(step * STEP, STEP)], preferred_element_type=jnp.float32
            )
            for tile in range(STEP // 128):
                place = lanes(step * (STEP // 128) + tile)
                gauss = jnp.exp2(power[:, tile * 128 : tile * 128 + 128])
                moved = held[pl.ds(first, GROUP), :, place].astype(jnp.float32)
                moved = moved.reshape(GROUP * CELLS, 128)
                mixed = moved + fraction * (gauss - moved)
                relaxed[pl.ds(first, GROUP), :, place] = mixed.reshape(
                    GROUP, CELLS, 128
                ).astype(jnp.bfloat16)
        for block in range(GROUP):
            pltpu.make_async_copy(
                relaxed.at[first + block], send.at[target[0, first + block]], out_sem
            ).start()

    pltpu.make_async_copy(relaxed, send.at[pl.ds(0, BLOCKS)], out_sem).wait()


def relax(asked, dist, basis, factors):
    devices = asked.shape[0]
    return pl.pallas_call(
        relax_kernel,
        out_shape=jax.ShapeDtypeStruct((devices, CELLS, TOTAL), jnp.bfloat16),
        in_specs=[VMEM, ANY, VMEM, VMEM],
        out_specs=ANY,
        scratch_shapes=[
            pltpu.VMEM(WHOLE, jnp.bfloat16),
            pltpu.VMEM(WHOLE, jnp.bfloat16),
            pltpu.VMEM((8, 128), jnp.int32),
            pltpu.SMEM((8, 128), jnp.int32),
            pltpu.SemaphoreType.DMA(()),
            pltpu.SemaphoreType.DMA((BLOCKS // GROUP,)),
            pltpu.SemaphoreType.DMA(()),
        ],
        compiler_params=pltpu.CompilerParams(vmem_limit_bytes=PACK_VMEM),
        cost_estimate=pl.CostEstimate(
            flops=2 * BLOCKS * CELLS * TOTAL * 64,
            bytes_accessed=4 * BLOCKS * CELLS * TOTAL,
            transcendentals=BLOCKS * CELLS * TOTAL,
        ),
        name="relax",
    )(asked, dist, basis, factors)


def row_masks():
    row = lax.broadcasted_iota(jnp.int32, (CELLS, 128), 0)
    return row < 4, (row & 2) == 0, (row & 1) == 0


def swap(x, distance):
    if distance == 4:
        return pltpu.roll(x, 4, 0)
    row = lax.broadcasted_iota(jnp.int32, (CELLS, 128), 0)
    return jnp.take_along_axis(x, row ^ distance, axis=0)


FACES = (("y", 0), ("y", 1), ("x", 0), ("x", 1))
FACE = (12, CELLS, TOTAL // 2)


def face_block(axis, up, pair):
    if axis == "x":
        return (BX - 1) * SLAB * up + 2 * pair
    return pair // 3 * SLAB + up * (BY - 1) * BZ + pair % 3 * 2


def face_tiles(axis, up):
    return [t for t in range(TILES) if up == (t % 2 if axis == "y" else t // (TILES // 2))]


GROUPS = (
    [(bx, 0) for bx in range(BX)],
    [(bx, BY - 1) for bx in range(BX)],
    [(0, by) for by in range(1, BY - 1)],
    [(BX - 1, by) for by in range(1, BY - 1)],
    [(bx, by) for bx in range(1, BX - 1) for by in range(1, BY - 1)],
)
PLACES = {column: BZ * n for n, column in enumerate(c for group in GROUPS for c in group)}


def faces_kernel(owner, arrived, mask, *rest):
    sent, (received, sems) = rest[: len(FACES)], rest[len(FACES) :]
    low_x, low_y, _ = row_masks()

    def fetch(group):
        for bx, by in GROUPS[group]:
            for bz in range(BZ):
                pltpu.make_async_copy(
                    arrived.at[owner[(bx * BY + by) * BZ + bz]],
                    received.at[PLACES[bx, by] + bz],
                    sems.at[group],
                ).start()

    def arrive(group):
        count = BZ * len(GROUPS[group])
        pltpu.make_async_copy(
            arrived.at[pl.ds(0, count)],
            received.at[pl.ds(PLACES[GROUPS[group][0]], count)],
            sems.at[group],
        ).wait()

    def write(axis, up):
        face = sent[FACES.index((axis, up))]
        low, distance = (low_x, 4) if axis == "x" else (low_y, 2)

        @pl.loop(0, 12)
        def _(pair):
            block = face_block(axis, up, pair)
            edge = (BX - 1) * up
            places = [PLACES[(edge, n) if axis == "x" else (n, edge)] for n in range(4)]
            line = pair // 3
            place = pair % 3 * 2 + jnp.where(
                line < 2,
                jnp.where(line == 0, places[0], places[1]),
                jnp.where(line == 2, places[2], places[3]),
            )
            masks = [mask[block + side] for side in range(2)]
            for n, tile in enumerate(face_tiles(axis, up)):
                a, b = (
                    received[place + side, :, lanes(tile)].astype(jnp.float32) * masks[side]
                    for side in range(2)
                )
                b = swap(b, distance)
                joined = jnp.where(low, b, a) if up else jnp.where(low, a, b)
                face[pair, :, lanes(n)] = joined.astype(jnp.bfloat16)

    fetch(0)
    fetch(1)
    fetch(2)
    arrive(0)
    write("y", 0)
    fetch(3)
    fetch(4)
    arrive(1)
    write("y", 1)
    arrive(2)
    write("x", 0)
    arrive(3)
    write("x", 1)
    arrive(4)


def faces(owner, received, mask):
    moved = 4 * math.prod(FACE)
    return pl.pallas_call(
        faces_kernel,
        out_shape=[jax.ShapeDtypeStruct(FACE, jnp.bfloat16) for _ in FACES]
        + [jax.ShapeDtypeStruct(WHOLE, received.dtype)],
        in_specs=[pl.BlockSpec(memory_space=pltpu.SMEM), ANY, VMEM],
        out_specs=[VMEM] * (len(FACES) + 1),
        scratch_shapes=[pltpu.SemaphoreType.DMA((len(GROUPS),))],
        compiler_params=pltpu.CompilerParams(vmem_limit_bytes=FACES_VMEM),
        cost_estimate=pl.CostEstimate(
            flops=8 * moved, bytes_accessed=4 * moved, transcendentals=0
        ),
        name="faces",
    )(owner, received, mask)


def speeds():
    lane = lax.broadcasted_iota(jnp.int32, (CELLS, 128), 1)
    speed_y = [
        SPACING * jnp.abs(2 * (lane // VS + 8 * odd) + 1 - VS).astype(jnp.float32)
        for odd in range(2)
    ]
    speed_z = SPACING * jnp.abs(2 * (lane % VS) + 1 - VS).astype(jnp.float32)
    return speed_y, speed_z, lane % VS >= VS // 2


def speed_x(tile):
    return SPACING * abs(2 * (tile // 2) + 1 - VS)


def advance_kernel(received, mask, rate, partial, kept):
    low_x, low_y, low_z = row_masks()
    speed_y, speed_z, rising_z = speeds()
    speed_yz = [speed + speed_z for speed in speed_y]
    from_below = rising_z & ~low_z
    from_above = ~rising_z & low_z
    nothing = jnp.zeros((CELLS, 128), jnp.float32)

    for (bx, by), place in PLACES.items():

        @pl.loop(0, BZ)
        def _(bz):
            block = (bx * BY + by) * BZ + bz
            own_mask = mask[block]
            for tile in range(TILES):
                kept[block, :, lanes(tile)] = (
                    received[place + bz, :, lanes(tile)].astype(jnp.float32) * own_mask
                )

    for bz in range(BZ):
        kept[BLOCKS + bz] = jnp.zeros((CELLS, TOTAL), jnp.float32)

    @pl.loop(0, BX * BY)
    def _(column):
        bx, by = column // BY, column % BY
        line = column * BZ
        outside = BLOCKS
        near_x = (
            jnp.where(bx == BX - 1, outside, line + SLAB),
            jnp.where(bx == 0, outside, line - SLAB),
        )
        near_y = (
            jnp.where(by == BY - 1, outside, line + BZ),
            jnp.where(by == 0, outside, line - BZ),
        )
        rates = [rate[line + bz] for bz in range(BZ)]
        for tile in range(TILES):
            x, y = tile // (TILES // 2), tile % 2
            own_line = [kept[line + bz, :, lanes(tile)] for bz in range(BZ)]
            total = speed_x(tile) + speed_yz[y]
            for bz in range(BZ):
                own = own_line[bz]
                below = own_line[bz - 1] if bz else nothing
                above = own_line[bz + 1] if bz < BZ - 1 else nothing
                other = kept[near_x[x] + bz, :, lanes(tile)]
                from_x = swap(
                    jnp.where(low_x, own, other) if x else jnp.where(low_x, other, own), 4
                )
                other = kept[near_y[y] + bz, :, lanes(tile)]
                from_y = swap(
                    jnp.where(low_y, own, other) if y else jnp.where(low_y, other, own), 2
                )
                from_z = swap(
                    jnp.where(from_below, below, jnp.where(from_above, above, own)), 1
                )
                gain = speed_x(tile) * from_x + speed_y[y] * from_y + speed_z * from_z
                partial[line + bz, :, lanes(tile)] = own + rates[bz] * (gain - total * own)


def advance(received, mask, rate):
    return pl.pallas_call(
        advance_kernel,
        out_shape=jax.ShapeDtypeStruct(WHOLE, jnp.float32),
        in_specs=[VMEM] * 3,
        out_specs=VMEM,
        scratch_shapes=[pltpu.VMEM((BLOCKS + BZ, CELLS, TOTAL), jnp.float32)],
        compiler_params=pltpu.CompilerParams(vmem_limit_bytes=ADVANCE_VMEM),
        cost_estimate=pl.CostEstimate(
            flops=100 * math.prod(WHOLE), bytes_accessed=6 * math.prod(WHOLE), transcendentals=0
        ),
        name="advance",
    )(received, mask, rate)


def edge_kernel(partial, rate, down_y, up_y, down_x, up_x, out, made, sems):
    low_x, low_y, _ = row_masks()
    speed_y, _, _ = speeds()

    def add(halo, axis, up, slots):
        low, distance = (low_x, 4) if axis == "x" else (low_y, 2)
        edge = ~low if up else low

        @pl.loop(*slots)
        def _(pair):
            block = face_block(axis, 1 - up, pair)
            for place, tile in enumerate(face_tiles(axis, up)):
                face = halo[pair, :, lanes(place)].astype(jnp.float32)
                speed = speed_x(tile) if axis == "x" else speed_y[up]
                other = swap(face, distance)
                near = (jnp.where(edge, face, 0.0), jnp.where(edge, other, 0.0))
                for side in range(2):
                    gain = rate[block + side] * (speed * swap(near[side], distance))
                    partial_at = (block + side, slice(None), lanes(tile))
                    partial[partial_at] = partial[partial_at] + gain

    def result_copy(bx):
        rows = pl.ds(bx * SLAB, SLAB)
        return pltpu.make_async_copy(made.at[rows], out.at[rows], sems.at[bx])

    for bx in range(BX):
        if bx == 0:
            add(up_x, "x", 1, (0, 12))
        if bx == BX - 1:
            add(down_x, "x", 0, (0, 12))
        add(down_y, "y", 0, (3 * bx, 3 * bx + 3))
        add(up_y, "y", 1, (3 * bx, 3 * bx + 3))

        @pl.loop(bx * SLAB, bx * SLAB + SLAB)
        def _(block):
            made[block] = partial[block].astype(jnp.bfloat16)

        result_copy(bx).start()
    for bx in range(BX):
        result_copy(bx).wait()


def edge(partial, rate, halos):
    return pl.pallas_call(
        edge_kernel,
        out_shape=jax.ShapeDtypeStruct(WHOLE, jnp.bfloat16),
        in_specs=[VMEM] * 6,
        out_specs=ANY,
        scratch_shapes=[pltpu.VMEM(WHOLE, jnp.bfloat16), pltpu.SemaphoreType.DMA((BX,))],
        compiler_params=pltpu.CompilerParams(vmem_limit_bytes=EDGE_VMEM),
        cost_estimate=pl.CostEstimate(
            flops=4 * math.prod(WHOLE), bytes_accessed=6 * math.prod(WHOLE), transcendentals=0
        ),
        name="edge",
    )(partial, rate, *halos)


def after(received, source_owner, levels, active):
    n_gx, n_gy = lax.axis_size("gx"), lax.axis_size("gy")
    mask = jnp.broadcast_to(
        active.astype(jnp.float32)[:, :, None], (BLOCKS, CELLS, 128)
    )
    courant = COURANT * jnp.exp2(levels.astype(jnp.float32))
    rate = mask * courant[:, None, None]

    def up(n):
        return [(i, i + 1) for i in range(n - 1)]

    def down(n):
        return [(i + 1, i) for i in range(n - 1)]

    *sent, received = faces(source_owner, received, mask)
    halos = []
    for (axis, to_above), face in zip(FACES, sent):
        name, n = ("gx", n_gx) if axis == "x" else ("gy", n_gy)
        halos.append(lax.ppermute(face, name, up(n) if to_above else down(n)))
    return edge(advance(received, mask, rate), rate, halos)


def per_device(dist_old, source_owner, levels, active):
    axes = ("gx", "gy")
    devices = lax.axis_size("gx") * lax.axis_size("gy")
    owners = lax.broadcasted_iota(jnp.int32, (devices, BLOCKS), 0)
    wanted = (source_owner[None, :] == owners).astype(jnp.bfloat16)
    slots = lax.broadcasted_iota(jnp.int32, (BLOCKS, 128), 0) - BLOCKS
    request = BLOCKS + jnp.dot(
        wanted, slots.astype(jnp.bfloat16), preferred_element_type=jnp.float32
    ).astype(jnp.int32)
    asked = lax.all_to_all(request, axes, split_axis=0, concat_axis=0, tiled=True)
    send = relax(asked, dist_old, jnp.asarray(basis_rows()), moments(dist_old))
    received = lax.all_to_all(send, axes, split_axis=0, concat_axis=0, tiled=True)
    return after(received, source_owner, levels, active)


def solution(mesh):
    return jax.shard_map(
        per_device,
        mesh=mesh,
        in_specs=(
            P(("gx", "gy"), None, None),
            P(("gx", "gy")),
            P(("gx", "gy")),
            P(("gx", "gy"), None),
        ),
        out_specs=P(("gx", "gy"), None, None),
        check_vma=False,
    )
```

```python
import math

import jax
import jax.numpy as jnp
import ml_dtypes
import numpy as np
from jax import lax
from jax.experimental import pallas as pl
from jax.experimental.pallas import tpu as pltpu
from jax.sharding import PartitionSpec as P

VS = 16
BX, BY, BZ = 4, 4, 6
BLOCKS = BX * BY * BZ
TOTAL = VS * VS * VS
CELLS = 8
SLAB = BY * BZ
RELAX_INCREMENT = 0.3
COURANT = 0.028
SPACING = 3.0 / VS
LOG2E = 1.0 / math.log(2.0)

TILES = TOTAL // 128
PIECE = 16
RELAX_VMEM = 50 << 20
PACK_VMEM = 49 << 20
FACES_VMEM = 16 << 20
ADVANCE_VMEM = 28 << 20
EDGE_VMEM = 20 << 20
GROUP = 16
STEP = 512


def lanes(tile):
    return pl.ds(tile * 128, 128)


def basis_rows():
    index = np.arange(TOTAL)
    x, y, z = (2 * i + 1 - VS for i in (index // (VS * VS), index // VS % VS, index % VS))
    rows = np.zeros((16, TOTAL), np.float32)
    rows[:10] = [np.ones_like(x), x, y, z, x * x, y * y, z * z, x * y, x * z, y * z]
    whole = np.zeros((48, TOTAL), np.float32)
    for copy in range(3):
        whole[16 * copy : 16 * copy + 16] = rows
    return whole.astype(ml_dtypes.bfloat16)


def coefficients_of(sums):
    raw = [sums[i : i + 1] * (1.0 / TOTAL) for i in range(10)]
    density = raw[0]
    drift = [SPACING * raw[1 + a] / density for a in range(3)]
    square = SPACING * SPACING
    spread = [square * raw[4 + a] / density - drift[a] * drift[a] for a in range(3)]
    spread_xy = square * raw[7] / density - drift[0] * drift[1]
    spread_xz = square * raw[8] / density - drift[0] * drift[2]
    spread_yz = square * raw[9] / density - drift[1] * drift[2]
    temperature = (spread[0] + spread[1] + spread[2]) / 3.0
    xx, yy, zz = (1.5 * temperature - 0.5 * s for s in spread)
    xy, xz, yz = (-0.5 * s for s in (spread_xy, spread_xz, spread_yz))
    adj_xx, adj_yy, adj_zz = yy * zz - yz * yz, xx * zz - xz * xz, xx * yy - xy * xy
    adj_xy, adj_xz, adj_yz = xz * yz - xy * zz, xy * yz - xz * yy, xy * xz - xx * yz
    determinant = xx * adj_xx + xy * adj_xy + xz * adj_xz
    inv = [a / determinant for a in (adj_xx, adj_yy, adj_zz, adj_xy, adj_xz, adj_yz)]
    pull = [
        inv[0] * drift[0] + inv[3] * drift[1] + inv[4] * drift[2],
        inv[3] * drift[0] + inv[1] * drift[1] + inv[5] * drift[2],
        inv[4] * drift[0] + inv[5] * drift[1] + inv[2] * drift[2],
    ]
    quadratic = drift[0] * pull[0] + drift[1] * pull[1] + drift[2] * pull[2]
    log_prefactor = (
        jnp.log(density)
        + (3.0 * math.log(6.0) - 1.5 * math.log(2.0 * math.pi))
        - 0.5 * jnp.log(determinant)
    )
    rows = [log_prefactor - 0.5 * quadratic]
    rows += [SPACING * p for p in pull]
    rows += [-0.5 * square * i for i in inv[:3]]
    rows += [-square * i for i in inv[3:]]
    fraction = 1.0 - jnp.exp(-RELAX_INCREMENT * density * jnp.sqrt(temperature))
    return [LOG2E * r for r in rows], fraction


def moments_kernel(dist, factors, held, basis, sums, in_sems):
    pieces = BLOCKS // PIECE

    def arrival(piece):
        rows = pl.ds(piece * PIECE, PIECE)
        return pltpu.make_async_copy(dist.at[rows], held.at[rows], in_sems.at[piece])

    for piece in range(pieces):
        arrival(piece).start()
    point = lax.broadcasted_iota(jnp.int32, (1, TOTAL), 1)
    x, y, z = (
        (2 * i + 1 - VS).astype(jnp.float32)
        for i in (point >> 8, (point >> 4) & (VS - 1), point & (VS - 1))
    )
    table = [jnp.ones_like(x), x, y, z, x * x, y * y, z * z, x * y, x * z, y * z]
    basis[...] = jnp.concatenate(
        table + [jnp.zeros((6, TOTAL), jnp.float32)], axis=0
    ).astype(jnp.bfloat16)
    for piece in range(pieces):
        arrival(piece).wait()
        cells = held[pl.ds(piece * PIECE, PIECE)].astype(jnp.float32)
        cells = cells.reshape(PIECE * CELLS, TOTAL).astype(jnp.bfloat16)
        sums[:, pl.ds(piece * PIECE * CELLS, PIECE * CELLS)] = lax.dot_general(
            basis[...], cells, (((1,), (1,)), ((), ())), preferred_element_type=jnp.float32
        )

    rows, fraction = coefficients_of(sums[...])
    exact = [[], [], []]
    for row in rows:
        for part in range(3):
            near = row.astype(jnp.bfloat16).astype(jnp.float32)
            exact[part].append(near)
            row = row - near
    zero = jnp.zeros((6, BLOCKS * CELLS), jnp.float32)
    stacked = jnp.concatenate(
        exact[0]
        + [zero]
        + exact[1]
        + [zero]
        + exact[2]
        + [zero, fraction, jnp.zeros((79, BLOCKS * CELLS), jnp.float32)],
        axis=0,
    )
    factors[...] = stacked.T


VMEM = pl.BlockSpec(memory_space=pltpu.VMEM)
ANY = pl.BlockSpec(memory_space=pl.ANY)
WHOLE = (BLOCKS, CELLS, TOTAL)


def moments(dist):
    return pl.pallas_call(
        moments_kernel,
        out_shape=jax.ShapeDtypeStruct((BLOCKS * CELLS, 128), jnp.float32),
        in_specs=[ANY],
        out_specs=VMEM,
        scratch_shapes=[
            pltpu.VMEM(WHOLE, jnp.bfloat16),
            pltpu.VMEM((16, TOTAL), jnp.bfloat16),
            pltpu.VMEM((16, BLOCKS * CELLS), jnp.float32),
            pltpu.SemaphoreType.DMA((BLOCKS // PIECE,)),
        ],
        compiler_params=pltpu.CompilerParams(vmem_limit_bytes=RELAX_VMEM),
        cost_estimate=pl.CostEstimate(
            flops=2 * BLOCKS * CELLS * TOTAL * 1500,
            bytes_accessed=2 * BLOCKS * CELLS * TOTAL,
            transcendentals=0,
        ),
        name="moments",
    )(dist)


def relax_kernel(
    asked, dist, basis, factors, send, held, relaxed, row, target, row_sem, in_sems, out_sem
):
    def arrival(group):
        rows = pl.ds(group * GROUP, GROUP)
        return pltpu.make_async_copy(dist.at[rows], held.at[rows], in_sems.at[group])

    for group in range(BLOCKS // GROUP):
        arrival(group).start()
    device = lax.broadcasted_iota(jnp.int32, asked.shape, 0)
    slot = lax.broadcasted_iota(jnp.int32, asked.shape, 1)
    row[...] = jnp.broadcast_to(
        jnp.sum(jnp.where(asked[...] == slot, device, 0), axis=0, keepdims=True), row.shape
    )
    to_scalars = pltpu.make_async_copy(row, target, row_sem)
    to_scalars.start()
    to_scalars.wait()

    @pl.loop(0, BLOCKS // GROUP)
    def _(group):
        first = group * GROUP
        arrival(group).wait()
        own = factors[pl.ds(pl.multiple_of(first * CELLS, GROUP * CELLS), GROUP * CELLS), :]
        left = own[:, :48].astype(jnp.bfloat16)
        fraction = jnp.broadcast_to(own[:, 48:49], (GROUP * CELLS, 128))
        for step in range(TOTAL // STEP):
            power = jnp.dot(
                left, basis[:, pl.ds(step * STEP, STEP)], preferred_element_type=jnp.float32
            )
            for tile in range(STEP // 128):
                place = lanes(step * (STEP // 128) + tile)
                gauss = jnp.exp2(power[:, tile * 128 : tile * 128 + 128])
                moved = held[pl.ds(first, GROUP), :, place].astype(jnp.float32)
                moved = moved.reshape(GROUP * CELLS, 128)
                mixed = moved + fraction * (gauss - moved)
                relaxed[pl.ds(first, GROUP), :, place] = mixed.reshape(
                    GROUP, CELLS, 128
                ).astype(jnp.bfloat16)
        for block in range(GROUP):
            pltpu.make_async_copy(
                relaxed.at[first + block], send.at[target[0, first + block]], out_sem
            ).start()

    pltpu.make_async_copy(relaxed, send.at[pl.ds(0, BLOCKS)], out_sem).wait()


def relax(asked, dist, basis, factors):
    devices = asked.shape[0]
    return pl.pallas_call(
        relax_kernel,
        out_shape=jax.ShapeDtypeStruct((devices, CELLS, TOTAL), jnp.bfloat16),
        in_specs=[VMEM, ANY, VMEM, VMEM],
        out_specs=ANY,
        scratch_shapes=[
            pltpu.VMEM(WHOLE, jnp.bfloat16),
            pltpu.VMEM(WHOLE, jnp.bfloat16),
            pltpu.VMEM((8, 128), jnp.int32),
            pltpu.SMEM((8, 128), jnp.int32),
            pltpu.SemaphoreType.DMA(()),
            pltpu.SemaphoreType.DMA((BLOCKS // GROUP,)),
            pltpu.SemaphoreType.DMA(()),
        ],
        compiler_params=pltpu.CompilerParams(vmem_limit_bytes=PACK_VMEM),
        cost_estimate=pl.CostEstimate(
            flops=2 * BLOCKS * CELLS * TOTAL * 64,
            bytes_accessed=4 * BLOCKS * CELLS * TOTAL,
            transcendentals=BLOCKS * CELLS * TOTAL,
        ),
        name="relax",
    )(asked, dist, basis, factors)


def row_masks():
    row = lax.broadcasted_iota(jnp.int32, (CELLS, 128), 0)
    return row < 4, (row & 2) == 0, (row & 1) == 0


def swap(x, distance):
    if distance == 4:
        return pltpu.roll(x, 4, 0)
    row = lax.broadcasted_iota(jnp.int32, (CELLS, 128), 0)
    return jnp.take_along_axis(x, row ^ distance, axis=0)


FACES = (("y", 0), ("y", 1), ("x", 0), ("x", 1))
FACE = (12, CELLS, TOTAL // 2)


def face_block(axis, up, pair):
    if axis == "x":
        return (BX - 1) * SLAB * up + 2 * pair
    return pair // 3 * SLAB + up * (BY - 1) * BZ + pair % 3 * 2


def face_tiles(axis, up):
    return [t for t in range(TILES) if up == (t % 2 if axis == "y" else t // (TILES // 2))]


GROUPS = (
    [(bx, 0) for bx in range(BX)],
    [(bx, BY - 1) for bx in range(BX)],
    [(0, by) for by in range(1, BY - 1)],
    [(BX - 1, by) for by in range(1, BY - 1)],
    [(bx, by) for bx in range(1, BX - 1) for by in range(1, BY - 1)],
)
PLACES = {column: BZ * n for n, column in enumerate(c for group in GROUPS for c in group)}


def faces_kernel(owner, arrived, mask, _, *rest):
    sent, (received, sems) = rest[: len(FACES)], rest[len(FACES) :]
    low_x, low_y, _ = row_masks()

    def fetch(group):
        for bx, by in GROUPS[group]:
            for bz in range(BZ):
                pltpu.make_async_copy(
                    arrived.at[owner[(bx * BY + by) * BZ + bz]],
                    received.at[PLACES[bx, by] + bz],
                    sems.at[group],
                ).start()

    def arrive(group):
        count = BZ * len(GROUPS[group])
        pltpu.make_async_copy(
            arrived.at[pl.ds(0, count)],
            received.at[pl.ds(PLACES[GROUPS[group][0]], count)],
            sems.at[group],
        ).wait()

    def write(axis, up):
        face = sent[FACES.index((axis, up))]
        low, distance = (low_x, 4) if axis == "x" else (low_y, 2)

        @pl.loop(0, 12)
        def _(pair):
            block = face_block(axis, up, pair)
            edge = (BX - 1) * up
            places = [PLACES[(edge, n) if axis == "x" else (n, edge)] for n in range(4)]
            line = pair // 3
            place = pair % 3 * 2 + jnp.where(
                line < 2,
                jnp.where(line == 0, places[0], places[1]),
                jnp.where(line == 2, places[2], places[3]),
            )
            masks = [mask[block + side] for side in range(2)]
            for n, tile in enumerate(face_tiles(axis, up)):
                a, b = (
                    received[place + side, :, lanes(tile)].astype(jnp.float32) * masks[side]
                    for side in range(2)
                )
                b = swap(b, distance)
                joined = jnp.where(low, b, a) if up else jnp.where(low, a, b)
                face[pair, :, lanes(n)] = joined.astype(jnp.bfloat16)

    fetch(0)
    fetch(1)
    fetch(2)
    arrive(0)
    write("y", 0)
    fetch(3)
    fetch(4)
    arrive(1)
    write("y", 1)
    arrive(2)
    write("x", 0)
    arrive(3)
    write("x", 1)
    arrive(4)


def faces(owner, received, mask, rate):
    moved = 4 * math.prod(FACE)
    return pl.pallas_call(
        faces_kernel,
        out_shape=[jax.ShapeDtypeStruct(FACE, jnp.bfloat16) for _ in FACES]
        + [jax.ShapeDtypeStruct(WHOLE, received.dtype)],
        in_specs=[pl.BlockSpec(memory_space=pltpu.SMEM), ANY, VMEM, ANY],
        out_specs=[VMEM] * (len(FACES) + 1),
        scratch_shapes=[pltpu.SemaphoreType.DMA((len(GROUPS),))],
        compiler_params=pltpu.CompilerParams(vmem_limit_bytes=FACES_VMEM),
        cost_estimate=pl.CostEstimate(
            flops=8 * moved, bytes_accessed=4 * moved, transcendentals=0
        ),
        name="faces",
    )(owner, received, mask, rate)


def speeds():
    lane = lax.broadcasted_iota(jnp.int32, (CELLS, 128), 1)
    speed_y = [
        SPACING * jnp.abs(2 * (lane // VS + 8 * odd) + 1 - VS).astype(jnp.float32)
        for odd in range(2)
    ]
    speed_z = SPACING * jnp.abs(2 * (lane % VS) + 1 - VS).astype(jnp.float32)
    return speed_y, speed_z, lane % VS >= VS // 2


def speed_x(tile):
    return SPACING * abs(2 * (tile // 2) + 1 - VS)


def advance_kernel(received, mask, rate, partial, kept):
    low_x, low_y, low_z = row_masks()
    speed_y, speed_z, rising_z = speeds()
    speed_yz = [speed + speed_z for speed in speed_y]
    from_below = rising_z & ~low_z
    from_above = ~rising_z & low_z
    nothing = jnp.zeros((CELLS, 128), jnp.float32)

    for (bx, by), place in PLACES.items():

        @pl.loop(0, BZ)
        def _(bz):
            block = (bx * BY + by) * BZ + bz
            own_mask = mask[block]
            for tile in range(TILES):
                kept[block, :, lanes(tile)] = (
                    received[place + bz, :, lanes(tile)].astype(jnp.float32) * own_mask
                )

    for bz in range(BZ):
        kept[BLOCKS + bz] = jnp.zeros((CELLS, TOTAL), jnp.float32)

    @pl.loop(0, BX * BY)
    def _(column):
        bx, by = column // BY, column % BY
        line = column * BZ
        outside = BLOCKS
        near_x = (
            jnp.where(bx == BX - 1, outside, line + SLAB),
            jnp.where(bx == 0, outside, line - SLAB),
        )
        near_y = (
            jnp.where(by == BY - 1, outside, line + BZ),
            jnp.where(by == 0, outside, line - BZ),
        )
        rates = [rate[line + bz] for bz in range(BZ)]
        for tile in range(TILES):
            x, y = tile // (TILES // 2), tile % 2
            own_line = [kept[line + bz, :, lanes(tile)] for bz in range(BZ)]
            total = speed_x(tile) + speed_yz[y]
            for bz in range(BZ):
                own = own_line[bz]
                below = own_line[bz - 1] if bz else nothing
                above = own_line[bz + 1] if bz < BZ - 1 else nothing
                other = kept[near_x[x] + bz, :, lanes(tile)]
                from_x = swap(
                    jnp.where(low_x, own, other) if x else jnp.where(low_x, other, own), 4
                )
                other = kept[near_y[y] + bz, :, lanes(tile)]
                from_y = swap(
                    jnp.where(low_y, own, other) if y else jnp.where(low_y, other, own), 2
                )
                from_z = swap(
                    jnp.where(from_below, below, jnp.where(from_above, above, own)), 1
                )
                gain = speed_x(tile) * from_x + speed_y[y] * from_y + speed_z * from_z
                partial[line + bz, :, lanes(tile)] = own + rates[bz] * (gain - total * own)


def advance(received, mask, rate):
    return pl.pallas_call(
        advance_kernel,
        out_shape=jax.ShapeDtypeStruct(WHOLE, jnp.float32),
        in_specs=[VMEM] * 3,
        out_specs=VMEM,
        scratch_shapes=[pltpu.VMEM((BLOCKS + BZ, CELLS, TOTAL), jnp.float32)],
        compiler_params=pltpu.CompilerParams(vmem_limit_bytes=ADVANCE_VMEM),
        cost_estimate=pl.CostEstimate(
            flops=100 * math.prod(WHOLE), bytes_accessed=6 * math.prod(WHOLE), transcendentals=0
        ),
        name="advance",
    )(received, mask, rate)


def edge_kernel(partial, rate, down_y, up_y, down_x, up_x, out, made, sems):
    low_x, low_y, _ = row_masks()
    speed_y, _, _ = speeds()

    def add(halo, axis, up, slots):
        low, distance = (low_x, 4) if axis == "x" else (low_y, 2)
        edge = ~low if up else low

        @pl.loop(*slots)
        def _(pair):
            block = face_block(axis, 1 - up, pair)
            for place, tile in enumerate(face_tiles(axis, up)):
                face = halo[pair, :, lanes(place)].astype(jnp.float32)
                speed = speed_x(tile) if axis == "x" else speed_y[up]
                other = swap(face, distance)
                near = (jnp.where(edge, face, 0.0), jnp.where(edge, other, 0.0))
                for side in range(2):
                    gain = rate[block + side] * (speed * swap(near[side], distance))
                    partial_at = (block + side, slice(None), lanes(tile))
                    partial[partial_at] = partial[partial_at] + gain

    def result_copy(bx):
        rows = pl.ds(bx * SLAB, SLAB)
        return pltpu.make_async_copy(made.at[rows], out.at[rows], sems.at[bx])

    for bx in (1, 2, 0, 3):
        if bx == 0:
            add(up_x, "x", 1, (0, 12))
        if bx == BX - 1:
            add(down_x, "x", 0, (0, 12))
        add(down_y, "y", 0, (3 * bx, 3 * bx + 3))
        add(up_y, "y", 1, (3 * bx, 3 * bx + 3))

        @pl.loop(bx * SLAB, bx * SLAB + SLAB)
        def _(block):
            made[block] = partial[block].astype(jnp.bfloat16)

        result_copy(bx).start()
    for bx in range(BX):
        result_copy(bx).wait()


def edge(partial, rate, halos):
    return pl.pallas_call(
        edge_kernel,
        out_shape=jax.ShapeDtypeStruct(WHOLE, jnp.bfloat16),
        in_specs=[VMEM] * 6,
        out_specs=ANY,
        scratch_shapes=[pltpu.VMEM(WHOLE, jnp.bfloat16), pltpu.SemaphoreType.DMA((BX,))],
        compiler_params=pltpu.CompilerParams(vmem_limit_bytes=EDGE_VMEM),
        cost_estimate=pl.CostEstimate(
            flops=4 * math.prod(WHOLE), bytes_accessed=6 * math.prod(WHOLE), transcendentals=0
        ),
        name="edge",
    )(partial, rate, *halos)


def after(received, source_owner, levels, active):
    n_gx, n_gy = lax.axis_size("gx"), lax.axis_size("gy")
    mask = jnp.broadcast_to(
        active.astype(jnp.float32)[:, :, None], (BLOCKS, CELLS, 128)
    )
    courant = COURANT * jnp.exp2(levels.astype(jnp.float32))
    rate = mask * courant[:, None, None]

    def up(n):
        return [(i, i + 1) for i in range(n - 1)]

    def down(n):
        return [(i + 1, i) for i in range(n - 1)]

    *sent, received = faces(source_owner, received, mask, rate)
    halos = []
    for (axis, to_above), face in zip(FACES, sent):
        name, n = ("gx", n_gx) if axis == "x" else ("gy", n_gy)
        halos.append(lax.ppermute(face, name, up(n) if to_above else down(n)))
    return edge(advance(received, mask, rate), rate, halos)


def per_device(dist_old, source_owner, levels, active):
    axes = ("gx", "gy")
    devices = lax.axis_size("gx") * lax.axis_size("gy")
    owners = lax.broadcasted_iota(jnp.int32, (devices, BLOCKS), 0)
    wanted = (source_owner[None, :] == owners).astype(jnp.bfloat16)
    slots = lax.broadcasted_iota(jnp.int32, (BLOCKS, 128), 0) - BLOCKS
    request = BLOCKS + jnp.dot(
        wanted, slots.astype(jnp.bfloat16), preferred_element_type=jnp.float32
    ).astype(jnp.int32)
    asked = lax.all_to_all(request, axes, split_axis=0, concat_axis=0, tiled=True)
    send = relax(asked, dist_old, jnp.asarray(basis_rows()), moments(dist_old))
    received = lax.all_to_all(send, axes, split_axis=0, concat_axis=0, tiled=True)
    return after(received, source_owner, levels, active)


def solution(mesh):
    return jax.shard_map(
        per_device,
        mesh=mesh,
        in_specs=(
            P(("gx", "gy"), None, None),
            P(("gx", "gy")),
            P(("gx", "gy")),
            P(("gx", "gy"), None),
        ),
        out_specs=P(("gx", "gy"), None, None),
        check_vma=False,
    )
```
